128 devices in a mesh: space: 16 (over y, x_lo, core), filt: 8 (over x_hi, z).
Axes of the slice: x: 4 (x_hi: 2, x_lo: 2; x = x_hi * 2 + x_lo), y: 4, z: 4, core: 2. Of those that a mesh axis runs over, the one named last changes fastest.
Arguments:
- volume: bfloat16 [64, 128, 16, 128], P('space', 'filt'), may hold values from -6 to 6
- w_early: bfloat16 [27, 128, 128], replicated, may hold values from -0.109375 to 0.109375
- w_deep: bfloat16 [27, 128, 256], P(None, None, 'filt'), may hold values from -0.109375 to 0.109375
- cotangent: bfloat16 [32, 64, 8, 256], P('space', None, None, 'filt'), may hold values from -6 to 6
Outputs:
- block_out: bfloat16 [32, 64, 8, 256], P('space', None, None, 'filt')
- grad_early: float32 [27, 128, 128], replicated
- grad_deep: float32 [27, 128, 256], P(None, None, 'filt')
The draws below stay inside these ranges and needn't reach their ends.
All inputs are finite; a program needn't handle non-finite values.
Results may differ from the reference program's by a relative error of at most 0.0059.
Values may be sent and summed in bfloat16 or wider, within the bound.
A program may use at most 128 MiB of HBM per device.

```python
import math
import jax
import jax.numpy as jnp
from jax import lax

C0 = 128
C1 = 128
C2 = 256
NZ = 16
NX = 64
NY = 128


def levels(stream_key, extent, pieces, least, top_value):
    factor_of = 1.0
    for position, parts in pieces:
        draws = jax.random.uniform(jax.random.fold_in(jax.random.fold_in(stream_key, 6), position), (parts,), jnp.float32, least / len(pieces), top_value / len(pieces))
        factor_of = factor_of * jnp.repeat(jnp.exp(draws), extent[position] // parts).reshape((-1,) + (1,) * (len(extent) - 1 - position))
    return factor_of


def noise(key, extent, scale, bound, split=(), held_as=jnp.bfloat16):
    drawn = jax.random.normal(key, extent, jnp.float32) * scale
    if len(split) > 0:
        drawn = levels(key, extent, split, -0.22, 0.18) * drawn
    return jnp.clip(drawn, min=-bound, max=bound).astype(held_as)


def setup_inputs(seed: int = 0) -> dict:
    keys = jax.random.split(jax.random.key(seed), 5)
    return {
        "volume": noise(keys[0], (NX, NY, NZ, C0), 1.0, 6.0, ((0, 16), (1, 8))),
        "w_early": noise(keys[1], (27, C0, C1), (27 * C0) ** -0.5, 0.109375),
        "w_deep": noise(keys[2], (27, C1, C2), (27 * C1) ** -0.5, 0.109375, ((2, 8),)),
        "cotangent": noise(keys[3], (NX // 2, NY // 2, NZ // 2, C2), 1.0, 6.0, ((0, 16), (3, 8))),
    }


def silu_grad(value):
    sig = jax.nn.sigmoid(value)
    return sig * (1.0 + value * (1.0 - sig))

def convolve(field, kernel):
    cin = kernel.shape[1]
    cout = kernel.shape[2]
    result = lax.conv_general_dilated(field[None], kernel.reshape(3, 3, 3, cin, cout), (1, 1, 1), 'SAME', dimension_numbers=('NDHWC', 'DHWIO', 'NDHWC'), precision=lax.Precision.HIGHEST)
    return result[0]

def reference(volume, w_early, w_deep, cotangent):
    field = volume.astype(jnp.float32)
    kernel_one = w_early.astype(jnp.float32)
    kernel_two = w_deep.astype(jnp.float32)
    pre_early = convolve(field, kernel_one)
    size_x, size_y, size_z, width = pre_early.shape
    pooled = jax.nn.silu(pre_early).reshape(size_x // 2, 2, size_y // 2, 2, size_z // 2, 2, width).mean(axis=(1, 3, 5)).astype(jnp.bfloat16)
    pooled_f = lax.optimization_barrier(pooled).astype(jnp.float32)
    pre_deep = convolve(pooled_f, kernel_two)
    block_out = jax.nn.silu(pre_deep).astype(jnp.bfloat16)
    grad_pre_deep = (cotangent.astype(jnp.float32) * silu_grad(pre_deep)).astype(jnp.bfloat16)
    grad_pre_deep = lax.optimization_barrier(grad_pre_deep).astype(jnp.float32)
    unused, pull_deep = jax.vjp(convolve, pooled_f, kernel_two)
    grad_pooled, grad_deep = pull_deep(grad_pre_deep)
    grad_pooled = lax.optimization_barrier(grad_pooled.astype(jnp.bfloat16)).astype(jnp.float32)
    spread = jnp.repeat(jnp.repeat(jnp.repeat(grad_pooled, 2, axis=0), 2, axis=1), 2, axis=2) / 8.0
    grad_pre_early = (spread * silu_grad(pre_early)).astype(jnp.bfloat16)
    grad_pre_early = lax.optimization_barrier(grad_pre_early).astype(jnp.float32)
    unused_two, pull_early = jax.vjp(lambda kernel: convolve(field, kernel), kernel_one)
    grad_early = pull_early(grad_pre_early)[0]
    total = size_x * size_y * size_z
    grad_early = grad_early / math.sqrt(total)
    grad_deep = grad_deep / math.sqrt(total // 8)
    return (block_out, grad_early, grad_deep)
```

```python
import functools
import math

import jax
import jax.numpy as jnp
from jax import lax
from jax.experimental import pallas as pl
from jax.experimental.pallas import tpu as pltpu
from jax.sharding import PartitionSpec as P

MESH = pl.DeviceIdType.MESH
BF = jnp.bfloat16
F32 = jnp.float32
SPACE, FILT, CHIPS = 16, 8, 64
DIRS = [(ds, df) for ds in (-1, 0, 1) for df in (-1, 0, 1) if ds or df]
GROUP = 4
OWNERS = 7


def rcopy(src, dst, send_sem, recv_sem, device):
    return pltpu.make_async_remote_copy(
        src_ref=src,
        dst_ref=dst,
        send_sem=send_sem,
        recv_sem=recv_sem,
        device_id=device,
        device_id_type=MESH,
    )


def sigmoid(v):
    return 1.0 / (1.0 + jnp.exp(-v))


def shift_rows(v, step):
    size = v.shape[1]
    row = lax.broadcasted_iota(jnp.int32, v.shape, 1)
    edge = size - 1 if step == 1 else 0
    rolled = pltpu.roll(v, (-step) % size, 1)
    return jnp.where(row == edge, 0.0, rolled)


def dot(a, b):
    return lax.dot_general(a, b, (((1,), (0,)), ((), ())), preferred_element_type=F32)


def dot_t(a, b):
    return lax.dot_general(a, b, (((1,), (1,)), ((), ())), preferred_element_type=F32)


def edges(step, size):
    if step == 1:
        return size - 1, 0, 1
    if step == -1:
        return 0, size + 1, 1
    return 0, 1, size


class Halo:
    def __init__(self, source, base, padded, nx, ny, sems, s, f):
        self.items = []
        for k, (ds, df) in enumerate(DIRS):
            sx, dx, lx = edges(ds, nx)
            sy, dy, ly = edges(df, ny)
            src = source.at[base + sx : base + sx + lx, base + sy : base + sy + ly]
            dst = padded.at[dx : dx + lx, dy : dy + ly]
            to_s, to_f, from_s, from_f = s + ds, f + df, s - ds, f - df
            send = (to_s >= 0) & (to_s < SPACE) & (to_f >= 0) & (to_f < FILT)
            recv = (from_s >= 0) & (from_s < SPACE) & (from_f >= 0) & (from_f < FILT)
            copy = rcopy(src, dst, sems.at[0, k], sems.at[1, k], (to_s, to_f))
            self.items.append((copy, send, recv))

    def start(self):
        for copy, send, _ in self.items:
            pl.when(send)(copy.start)

    def wait_recv(self):
        for copy, _, recv in self.items:
            pl.when(recv)(copy.wait_recv)

    def wait_send(self):
        for copy, send, _ in self.items:
            pl.when(send)(copy.wait_send)


def zero_rim(padded, nx, ny, s, f):
    shape = padded.shape

    @pl.when(s == 0)
    def _():
        padded[0:1] = jnp.zeros((1,) + shape[1:], padded.dtype)

    @pl.when(s == SPACE - 1)
    def _():
        padded[nx + 1 : nx + 2] = jnp.zeros((1,) + shape[1:], padded.dtype)

    @pl.when(f == 0)
    def _():
        padded[:, 0:1] = jnp.zeros((shape[0], 1) + shape[2:], padded.dtype)

    @pl.when(f == FILT - 1)
    def _():
        padded[:, ny + 1 : ny + 2] = jnp.zeros((shape[0], 1) + shape[2:], padded.dtype)


SCRATCH = dict(
    vp=((6, 18, 16, 128), BF),
    zc=((6, 18, 16, 384), BF),
    we=((9, 384, 128), BF),
    wd=((27, 128, 32), BF),
    ct=((2, 64, 8, 32), BF),
    wg=((9, 256, 384), BF),
    cs=((8, 2, 16, 128), BF),
    cr=((2, 8, 16, 128), BF),
    acc=((1024, 128), F32),
    sg=((4, 16, 16, 128), F32),
    tmp=((16, 16, 128), F32),
    pp=((4, 10, 8, 128), BF),
    pz=((4, 10, 8, 384), F32),
    ps=((2, 66, 8, 128), BF),
    ps3=((2, 66, 8, 384), F32),
    bs=((2, 8, 16, 128), BF),
    br=((8, 2, 16, 128), BF),
    gp=((4, 10, 8, 256), BF),
    gf=((4, 10, 8, 256), F32),
    gs=((2, 3, 8, 16, 128), BF),
    gr=((2, 3, 16, 1024), BF),
    gt=((128, 1024), BF),
    xs=((9, 64, 384), BF),
    xr=((9, 64, 384), BF),
    xo=((9, 64, 384), F32),
    es=((8, 28, 8, 128), BF),
    er=((64, 4, 8, 128), BF),
    ea=((2, 8, 28, 8, 128), BF),
    pb=((1024, 1152), BF),
    hs=((48, 1152), BF),
    hr=((48, 1152), BF),
    ho=((48, 1152), F32),
    dsd=((28, 16, 128), BF),
    dr=((8, 4, 16, 128), BF),
    da=((2, 28, 16, 128), BF),
)
SEMS = dict(
    local=(3,),
    halo_v=(2, 8),
    halo_p=(2, 8),
    halo_g=(2, 8),
    s_cot=(2, 8),
    s_wg=(2, 8),
    s_wrel=(2,),
    s_ps=(2, 8),
    s_bo=(2, 8),
    s_g=(2, 8),
    s_x=(2, 9),
    s_rs=(2, 64),
    s_ag=(2, 64),
    s_ear=(2,),
    s_h=(2,),
    s_drs=(2, 8),
    s_dag=(2, 8),
    s_dar=(2,),
)


def kernel(early_scale, deep_scale, vol, we_in, wd_in, ct_in, bo_out, ge_out, gd_out, *scratch):
    r = dict(zip(list(SCRATCH) + list(SEMS), scratch))
    s = lax.axis_index("space")
    f = lax.axis_index("filt")
    core = lax.rem(s, 2)
    other = 1 - core
    sib = s + 1 - 2 * core
    j = lax.div(s, 2)

    def filt_peer(k):
        return lax.rem(f + k, FILT)

    def filt_from(k):
        return lax.rem(f + FILT - k, FILT)

    def chip(k):
        dj, df = lax.div(k, 8), lax.rem(k, 8)
        return lax.rem(s + 2 * dj, SPACE), lax.rem(f + df, FILT)

    def chip_from(k):
        dj, df = lax.div(k, 8), lax.rem(k, 8)
        return lax.rem(s + SPACE - 2 * dj, SPACE), lax.rem(f + FILT - df, FILT)

    barrier = pltpu.get_barrier_semaphore()

    def greet(k, carry):
        pl.semaphore_signal(barrier, inc=1, device_id=chip(k), device_id_type=MESH)
        return carry

    for d in (1, SPACE - 1):
        for df in (0, 1, FILT - 1):
            pl.semaphore_signal(
                barrier,
                inc=1,
                device_id=(lax.rem(s + d, SPACE), lax.rem(f + df, FILT)),
                device_id_type=MESH,
            )
    lax.fori_loop(1, CHIPS, greet, 0)

    own_vol = pltpu.make_async_copy(vol, r["vp"].at[1:5, 1:17], r["local"].at[0])
    own_vol.start()
    own_wd = pltpu.make_async_copy(wd_in, r["wd"], r["local"].at[1])
    own_wd.start()
    own_ct = pltpu.make_async_copy(ct_in, r["ct"], r["local"].at[2])
    own_ct.start()
    own_wd.wait()
    wg = r["wg"]
    for t in range(27):
        wt = r["wd"][t].astype(F32).T.astype(BF)
        lanes = slice(128 * (t % 3), 128 * (t % 3) + 128)
        for h in range(2):

            @pl.when(core == h)
            def _():
                rows = pl.ds(pl.multiple_of(128 * h + 16 * f, 16), 16)
                wg[t // 3, rows, lanes] = wt[16 * h : 16 * h + 16]

    own_ct.wait()
    for q in range(8):
        piece = r["ct"][:, 8 * q : 8 * q + 8].astype(F32).reshape(128, 32)
        r["cs"][q] = piece.T.astype(BF).reshape(2, 16, 128)
    zero_rim(r["vp"], 4, 16, s, f)
    zero_rim(r["pp"], 2, 8, s, f)
    zero_rim(r["gp"], 2, 8, s, f)
    r["ps"][:, 0:1] = jnp.zeros((2, 1, 8, 128), BF)
    r["ps"][:, 65:66] = jnp.zeros((2, 1, 8, 128), BF)

    pl.semaphore_wait(barrier, CHIPS - 1 + 6)
    halo_v = Halo(vol, 0, r["vp"], 4, 16, r["halo_v"], s, f)
    halo_v.start()
    own_we = pltpu.make_async_copy(we_in, r["we"], r["local"].at[1])
    own_we.start()

    cots = []
    for k in range(1, FILT):
        cots.append(
            rcopy(
                r["cs"].at[filt_peer(k)],
                r["cr"].at[:, f],
                r["s_cot"].at[0, k],
                r["s_cot"].at[1, k],
                (s, filt_peer(k)),
            )
        )
        cots[-1].start()
    wgs = []
    for k in range(1, FILT):
        rows = pl.ds(pl.multiple_of(128 * core + 16 * f, 16), 16)
        wgs.append(
            rcopy(
                wg.at[:, rows],
                wg.at[:, rows],
                r["s_wg"].at[0, k],
                r["s_wg"].at[1, k],
                (s, filt_peer(k)),
            )
        )
        wgs[-1].start()
    r["cr"][:, pl.ds(f, 1)] = r["cs"][pl.ds(f, 1)].reshape(2, 1, 16, 128)

    own_vol.wait()
    halo_v.wait_recv()
    zc = r["zc"]
    for row in range(6):
        x = r["vp"][row].astype(F32)
        zc[row, :, :, 0:128] = shift_rows(x, -1).astype(BF)
        zc[row, :, :, 128:256] = r["vp"][row]
        zc[row, :, :, 256:384] = shift_rows(x, 1).astype(BF)
    own_we.wait()
    acc = r["acc"]
    for ab in range(9):
        a, b = ab // 3, ab % 3
        patch = zc[a : a + 4, b : b + 16].reshape(1024, 384)
        term = dot(patch, r["we"][ab])
        if ab == 0:
            acc[...] = term
        else:
            acc[...] += term
    for half in range(2):
        v = acc[512 * half : 512 * half + 512].reshape(2, 16, 16, 128)
        sig = sigmoid(v)
        r["sg"][2 * half : 2 * half + 2] = sig * (1.0 + v * (1.0 - sig)) * 0.125
        act = v * sig
        act = (act[0] + act[1]).reshape(8, 2, 16, 128)
        r["tmp"][8 * half : 8 * half + 8] = act[:, 0] + act[:, 1]
    tmp = r["tmp"]
    pooled = (tmp[:, pl.ds(0, 8, stride=2), :] + tmp[:, pl.ds(1, 8, stride=2), :]) * 0.125
    pooled = pooled.reshape(2, 8, 8, 128).astype(BF)
    r["pp"][1:3, 1:9] = pooled
    halo_p = Halo(r["pp"], 1, r["pp"], 2, 8, r["halo_p"], s, f)
    halo_p.start()
    pss = []
    for k in range(1, FILT):
        pss.append(
            rcopy(
                r["pp"].at[1:3, 1:9],
                r["ps"].at[:, pl.ds(1 + 8 * f, 8)],
                r["s_ps"].at[0, k],
                r["s_ps"].at[1, k],
                (s, filt_peer(k)),
            )
        )
        pss[-1].start()
    r["ps"][:, pl.ds(1 + 8 * f, 8)] = pooled

    for c in wgs:
        c.wait_recv()
    mine = pl.ds(pl.multiple_of(128 * core, 128), 128)
    wrel = rcopy(wg.at[:, mine], wg.at[:, mine], r["s_wrel"].at[0], r["s_wrel"].at[1], (sib, f))
    wrel.start()
    for c in cots:
        c.wait_recv()
    cot = r["cr"][...].reshape(256, 128).astype(F32).T
    halo_p.wait_recv()
    pz = r["pz"]
    for row in range(4):
        x = r["pp"][row].astype(F32)
        pz[row, :, :, 0:128] = shift_rows(x, -1)
        pz[row, :, :, 128:256] = x
        pz[row, :, :, 256:384] = shift_rows(x, 1)
    wrel.wait_recv()

    pre = jnp.zeros((128, 256), F32)
    for ab in range(9):
        a, b = ab // 3, ab % 3
        patch = pz[a : a + 2, b : b + 8].reshape(128, 384).astype(BF)
        pre = pre + dot_t(patch, wg[ab])
    sig = sigmoid(pre)
    g = (cot * (sig * (1.0 + pre * (1.0 - sig)))).astype(BF)
    r["gp"][1:3, 1:9] = g.astype(F32).reshape(2, 8, 8, 256).astype(BF)
    halo_g = Halo(r["gp"], 1, r["gp"], 2, 8, r["halo_g"], s, f)
    halo_g.start()
    r["bs"][...] = (pre * sig).T.astype(BF).reshape(2, 8, 16, 128)
    bos = []
    for k in range(1, FILT):
        bos.append(
            rcopy(
                r["bs"].at[:, filt_peer(k)],
                r["br"].at[f],
                r["s_bo"].at[0, k],
                r["s_bo"].at[1, k],
                (s, filt_peer(k)),
            )
        )
        bos[-1].start()
    r["br"][pl.ds(f, 1)] = r["bs"][:, pl.ds(f, 1)].reshape(1, 2, 16, 128)

    halo_g.wait_recv()
    gf = r["gf"]
    gf[...] = r["gp"][...].astype(F32)
    back = jnp.zeros((128, 384), F32)
    for ab in range(9):
        a, b = ab // 3, ab % 3
        patch = gf[2 - a : 4 - a, 2 - b : 10 - b].reshape(128, 256).astype(BF)
        back = back + dot(patch, wg[ab])
    back = back.reshape(16, 8, 384)
    gpool = (
        shift_rows(back[:, :, 0:128], 1)
        + back[:, :, 128:256]
        + shift_rows(back[:, :, 256:384], -1)
    )
    gpool = gpool.astype(BF).astype(F32)
    tmp[:, pl.ds(0, 8, stride=2), :] = gpool
    tmp[:, pl.ds(1, 8, stride=2), :] = gpool
    for row in range(4):
        spread = tmp[8 * (row // 2) : 8 * (row // 2) + 8]
        spread = jnp.broadcast_to(spread[:, None], (8, 2, 16, 128)).reshape(16, 16, 128)
        grad = (spread * r["sg"][row]).astype(BF).astype(F32).reshape(256, 128)
        r["gt"][:, 256 * row : 256 * row + 256] = grad.T.astype(BF)

    gt = r["gt"][...]
    xcs = []
    for ab in range(9):
        a, b = ab // 3, ab % 3
        term = dot(gt, zc[a : a + 4, b : b + 16].reshape(1024, 384))

        @pl.when(core == 0)
        def _():
            r["xo"][ab] = term[0:64]
            r["xs"][ab] = term[64:128].astype(BF)

        @pl.when(core == 1)
        def _():
            r["xo"][ab] = term[64:128]
            r["xs"][ab] = term[0:64].astype(BF)

        xcs.append(
            rcopy(r["xs"].at[ab], r["xr"].at[ab], r["s_x"].at[0, ab], r["s_x"].at[1, ab], (sib, f))
        )
        xcs[-1].start()

    for a in range(3):
        piece = gf[2 - a : 4 - a, 1:9].reshape(128, 256)
        r["gs"][:, a] = piece.T.astype(BF).reshape(2, 8, 16, 128)
    gcs = []
    lanes = pl.ds(pl.multiple_of(128 * f, 128), 128)
    for k in range(1, FILT):
        gcs.append(
            rcopy(
                r["gs"].at[:, :, filt_peer(k)],
                r["gr"].at[:, :, :, lanes],
                r["s_g"].at[0, k],
                r["s_g"].at[1, k],
                (s, filt_peer(k)),
            )
        )
        gcs[-1].start()
    r["gr"][:, :, :, lanes] = r["gs"][:, :, pl.ds(f, 1)].reshape(2, 3, 16, 128)

    es = r["es"]
    es[:, 27:28] = jnp.zeros((8, 1, 8, 128), BF)
    for ab in range(9):
        xcs[ab].wait_recv()
        total = r["xo"][ab] + r["xr"][ab].astype(F32)
        for c in range(3):
            es[:, 3 * ab + c] = total[:, 128 * c : 128 * c + 128].reshape(8, 8, 128).astype(BF)

    er = r["er"]

    def rs_copy(k):
        to_s, to_f = chip(k)
        to_j = lax.div(to_s, 2)
        first = jnp.minimum(GROUP * to_j, GROUP * (OWNERS - 1))
        copy = rcopy(
            es.at[to_f, pl.ds(first, GROUP)],
            er.at[k],
            r["s_rs"].at[0, k],
            r["s_rs"].at[1, k],
            (to_s, to_f),
        )
        return copy, to_j < OWNERS

    def rs_start(k, carry):
        copy, active = rs_copy(k)
        pl.when(active)(copy.start)
        return carry

    lax.fori_loop(1, CHIPS, rs_start, 0)

    for c in pss:
        c.wait_recv()
    ps3 = r["ps3"]
    for row in range(2):
        x = r["ps"][row].astype(F32)
        ps3[row, :, :, 0:128] = shift_rows(x, -1)
        ps3[row, :, :, 128:256] = x
        ps3[row, :, :, 256:384] = shift_rows(x, 1)
    for q in range(8):
        for b in range(3):
            patch = ps3[:, 8 * q + b : 8 * q + b + 8].reshape(128, 384).astype(BF)
            r["pb"][128 * q : 128 * q + 128, 384 * b : 384 * b + 384] = patch
    for c in gcs:
        c.wait_recv()
    deep = dot(r["gr"][...].reshape(96, 1024), r["pb"][...])

    @pl.when(core == 0)
    def _():
        r["ho"][...] = deep[0:48]
        r["hs"][...] = deep[48:96].astype(BF)

    @pl.when(core == 1)
    def _():
        r["ho"][...] = deep[48:96]
        r["hs"][...] = deep[0:48].astype(BF)

    hcopy = rcopy(r["hs"], r["hr"], r["s_h"].at[0], r["s_h"].at[1], (sib, f))
    hcopy.start()

    for c in bos:
        c.wait_recv()
    for q in range(8):
        piece = r["br"][q].reshape(32, 128).astype(F32).T
        bo_out[:, 8 * q : 8 * q + 8] = piece.reshape(2, 8, 8, 32).astype(BF)

    hcopy.wait_recv()
    dsd = r["dsd"]
    dsd[27:28] = jnp.zeros((1, 16, 128), BF)
    total = r["ho"][...] + r["hr"][...].astype(F32)
    for a in range(3):
        for bc in range(9):
            dsd[9 * a + bc] = total[16 * a : 16 * a + 16, 128 * bc : 128 * bc + 128].astype(BF)

    def space_chip(k):
        return lax.rem(s + 2 * k, SPACE)

    def first_of(jj):
        return jnp.minimum(GROUP * jj, GROUP * (OWNERS - 1))

    drs = []
    for k in range(1, 8):
        to_s = space_chip(k)
        to_j = lax.div(to_s, 2)
        copy = rcopy(
            dsd.at[pl.ds(first_of(to_j), GROUP)],
            r["dr"].at[k],
            r["s_drs"].at[0, k],
            r["s_drs"].at[1, k],
            (to_s, f),
        )
        pl.when(to_j < OWNERS)(copy.start)
        drs.append((copy, to_j < OWNERS))

    mine_t = pl.ds(first_of(j), GROUP)
    owner = j < OWNERS

    def rs_wait(k, carry):
        copy, _ = rs_copy(k)
        copy.wait_recv()
        return carry

    ea = r["ea"]

    def ag_copy(k):
        to_s, to_f = chip(k)
        piece = ea.at[core, f, mine_t]
        return rcopy(piece, piece, r["s_ag"].at[0, k], r["s_ag"].at[1, k], (to_s, to_f))

    @pl.when(owner)
    def _():
        lax.fori_loop(1, CHIPS, rs_wait, 0)
        total = es[pl.ds(f, 1), mine_t].reshape(GROUP, 8, 128).astype(F32)

        def add(k, total):
            return total + er[k].astype(F32)

        total = lax.fori_loop(1, CHIPS, add, total)
        total = (total * early_scale).astype(BF).reshape(1, 1, GROUP, 8, 128)
        ea[pl.ds(core, 1), pl.ds(f, 1), mine_t] = total

        def ag_start(k, carry):
            ag_copy(k).start()
            return carry

        lax.fori_loop(1, CHIPS, ag_start, 0)

    da = r["da"]
    piece = da.at[core, mine_t]
    dag = []
    for k in range(1, 8):
        dag.append(
            rcopy(piece, piece, r["s_dag"].at[0, k], r["s_dag"].at[1, k], (space_chip(k), f))
        )

    @pl.when(owner)
    def _():
        total = dsd[mine_t].astype(F32)
        for k in range(1, 8):
            drs[k - 1][0].wait_recv()
            total = total + r["dr"][k].astype(F32)
        da[pl.ds(core, 1), mine_t] = (total * deep_scale).astype(BF).reshape(1, GROUP, 16, 128)
        for c in dag:
            c.start()

    for k in range(1, 8):
        from_j = lax.div(lax.rem(s + SPACE - 2 * k, SPACE), 2)
        pl.when(from_j < OWNERS)(dag[k - 1].wait_recv)
    dar = rcopy(da.at[core], da.at[core], r["s_dar"].at[0], r["s_dar"].at[1], (sib, f))
    dar.start()

    def ag_wait(k, carry):
        from_s, _ = chip_from(k)
        pl.when(lax.div(from_s, 2) < OWNERS)(ag_copy(k).wait_recv)
        return carry

    lax.fori_loop(1, CHIPS, ag_wait, 0)
    ear = rcopy(ea.at[core], ea.at[core], r["s_ear"].at[0], r["s_ear"].at[1], (sib, f))
    ear.start()

    dar.wait_recv()
    for t in range(27):
        gd_out[t] = da[:, t].reshape(32, 128).astype(F32).T
    ear.wait_recv()
    for t in range(27):
        ge_out[t] = ea[:, :, t].astype(F32).reshape(128, 128).T

    for h in (halo_v, halo_p, halo_g):
        h.wait_send()
    for c in cots + wgs + pss + bos + gcs + xcs + [wrel, hcopy, dar, ear]:
        c.wait_send()
    for copy, active in drs:
        pl.when(active)(copy.wait_send)

    def rs_sent(k, carry):
        copy, active = rs_copy(k)
        pl.when(active)(copy.wait_send)
        return carry

    lax.fori_loop(1, CHIPS, rs_sent, 0)

    @pl.when(owner)
    def _():
        for c in dag:
            c.wait_send()

        def ag_sent(k, carry):
            ag_copy(k).wait_send()
            return carry

        lax.fori_loop(1, CHIPS, ag_sent, 0)


def shards(volume, w_early, w_deep, cotangent):
    any_ = pl.BlockSpec(memory_space=pl.ANY)
    vmem = pl.BlockSpec(memory_space=pltpu.VMEM)
    cells = volume.shape[0] * volume.shape[1] * volume.shape[2] * SPACE * FILT
    body = functools.partial(kernel, 1.0 / math.sqrt(cells), 1.0 / math.sqrt(cells // 8))
    return pl.pallas_call(
        body,
        out_shape=(
            jax.ShapeDtypeStruct((2, 64, 8, 32), BF),
            jax.ShapeDtypeStruct((27, 128, 128), F32),
            jax.ShapeDtypeStruct((27, 128, 32), F32),
        ),
        in_specs=[any_] * 4,
        out_specs=(vmem,) * 3,
        scratch_shapes=[pltpu.VMEM(*v) for v in SCRATCH.values()]
        + [pltpu.SemaphoreType.DMA(v) for v in SEMS.values()],
        compiler_params=pltpu.CompilerParams(
            collective_id=0, has_side_effects=True, vmem_limit_bytes=56 << 20
        ),
        name="step",
    )(volume, w_early.reshape(9, 384, 128), w_deep, cotangent)


def solution(mesh):
    return jax.shard_map(
        shards,
        mesh=mesh,
        in_specs=(
            P("space", "filt", None, None),
            P(),
            P(None, None, "filt"),
            P("space", None, None, "filt"),
        ),
        out_specs=(P("space", None, None, "filt"), P(), P(None, None, "filt")),
        check_vma=False,
    )
```

```python
import functools
import math

import jax
import jax.numpy as jnp
from jax import lax
from jax.experimental import pallas as pl
from jax.experimental.pallas import tpu as pltpu
from jax.sharding import PartitionSpec as P

MESH = pl.DeviceIdType.MESH
BF = jnp.bfloat16
F32 = jnp.float32
SPACE, FILT, CHIPS = 16, 8, 64
DIRS = [(ds, df) for ds in (-1, 0, 1) for df in (-1, 0, 1) if ds or df]
GROUP = 4
DIRECT = 15
SHARE = 3
OWNERS = 7


def rcopy(src, dst, send_sem, recv_sem, device):
    return pltpu.make_async_remote_copy(
        src_ref=src,
        dst_ref=dst,
        send_sem=send_sem,
        recv_sem=recv_sem,
        device_id=device,
        device_id_type=MESH,
    )


def sigmoid(v):
    return 1.0 / (1.0 + jnp.exp(-v))


def shift_rows(v, step):
    size = v.shape[1]
    row = lax.broadcasted_iota(jnp.int32, v.shape, 1)
    edge = size - 1 if step == 1 else 0
    rolled = pltpu.roll(v, (-step) % size, 1)
    return jnp.where(row == edge, 0.0, rolled)


def dot(a, b):
    return lax.dot_general(a, b, (((1,), (0,)), ((), ())), preferred_element_type=F32)


def dot_t(a, b):
    return lax.dot_general(a, b, (((1,), (1,)), ((), ())), preferred_element_type=F32)


def edges(step, size):
    if step == 1:
        return size - 1, 0, 1
    if step == -1:
        return 0, size + 1, 1
    return 0, 1, size


def swap_cells(ref, v):
    halves = []
    for h in range(2):
        ref[h] = v[:, 128 * h : 128 * h + 128]
        rows = [ref[h, pl.ds(64 * x + n, 8, stride=8), :] for x in range(2) for n in range(8)]
        halves.append(jnp.concatenate(rows, axis=0))
    return jnp.concatenate(halves, axis=1)


class Halo:
    def __init__(self, source, base, padded, nx, ny, sems, s, f):
        self.items = []
        for k, (ds, df) in enumerate(DIRS):
            sx, dx, lx = edges(ds, nx)
            sy, dy, ly = edges(df, ny)
            src = source.at[base + sx : base + sx + lx, base + sy : base + sy + ly]
            dst = padded.at[dx : dx + lx, dy : dy + ly]
            to_s, to_f, from_s, from_f = s + ds, f + df, s - ds, f - df
            send = (to_s >= 0) & (to_s < SPACE) & (to_f >= 0) & (to_f < FILT)
            recv = (from_s >= 0) & (from_s < SPACE) & (from_f >= 0) & (from_f < FILT)
            copy = rcopy(src, dst, sems.at[0, k], sems.at[1, k], (to_s, to_f))
            self.items.append((copy, send, recv))

    def start(self):
        for copy, send, _ in self.items:
            pl.when(send)(copy.start)

    def wait_recv(self):
        for copy, _, recv in self.items:
            pl.when(recv)(copy.wait_recv)

    def wait_send(self):
        for copy, send, _ in self.items:
            pl.when(send)(copy.wait_send)


def zero_rim(padded, nx, ny, s, f):
    shape = padded.shape

    @pl.when(s == 0)
    def _():
        padded[0:1] = jnp.zeros((1,) + shape[1:], padded.dtype)

    @pl.when(s == SPACE - 1)
    def _():
        padded[nx + 1 : nx + 2] = jnp.zeros((1,) + shape[1:], padded.dtype)

    @pl.when(f == 0)
    def _():
        padded[:, 0:1] = jnp.zeros((shape[0], 1) + shape[2:], padded.dtype)

    @pl.when(f == FILT - 1)
    def _():
        padded[:, ny + 1 : ny + 2] = jnp.zeros((shape[0], 1) + shape[2:], padded.dtype)


SCRATCH = dict(
    vp=((6, 18, 16, 128), BF),
    zc=((6, 18, 16, 384), BF),
    we=((9, 384, 128), BF),
    ct=((16, 32, 64), BF),
    wg=((27, 256, 128), BF),
    cs=((8, 2, 16, 128), BF),
    cr=((2, 8, 16, 128), BF),
    acc=((1024, 128), F32),
    sg=((4, 16, 16, 128), F32),
    tmp=((16, 16, 128), F32),
    cells=((2, 128, 128), F32),
    pp=((4, 10, 8, 128), BF),
    pz=((4, 10, 8, 384), F32),
    ps=((2, 66, 8, 128), BF),
    ps3=((2, 66, 8, 384), F32),
    bs=((2, 8, 16, 128), BF),
    br=((8, 2, 16, 128), BF),
    gp=((4, 10, 8, 256), BF),
    gf=((4, 10, 8, 256), F32),
    gs=((2, 3, 8, 16, 128), BF),
    gr=((2, 3, 16, 1024), BF),
    gt=((128, 1024), BF),
    xs=((7, 64, 512), BF),
    xr=((7, 64, 512), BF),
    xo=((7, 64, 512), F32),
    es=((7, 8, 8, 512), BF),
    er=((64, 8, 512), BF),
    ea=((2, 7, 8, 8, 512), BF),
    bo=((16, 32, 64), BF),
    gd=((27, 32, 128), F32),
    pb=((1024, 1152), BF),
    hs=((48, 1152), BF),
    hr=((48, 1152), BF),
    ho=((48, 1152), F32),
    dsd=((28, 16, 128), BF),
    dr=((8, 4, 16, 128), BF),
    da=((2, 28, 16, 128), BF),
)
SEMS = dict(
    local=(4,),
    halo_v=(2, 8),
    halo_p=(2, 8),
    halo_g=(2, 8),
    s_cot=(2, 8),
    s_wa=(2, 8),
    s_wb=(2, 8),
    s_wy=(2, 4),
    s_wrel=(2, 5),
    s_ps=(2, 8),
    s_bo=(2, 8),
    s_g=(2, 8),
    s_x=(2, 7),
    s_rs=(7,),
    r_rs=(1,),
    s_ag=(1,),
    r_ag=(8,),
    s_ear=(2, 8),
    s_out=(2,),
    s_ea=(2, 8),
    s_h=(2,),
    s_drs=(2, 8),
    s_dag=(2, 8),
    s_dar=(2,),
)


def kernel(early_scale, deep_scale, vol, we_in, wd_in, ct_in, bo_out, ea_out, gd_out, *scratch):
    r = dict(zip(list(SCRATCH) + list(SEMS), scratch))
    ready = scratch[-1]
    s = lax.axis_index("space")
    f = lax.axis_index("filt")
    core = lax.rem(s, 2)
    other = 1 - core
    sib = s + 1 - 2 * core
    j = lax.div(s, 2)

    def filt_peer(k):
        return lax.rem(f + k, FILT)

    def filt_from(k):
        return lax.rem(f + FILT - k, FILT)

    chips_s = [lax.rem(s + 2 * dj, SPACE) for dj in range(8)]
    chips_f = [lax.rem(f + df, FILT) for df in range(8)]
    owner = j < OWNERS

    barrier = pltpu.get_barrier_semaphore()

    def space_chip(k):
        return lax.rem(s + 2 * k, SPACE)

    greeted = [(s, filt_peer(k)) for k in range(1, FILT)]
    greeted += [(space_chip(k), f) for k in range(1, 8)]
    greeted += [
        (lax.rem(s + d, SPACE), lax.rem(f + df, FILT))
        for d in (1, SPACE - 1)
        for df in (0, 1, FILT - 1)
    ]
    for device in greeted:
        pl.semaphore_signal(barrier, inc=1, device_id=device, device_id_type=MESH)

    own_vol = pltpu.make_async_copy(vol, r["vp"].at[1:5, 1:17], r["local"].at[0])
    own_vol.start()
    wg = r["wg"]
    w_rows = pl.ds(pl.multiple_of(128 * core + 16 * f, 16), 16)
    w_half = pl.ds(pl.multiple_of(16 * core, 16), 16)
    y = lax.div(s, 4)

    def share(yy):
        return pl.ds(DIRECT + SHARE * yy, SHARE)

    own_wd = [
        pltpu.make_async_copy(wd_in.at[taps, w_half], wg.at[taps, w_rows], r["local"].at[n])
        for n, taps in ((1, pl.ds(0, DIRECT)), (3, share(y)))
    ]
    for c in own_wd:
        c.start()
    own_ct = pltpu.make_async_copy(ct_in, r["ct"], r["local"].at[2])
    own_ct.start()
    own_ct.wait()
    lane = lax.broadcasted_iota(jnp.int32, (32, 128), 1)
    parts = [jnp.zeros((32, 128), F32)] * FILT
    for p in range(16):
        x = r["ct"][p].astype(F32)
        x = jnp.concatenate([x, x], axis=1)
        for q in range(FILT):
            moved = pltpu.roll(x, (8 * p - 8 * q) % 128, 1)
            parts[q] = jnp.where(lane // 8 == p, moved, parts[q])
    for q in range(FILT):
        r["cs"][q] = parts[q].astype(BF).reshape(2, 16, 128)
    zero_rim(r["vp"], 4, 16, s, f)
    zero_rim(r["pp"], 2, 8, s, f)
    zero_rim(r["gp"], 2, 8, s, f)
    r["ps"][:, 0:1] = jnp.zeros((2, 1, 8, 128), BF)
    r["ps"][:, 65:66] = jnp.zeros((2, 1, 8, 128), BF)

    pl.semaphore_wait(barrier, len(greeted))
    halo_v = Halo(vol, 0, r["vp"], 4, 16, r["halo_v"], s, f)
    halo_v.start()
    own_we = pltpu.make_async_copy(we_in, r["we"], r["local"].at[2])
    own_we.start()

    def w_send(taps, sems, k):
        return rcopy(
            wd_in.at[taps, w_half],
            wg.at[taps, w_rows],
            r[sems].at[0, k],
            r[sems].at[1, k],
            (s, filt_peer(k)),
        )

    for k in range(1, 8):
        pl.semaphore_signal(ready, inc=1, device_id=(space_chip(k), f), device_id_type=MESH)

    wb = []
    for k in range(1, FILT):
        wb.append(w_send(share(y), "s_wb", k))
        wb[-1].start()
    cots = []
    for k in range(1, FILT):
        cots.append(
            rcopy(
                r["cs"].at[filt_peer(k)],
                r["cr"].at[:, f],
                r["s_cot"].at[0, k],
                r["s_cot"].at[1, k],
                (s, filt_peer(k)),
            )
        )
        cots[-1].start()
    wa = []
    for k in range(1, FILT):
        wa.append(w_send(pl.ds(0, DIRECT), "s_wa", k))
        wa[-1].start()
    r["cr"][:, pl.ds(f, 1)] = r["cs"][pl.ds(f, 1)].reshape(2, 1, 16, 128)

    own_vol.wait()
    halo_v.wait_recv()
    for c in own_wd:
        c.wait()
    for c in wb:
        c.wait_recv()
    w_core = pl.ds(pl.multiple_of(128 * core, 128), 128)

    def w_pass(taps, sems, k, device):
        piece = wg.at[taps, w_core]
        return rcopy(piece, piece, r[sems].at[0, k], r[sems].at[1, k], device)

    wy = []
    for k in range(1, 4):
        wy.append(w_pass(share(y), "s_wy", k, (lax.rem(s + 4 * k, SPACE), f)))
        wy[-1].start()
    relay = [w_pass(share(y), "s_wrel", 0, (sib, f))]
    relay[-1].start()
    zc = r["zc"]
    for row in range(6):
        x = r["vp"][row].astype(F32)
        zc[row, :, :, 0:128] = shift_rows(x, -1).astype(BF)
        zc[row, :, :, 128:256] = r["vp"][row]
        zc[row, :, :, 256:384] = shift_rows(x, 1).astype(BF)
    own_we.wait()
    acc = r["acc"]
    for ab in range(9):
        a, b = ab // 3, ab % 3
        patch = zc[a : a + 4, b : b + 16].reshape(1024, 384)
        term = dot(patch, r["we"][ab])
        if ab == 0:
            acc[...] = term
        else:
            acc[...] += term
    for half in range(2):
        v = acc[512 * half : 512 * half + 512].reshape(2, 16, 16, 128)
        sig = sigmoid(v)
        r["sg"][2 * half : 2 * half + 2] = sig * (1.0 + v * (1.0 - sig)) * 0.125
        act = v * sig
        act = (act[0] + act[1]).reshape(8, 2, 16, 128)
        r["tmp"][8 * half : 8 * half + 8] = act[:, 0] + act[:, 1]
    tmp = r["tmp"]
    pooled = (tmp[:, pl.ds(0, 8, stride=2), :] + tmp[:, pl.ds(1, 8, stride=2), :]) * 0.125
    pooled = pooled.reshape(2, 8, 8, 128).astype(BF)
    r["pp"][1:3, 1:9] = pooled
    halo_p = Halo(r["pp"], 1, r["pp"], 2, 8, r["halo_p"], s, f)
    halo_p.start()
    r["ps"][:, pl.ds(1 + 8 * f, 8)] = pooled

    for c in wa:
        c.wait_recv()
    relay.append(w_pass(pl.ds(0, DIRECT), "s_wrel", 4, (sib, f)))
    relay[-1].start()
    for k in range(1, 4):
        wy[k - 1].wait_recv()
        relay.append(w_pass(share(lax.rem(y + 4 - k, 4)), "s_wrel", k, (sib, f)))
        relay[-1].start()
    for c in cots:
        c.wait_recv()
    cot = swap_cells(r["cells"], r["cr"][...].reshape(256, 128).astype(F32).T)
    halo_p.wait_recv()
    pz = r["pz"]
    for row in range(4):
        x = r["pp"][row].astype(F32)
        pz[row, :, :, 0:128] = shift_rows(x, -1)
        pz[row, :, :, 128:256] = x
        pz[row, :, :, 256:384] = shift_rows(x, 1)
    for c in relay:
        c.wait_recv()

    pre = jnp.zeros((128, 256), F32)
    for ab in range(9):
        a, b = ab // 3, ab % 3
        patch = pz[a : a + 2, b : b + 8].reshape(128, 384).astype(BF)
        taps = jnp.concatenate([wg[3 * ab + c] for c in range(3)], axis=1)
        pre = pre + dot_t(patch, taps)
    sig = sigmoid(pre)
    g = (cot * (sig * (1.0 + pre * (1.0 - sig)))).astype(BF)
    r["gp"][1:3, 1:9] = g.astype(F32).reshape(2, 8, 8, 256).astype(BF)
    halo_g = Halo(r["gp"], 1, r["gp"], 2, 8, r["halo_g"], s, f)
    halo_g.start()
    pss = []
    for k in range(1, FILT):
        pss.append(
            rcopy(
                r["pp"].at[1:3, 1:9],
                r["ps"].at[:, pl.ds(1 + 8 * f, 8)],
                r["s_ps"].at[0, k],
                r["s_ps"].at[1, k],
                (s, filt_peer(k)),
            )
        )
        pss[-1].start()
    act = swap_cells(r["cells"], pre * sig)
    r["bs"][...] = act.T.astype(BF).reshape(2, 8, 16, 128)
    bos = []
    for k in range(1, FILT):
        bos.append(
            rcopy(
                r["bs"].at[:, filt_peer(k)],
                r["br"].at[f],
                r["s_bo"].at[0, k],
                r["s_bo"].at[1, k],
                (s, filt_peer(k)),
            )
        )
        bos[-1].start()
    r["br"][pl.ds(f, 1)] = r["bs"][:, pl.ds(f, 1)].reshape(1, 2, 16, 128)

    halo_g.wait_recv()
    gf = r["gf"]
    gf[...] = r["gp"][...].astype(F32)
    back = jnp.zeros((128, 384), F32)
    for ab in range(9):
        a, b = ab // 3, ab % 3
        patch = gf[2 - a : 4 - a, 2 - b : 10 - b].reshape(128, 256).astype(BF)
        taps = jnp.concatenate([wg[3 * ab + c] for c in range(3)], axis=1)
        back = back + dot(patch, taps)
    back = back.reshape(16, 8, 384)
    gpool = (
        shift_rows(back[:, :, 0:128], 1)
        + back[:, :, 128:256]
        + shift_rows(back[:, :, 256:384], -1)
    )
    gpool = gpool.astype(BF).astype(F32)
    tmp[:, pl.ds(0, 8, stride=2), :] = gpool
    tmp[:, pl.ds(1, 8, stride=2), :] = gpool
    for row in range(4):
        spread = tmp[8 * (row // 2) : 8 * (row // 2) + 8]
        spread = jnp.broadcast_to(spread[:, None], (8, 2, 16, 128)).reshape(16, 16, 128)
        grad = (spread * r["sg"][row]).astype(BF).astype(F32).reshape(256, 128)
        r["gt"][:, 256 * row : 256 * row + 256] = grad.T.astype(BF)

    gt = r["gt"][...]
    es, er, ea = r["es"], r["er"], r["ea"]
    pl.semaphore_wait(ready, 7)

    def group_of(k):
        return lax.rem(j + k, OWNERS)

    def x_copy(k):
        return rcopy(
            r["xs"].at[k], r["xr"].at[k], r["s_x"].at[0, k], r["s_x"].at[1, k], (sib, f)
        )

    for k in range(OWNERS + 1):
        if k < OWNERS:
            patches = []
            for n in range(GROUP):
                t = jnp.minimum(GROUP * group_of(k) + n, 26)
                a, b, c = lax.div(t, 9), lax.rem(lax.div(t, 3), 3), lax.rem(t, 3)
                lanes = pl.ds(pl.multiple_of(128 * c, 128), 128)
                patch = zc[pl.ds(a, 4), pl.ds(b, 16), :, lanes]
                patches.append(patch.reshape(1024, 128))
            term = dot(gt, jnp.concatenate(patches, axis=1))

            @pl.when(core == 0)
            def _():
                r["xo"][k] = term[0:64]
                r["xs"][k] = term[64:128].astype(BF)

            @pl.when(core == 1)
            def _():
                r["xo"][k] = term[64:128]
                r["xs"][k] = term[0:64].astype(BF)

            x_copy(k).start()
        if k >= 1:
            p = k - 1
            x_copy(p).wait_recv()
            total = r["xo"][p] + r["xr"][p].astype(F32)
            es[p] = total.reshape(8, 8, 512).astype(BF)
            to_j = group_of(p)
            dj = lax.rem(to_j - j + 8, 8)
            for df in range(8):
                copy = rcopy(
                    es.at[p, chips_f[df]],
                    er.at[8 * dj + df],
                    r["s_rs"].at[p],
                    r["r_rs"].at[0],
                    (2 * to_j + core, chips_f[df]),
                )
                if p == 0 and df == 0:
                    pl.when(j >= OWNERS)(copy.start)
                else:
                    copy.start()

    for a in range(3):
        piece = gf[2 - a : 4 - a, 1:9].reshape(128, 256)
        r["gs"][:, a] = piece.T.astype(BF).reshape(2, 8, 16, 128)
    gcs = []
    lanes = pl.ds(pl.multiple_of(128 * f, 128), 128)
    for k in range(1, FILT):
        gcs.append(
            rcopy(
                r["gs"].at[:, :, filt_peer(k)],
                r["gr"].at[:, :, :, lanes],
                r["s_g"].at[0, k],
                r["s_g"].at[1, k],
                (s, filt_peer(k)),
            )
        )
        gcs[-1].start()
    r["gr"][:, :, :, lanes] = r["gs"][:, :, pl.ds(f, 1)].reshape(2, 3, 16, 128)

    for c in pss:
        c.wait_recv()
    ps3 = r["ps3"]
    for row in range(2):
        x = r["ps"][row].astype(F32)
        ps3[row, :, :, 0:128] = shift_rows(x, -1)
        ps3[row, :, :, 128:256] = x
        ps3[row, :, :, 256:384] = shift_rows(x, 1)
    for q in range(8):
        for b in range(3):
            patch = ps3[:, 8 * q + b : 8 * q + b + 8].reshape(128, 384).astype(BF)
            r["pb"][128 * q : 128 * q + 128, 384 * b : 384 * b + 384] = patch
    for c in gcs:
        c.wait_recv()
    deep = dot(r["gr"][...].reshape(96, 1024), r["pb"][...])

    @pl.when(core == 0)
    def _():
        r["ho"][...] = deep[0:48]
        r["hs"][...] = deep[48:96].astype(BF)

    @pl.when(core == 1)
    def _():
        r["ho"][...] = deep[48:96]
        r["hs"][...] = deep[0:48].astype(BF)

    hcopy = rcopy(r["hs"], r["hr"], r["s_h"].at[0], r["s_h"].at[1], (sib, f))
    hcopy.start()

    for c in bos:
        c.wait_recv()
    parts = [jnp.zeros((32, 128), F32)] * 16
    for q in range(FILT):
        x = r["br"][q].reshape(32, 128).astype(F32)
        for p in range(16):
            moved = pltpu.roll(x, (8 * q - 8 * p) % 128, 1)
            parts[p] = jnp.where(lane // 8 == q, moved, parts[p])
    for p in range(16):
        r["bo"][p] = parts[p][:, 0:64].astype(BF)
    bo_copy = pltpu.make_async_copy(r["bo"], bo_out, r["s_out"].at[0])
    bo_copy.start()

    hcopy.wait_recv()
    dsd = r["dsd"]
    dsd[27:28] = jnp.zeros((1, 16, 128), BF)
    total = r["ho"][...] + r["hr"][...].astype(F32)
    for a in range(3):
        for bc in range(9):
            dsd[9 * a + bc] = total[16 * a : 16 * a + 16, 128 * bc : 128 * bc + 128].astype(BF)

    def first_of(jj):
        return jnp.minimum(GROUP * jj, GROUP * (OWNERS - 1))

    drs = []
    for k in range(1, 8):
        to_s = space_chip(k)
        to_j = lax.div(to_s, 2)
        copy = rcopy(
            dsd.at[pl.ds(first_of(to_j), GROUP)],
            r["dr"].at[k],
            r["s_drs"].at[0, k],
            r["s_drs"].at[1, k],
            (to_s, f),
        )
        pl.when(to_j < OWNERS)(copy.start)
        drs.append((copy, to_j < OWNERS))

    mine_t = pl.ds(first_of(j), GROUP)

    ag_sends = []
    for k in range(1, CHIPS):
        piece = ea.at[core, jnp.minimum(j, OWNERS - 1), f]
        device = (chips_s[k // 8], chips_f[k % 8])
        ag_sends.append(rcopy(piece, piece, r["s_ag"].at[0], r["r_ag"].at[k // 8], device))

    @pl.when(owner)
    def _():
        er[0] = es[0, pl.ds(f, 1)].reshape(8, 512)
        landed = er.at[1:CHIPS]
        rcopy(landed, landed, r["s_rs"].at[0], r["r_rs"].at[0], (s, f)).wait_recv()
        total = jnp.sum(er[0:8].astype(F32), axis=0)
        for n in range(1, 8):
            total = total + jnp.sum(er[8 * n : 8 * n + 8].astype(F32), axis=0)
        total = (total * early_scale).astype(BF).reshape(1, 1, 1, 8, 512)
        ea[pl.ds(core, 1), pl.ds(j, 1), pl.ds(f, 1)] = total
        for c in ag_sends:
            c.start()

    da = r["da"]
    piece = da.at[core, mine_t]
    dag = []
    for k in range(1, 8):
        dag.append(
            rcopy(piece, piece, r["s_dag"].at[0, k], r["s_dag"].at[1, k], (space_chip(k), f))
        )

    @pl.when(owner)
    def _():
        total = dsd[mine_t].astype(F32)
        for k in range(1, 8):
            drs[k - 1][0].wait_recv()
            total = total + r["dr"][k].astype(F32)
        da[pl.ds(core, 1), mine_t] = (total * deep_scale).astype(BF).reshape(1, GROUP, 16, 128)
        for c in dag:
            c.start()

    for k in range(1, 8):
        from_j = lax.div(lax.rem(s + SPACE - 2 * k, SPACE), 2)
        pl.when(from_j < OWNERS)(dag[k - 1].wait_recv)
    dar = rcopy(da.at[core], da.at[core], r["s_dar"].at[0], r["s_dar"].at[1], (sib, f))
    dar.start()

    dar.wait_recv()
    for t in range(27):
        r["gd"][t] = da[:, t].reshape(32, 128).astype(F32)
    gd_copy = pltpu.make_async_copy(r["gd"], gd_out, r["s_out"].at[1])
    gd_copy.start()

    def ear_copy(dj):
        piece = ea.at[core, lax.rem(j - dj + 8, 8)]
        return rcopy(piece, piece, r["s_ear"].at[0, dj], r["s_ear"].at[1, dj], (sib, f))

    def ea_copy(half, dj):
        g = lax.rem(j - dj + 8, 8)
        return pltpu.make_async_copy(ea.at[half, g], ea_out.at[half, g], r["s_ea"].at[half, dj])

    for dj in range(8):

        @pl.when(lax.rem(j - dj + 8, 8) < OWNERS)
        def _():
            landed = ea.at[core, lax.rem(j - dj + 8, 8), 0 : (8 if dj else 7)]
            rcopy(landed, landed, r["s_ag"].at[0], r["r_ag"].at[dj], (s, f)).wait_recv()
            ear_copy(dj).start()
            ea_copy(core, dj).start()

    for dj in range(8):

        @pl.when(lax.rem(j - dj + 8, 8) < OWNERS)
        def _():
            ear_copy(dj).wait_recv()
            ea_copy(other, dj).start()

    for h in (halo_v, halo_p, halo_g):
        h.wait_send()
    for c in cots + wa + wb + wy + relay + pss + bos + gcs + [hcopy, dar]:
        c.wait_send()
    for copy, active in drs:
        pl.when(active)(copy.wait_send)

    for k in range(OWNERS):
        x_copy(k).wait_send()

    def rs_sent(k, count):
        left = es.at[k, 0:count]
        rcopy(left, left, r["s_rs"].at[k], r["r_rs"].at[0], (s, f)).wait_send()

    for k in range(1, OWNERS):
        rs_sent(k, 8)

    @pl.when(owner)
    def _():
        rs_sent(0, 7)
        left = er.at[1:CHIPS]
        rcopy(left, left, r["s_ag"].at[0], r["r_rs"].at[0], (s, f)).wait_send()
        for c in dag:
            c.wait_send()

    pl.when(j >= OWNERS)(functools.partial(rs_sent, 0, 8))
    for dj in range(8):

        @pl.when(lax.rem(j - dj + 8, 8) < OWNERS)
        def _():
            ear_copy(dj).wait_send()
            ea_copy(core, dj).wait()
            ea_copy(other, dj).wait()

    bo_copy.wait()
    gd_copy.wait()


def results(bo_in, ea_in, gd_in, bo_out, ge_out, gd_out, bo, ea, gd, ge, sems):
    ins = [pltpu.make_async_copy(ea_in.at[:, g], ea.at[g], sems.at[0, g]) for g in range(OWNERS)]
    ins.append(pltpu.make_async_copy(bo_in, bo, sems.at[0, 7]))
    ins.append(pltpu.make_async_copy(gd_in, gd, sems.at[0, 8]))
    outs = []
    for g in range(OWNERS):
        taps = min(GROUP, 27 - GROUP * g)
        src, dst = ge.at[pl.ds(GROUP * g, taps)], ge_out.at[pl.ds(GROUP * g, taps)]
        outs.append(pltpu.make_async_copy(src, dst, sems.at[1, g]))
    outs.append(pltpu.make_async_copy(bo, bo_out, sems.at[1, 7]))
    outs.append(pltpu.make_async_copy(gd, gd_out, sems.at[1, 8]))
    for c in ins:
        c.start()
    for g in range(OWNERS):
        ins[g].wait()
        block = ea[g].reshape(128, 512).astype(F32)
        for t in range(GROUP * g, min(GROUP * g + GROUP, 27)):
            n = t - GROUP * g
            ge[t] = block[:, 128 * n : 128 * n + 128].T
        outs[g].start()
    for n in (7, 8):
        ins[n].wait()
        outs[n].start()
    for c in outs:
        c.wait()


def shards(volume, w_early, w_deep, cotangent):
    any_ = pl.BlockSpec(memory_space=pl.ANY)
    cells = volume.shape[0] * volume.shape[1] * volume.shape[2] * SPACE * FILT
    body = functools.partial(kernel, 1.0 / math.sqrt(cells), 1.0 / math.sqrt(cells // 8))
    block, early, deep = pl.pallas_call(
        body,
        out_shape=(
            jax.ShapeDtypeStruct((16, 32, 64), BF),
            jax.ShapeDtypeStruct((2, 7, 8, 8, 512), BF),
            jax.ShapeDtypeStruct((27, 32, 128), F32),
        ),
        in_specs=[any_] * 4,
        out_specs=(any_,) * 3,
        scratch_shapes=[pltpu.VMEM(*v) for v in SCRATCH.values()]
        + [pltpu.SemaphoreType.DMA(v) for v in SEMS.values()]
        + [pltpu.SemaphoreType.REGULAR],
        compiler_params=pltpu.CompilerParams(
            collective_id=0, has_side_effects=True, vmem_limit_bytes=56 << 20
        ),
        name="step",
    )(
        volume,
        w_early.reshape(9, 384, 128),
        w_deep.transpose(0, 2, 1),
        cotangent.transpose(0, 2, 3, 1).reshape(16, 32, 64),
    )
    block, early, deep = pl.pallas_call(
        results,
        out_shape=(
            jax.ShapeDtypeStruct((16, 32, 64), BF),
            jax.ShapeDtypeStruct((27, 128, 128), F32),
            jax.ShapeDtypeStruct((27, 32, 128), F32),
        ),
        in_specs=[any_] * 3,
        out_specs=(any_,) * 3,
        scratch_shapes=[
            pltpu.VMEM((16, 32, 64), BF),
            pltpu.VMEM((7, 2, 8, 8, 512), BF),
            pltpu.VMEM((27, 32, 128), F32),
            pltpu.VMEM((27, 128, 128), F32),
            pltpu.SemaphoreType.DMA((2, 9)),
        ],
        compiler_params=pltpu.CompilerParams(vmem_limit_bytes=60 << 20),
        name="results",
    )(block, early, deep)
    block = block.reshape(2, 8, 32, 64).transpose(0, 3, 1, 2)
    return block, early, deep.transpose(0, 2, 1)


def solution(mesh):
    return jax.shard_map(
        shards,
        mesh=mesh,
        in_specs=(
            P("space", "filt", None, None),
            P(),
            P(None, None, "filt"),
            P("space", None, None, "filt"),
        ),
        out_specs=(P("space", None, None, "filt"), P(), P(None, None, "filt")),
        check_vma=False,
    )
```

```python
import functools
import math

import jax
import jax.numpy as jnp
from jax import lax
from jax.experimental import pallas as pl
from jax.experimental.pallas import tpu as pltpu
from jax.sharding import PartitionSpec as P

MESH = pl.DeviceIdType.MESH
BF = jnp.bfloat16
F32 = jnp.float32
SPACE, FILT, CHIPS = 16, 8, 64
DIRS = [(ds, df) for ds in (-1, 0, 1) for df in (-1, 0, 1) if ds or df]
GROUP = 4
DIRECT = 15
SHARE = 3
OWNERS = 7


def rcopy(src, dst, send_sem, recv_sem, device):
    return pltpu.make_async_remote_copy(
        src_ref=src,
        dst_ref=dst,
        send_sem=send_sem,
        recv_sem=recv_sem,
        device_id=device,
        device_id_type=MESH,
    )


def sigmoid(v):
    return 1.0 / (1.0 + jnp.exp(-v))


def shift_rows(v, step):
    size = v.shape[1]
    row = lax.broadcasted_iota(jnp.int32, v.shape, 1)
    edge = size - 1 if step == 1 else 0
    rolled = pltpu.roll(v, (-step) % size, 1)
    return jnp.where(row == edge, 0.0, rolled)


def dot(a, b):
    return lax.dot_general(a, b, (((1,), (0,)), ((), ())), preferred_element_type=F32)


def dot_t(a, b):
    return lax.dot_general(a, b, (((1,), (1,)), ((), ())), preferred_element_type=F32)


def edges(step, size, width):
    if step == 1:
        return size - width, 0, width
    if step == -1:
        return 0, size + width, width
    return 0, width, size


def swap_cells(ref, v):
    halves = []
    for h in range(2):
        ref[h] = v[:, 128 * h : 128 * h + 128]
        rows = [ref[h, pl.ds(64 * x + n, 8, stride=8), :] for x in range(2) for n in range(8)]
        halves.append(jnp.concatenate(rows, axis=0))
    return jnp.concatenate(halves, axis=1)


class Halo:
    def __init__(self, source, base, padded, nx, ny, width, sems, s, f):
        self.items = []
        for k, (ds, df) in enumerate(DIRS):
            sx, dx, lx = edges(ds, nx, width)
            sy, dy, ly = edges(df, ny, width)
            src = source.at[base + sx : base + sx + lx, base + sy : base + sy + ly]
            dst = padded.at[dx : dx + lx, dy : dy + ly]
            to_s, to_f, from_s, from_f = s + ds, f + df, s - ds, f - df
            send = (to_s >= 0) & (to_s < SPACE) & (to_f >= 0) & (to_f < FILT)
            recv = (from_s >= 0) & (from_s < SPACE) & (from_f >= 0) & (from_f < FILT)
            copy = rcopy(src, dst, sems.at[0, k], sems.at[1, k], (to_s, to_f))
            self.items.append((copy, send, recv))

    def start(self):
        for copy, send, _ in self.items:
            pl.when(send)(copy.start)

    def wait_recv(self):
        for copy, _, recv in self.items:
            pl.when(recv)(copy.wait_recv)

    def wait_send(self):
        for copy, send, _ in self.items:
            pl.when(send)(copy.wait_send)


def zero_rim(padded, nx, ny, width, s, f):
    shape = padded.shape
    w = width

    @pl.when(s == 0)
    def _():
        padded[0:w] = jnp.zeros((w,) + shape[1:], padded.dtype)

    @pl.when(s == SPACE - 1)
    def _():
        padded[nx + w : nx + 2 * w] = jnp.zeros((w,) + shape[1:], padded.dtype)

    @pl.when(f == 0)
    def _():
        padded[:, 0:w] = jnp.zeros((shape[0], w) + shape[2:], padded.dtype)

    @pl.when(f == FILT - 1)
    def _():
        padded[:, ny + w : ny + 2 * w] = jnp.zeros((shape[0], w) + shape[2:], padded.dtype)


SCRATCH = dict(
    vp=((6, 18, 16, 128), BF),
    zc=((6, 18, 16, 384), BF),
    we=((9, 384, 128), BF),
    ct=((16, 32, 64), BF),
    wg=((27, 256, 128), BF),
    cs=((8, 2, 2, 16, 128), BF),
    cr=((4, 2, 8, 16, 128), BF),
    acc=((1024, 128), F32),
    sg=((4, 16, 16, 128), F32),
    tmp=((16, 16, 128), F32),
    cells=((2, 128, 128), F32),
    act=((128, 256), F32),
    pp=((6, 12, 8, 128), BF),
    pz=((6, 12, 8, 384), F32),
    ps=((2, 66, 8, 128), BF),
    ps3=((2, 66, 8, 384), F32),
    bs=((2, 8, 16, 128), BF),
    br=((8, 2, 16, 128), BF),
    gf=((4, 10, 8, 256), F32),
    gs=((2, 3, 8, 16, 128), BF),
    gr=((2, 3, 16, 1024), BF),
    gt=((128, 1024), BF),
    xs=((7, 64, 512), BF),
    xr=((7, 64, 512), BF),
    xo=((7, 64, 512), F32),
    es=((7, 8, 8, 512), BF),
    er=((64, 8, 512), BF),
    ea=((2, 7, 8, 8, 512), BF),
    bo=((16, 32, 64), BF),
    gd=((27, 32, 128), F32),
    pb=((1024, 1152), BF),
    hs=((48, 1152), BF),
    hr=((48, 1152), BF),
    ho=((48, 1152), F32),
    dsd=((28, 16, 128), BF),
    dr=((8, 4, 16, 128), BF),
    da=((2, 28, 16, 128), BF),
)
SEMS = dict(
    local=(4,),
    halo_v=(2, 8),
    halo_p=(2, 8),
    s_cot=(2, 3),
    s_wa=(2, 8),
    s_wb=(2, 8),
    s_wy=(2, 4),
    s_wrel=(2, 5),
    s_ps=(2, 8),
    s_bo=(2, 8),
    s_g=(2, 8),
    s_x=(2, 7),
    s_rs=(7,),
    r_rs=(1,),
    s_ag=(1,),
    r_ag=(8,),
    s_ear=(2, 8),
    s_out=(2,),
    s_ea=(2, 8),
    s_h=(2,),
    s_drs=(2, 8),
    s_dag=(2, 8),
    s_dar=(2,),
)


def kernel(early_scale, deep_scale, vol, we_in, wd_in, ct_in, bo_out, ea_out, gd_out, *scratch):
    r = dict(zip(list(SCRATCH) + list(SEMS), scratch))
    ready = scratch[-1]
    s = lax.axis_index("space")
    f = lax.axis_index("filt")
    core = lax.rem(s, 2)
    other = 1 - core
    sib = s + 1 - 2 * core
    j = lax.div(s, 2)

    def filt_peer(k):
        return lax.rem(f + k, FILT)

    def filt_from(k):
        return lax.rem(f + FILT - k, FILT)

    chips_s = [lax.rem(s + 2 * dj, SPACE) for dj in range(8)]
    chips_f = [lax.rem(f + df, FILT) for df in range(8)]
    owner = j < OWNERS

    barrier = pltpu.get_barrier_semaphore()

    def space_chip(k):
        return lax.rem(s + 2 * k, SPACE)

    greeted = [(s, filt_peer(k)) for k in range(1, FILT)]
    greeted += [(space_chip(k), f) for k in range(1, 8)]
    greeted += [
        (lax.rem(s + d, SPACE), lax.rem(f + df, FILT))
        for d in (1, SPACE - 1)
        for df in range(FILT)
    ]
    for device in greeted:
        pl.semaphore_signal(barrier, inc=1, device_id=device, device_id_type=MESH)

    own_vol = pltpu.make_async_copy(vol, r["vp"].at[1:5, 1:17], r["local"].at[0])
    own_vol.start()
    wg = r["wg"]
    w_rows = pl.ds(pl.multiple_of(128 * core + 16 * f, 16), 16)
    w_half = pl.ds(pl.multiple_of(16 * core, 16), 16)
    y = lax.div(s, 4)

    def share(yy):
        return pl.ds(DIRECT + SHARE * yy, SHARE)

    own_wd = [
        pltpu.make_async_copy(wd_in.at[taps, w_half], wg.at[taps, w_rows], r["local"].at[n])
        for n, taps in ((1, pl.ds(0, DIRECT)), (3, share(y)))
    ]
    for c in own_wd:
        c.start()
    own_ct = pltpu.make_async_copy(ct_in, r["ct"], r["local"].at[2])
    own_ct.start()
    own_ct.wait()
    lane = lax.broadcasted_iota(jnp.int32, (32, 128), 1)
    for x in range(2):
        parts = [jnp.zeros((32, 128), F32)] * FILT
        for z in range(8):
            v = r["ct"][8 * x + z].astype(F32)
            v = jnp.concatenate([v, jnp.zeros_like(v)], axis=1)
            here = (lane >= 16 * z) & (lane < 16 * z + 10)
            for q in range(FILT):
                moved = pltpu.roll(v, (16 * z - 8 * q + 1) % 128, 1)
                parts[q] = jnp.where(here, moved, parts[q])
        for q in range(FILT):
            r["cs"][q, x] = parts[q].astype(BF).reshape(2, 16, 128)

    @pl.when(s == 0)
    def _():
        r["cr"][0] = jnp.zeros((2, 8, 16, 128), BF)

    @pl.when(s == SPACE - 1)
    def _():
        r["cr"][3] = jnp.zeros((2, 8, 16, 128), BF)

    zero_rim(r["vp"], 4, 16, 1, s, f)
    zero_rim(r["pp"], 2, 8, 2, s, f)
    r["ps"][:, 0:1] = jnp.zeros((2, 1, 8, 128), BF)
    r["ps"][:, 65:66] = jnp.zeros((2, 1, 8, 128), BF)

    pl.semaphore_wait(barrier, len(greeted))
    halo_v = Halo(vol, 0, r["vp"], 4, 16, 1, r["halo_v"], s, f)
    halo_v.start()
    own_we = pltpu.make_async_copy(we_in, r["we"], r["local"].at[2])
    own_we.start()

    def w_send(taps, sems, k):
        return rcopy(
            wd_in.at[taps, w_half],
            wg.at[taps, w_rows],
            r[sems].at[0, k],
            r[sems].at[1, k],
            (s, filt_peer(k)),
        )

    for k in range(1, 8):
        pl.semaphore_signal(ready, inc=1, device_id=(space_chip(k), f), device_id_type=MESH)

    wb = []
    for k in range(1, FILT):
        wb.append(w_send(share(y), "s_wb", k))
        wb[-1].start()

    wa = []
    for k in range(1, FILT):
        wa.append(w_send(pl.ds(0, DIRECT), "s_wa", k))
        wa[-1].start()

    def cot_copy(src, row, n, device):
        return rcopy(
            src, r["cr"].at[row, :, f], r["s_cot"].at[0, n], r["s_cot"].at[1, n], device
        )

    def cot_all(n):
        whole = r["cs"].at[0:7] if n == 0 else r["cr"].at[0]
        return rcopy(whole, whole, r["s_cot"].at[0, n], r["s_cot"].at[1, n], (s, f))

    for k in range(1, FILT):
        cot_copy(r["cs"].at[filt_peer(k)], slice(1, 3), 0, (s, filt_peer(k))).start()

    @pl.when(s > 0)
    def _():
        for q in range(FILT):
            cot_copy(r["cs"].at[q, 0], 3, 1, (s - 1, q)).start()

    @pl.when(s < SPACE - 1)
    def _():
        for q in range(FILT):
            cot_copy(r["cs"].at[q, 1], 0, 2, (s + 1, q)).start()

    r["cr"][1:3, :, pl.ds(f, 1)] = r["cs"][pl.ds(f, 1)].reshape(2, 2, 1, 16, 128)

    own_vol.wait()
    halo_v.wait_recv()
    for c in own_wd:
        c.wait()
    for c in wb:
        c.wait_recv()
    w_core = pl.ds(pl.multiple_of(128 * core, 128), 128)

    def w_pass(taps, sems, k, device):
        piece = wg.at[taps, w_core]
        return rcopy(piece, piece, r[sems].at[0, k], r[sems].at[1, k], device)

    wy = []
    for k in range(1, 4):
        wy.append(w_pass(share(y), "s_wy", k, (lax.rem(s + 4 * k, SPACE), f)))
        wy[-1].start()
    relay = [w_pass(share(y), "s_wrel", 0, (sib, f))]
    relay[-1].start()
    zc = r["zc"]
    for row in range(6):
        x = r["vp"][row].astype(F32)
        zc[row, :, :, 0:128] = shift_rows(x, -1).astype(BF)
        zc[row, :, :, 128:256] = r["vp"][row]
        zc[row, :, :, 256:384] = shift_rows(x, 1).astype(BF)
    own_we.wait()
    acc = r["acc"]
    for ab in range(9):
        a, b = ab // 3, ab % 3
        patch = zc[a : a + 4, b : b + 16].reshape(1024, 384)
        term = dot(patch, r["we"][ab])
        if ab == 0:
            acc[...] = term
        else:
            acc[...] += term
    for half in range(2):
        v = acc[512 * half : 512 * half + 512].reshape(2, 16, 16, 128)
        sig = sigmoid(v)
        r["sg"][2 * half : 2 * half + 2] = sig * (1.0 + v * (1.0 - sig)) * 0.125
        act = v * sig
        act = (act[0] + act[1]).reshape(8, 2, 16, 128)
        r["tmp"][8 * half : 8 * half + 8] = act[:, 0] + act[:, 1]
    tmp = r["tmp"]
    pooled = (tmp[:, pl.ds(0, 8, stride=2), :] + tmp[:, pl.ds(1, 8, stride=2), :]) * 0.125
    pooled = pooled.reshape(2, 8, 8, 128).astype(BF)
    r["pp"][2:4, 2:10] = pooled
    halo_p = Halo(r["pp"], 2, r["pp"], 2, 8, 2, r["halo_p"], s, f)
    halo_p.start()
    r["ps"][:, pl.ds(1 + 8 * f, 8)] = pooled

    for c in wa:
        c.wait_recv()
    relay.append(w_pass(pl.ds(0, DIRECT), "s_wrel", 4, (sib, f)))
    relay[-1].start()
    for k in range(1, 4):
        wy[k - 1].wait_recv()
        relay.append(w_pass(share(lax.rem(y + 4 - k, 4)), "s_wrel", k, (sib, f)))
        relay[-1].start()
    cot_all(0).wait_recv()
    pl.when(s > 0)(cot_all(2).wait_recv)
    pl.when(s < SPACE - 1)(cot_all(1).wait_recv)
    cells = r["cells"]
    cot = []
    for row in range(4):
        v = r["cr"][row].reshape(256, 128).astype(F32).T
        halves = []
        for h in range(2):
            cells[h] = v[:, 128 * h : 128 * h + 128]
            cols = [cells[h, pl.ds(col, 8, stride=16), :] for col in range(10)]
            halves.append(jnp.concatenate(cols, axis=0))
        cot.append(jnp.concatenate(halves, axis=1))
    cot = jnp.concatenate(cot, axis=0)
    halo_p.wait_recv()
    pz = r["pz"]
    for row in range(6):
        x = r["pp"][row].astype(F32)
        pz[row, :, :, 0:128] = shift_rows(x, -1)
        pz[row, :, :, 128:256] = x
        pz[row, :, :, 256:384] = shift_rows(x, 1)
    for c in relay:
        c.wait_recv()

    pss = []
    for k in range(1, FILT):
        pss.append(
            rcopy(
                r["pp"].at[2:4, 2:10],
                r["ps"].at[:, pl.ds(1 + 8 * f, 8)],
                r["s_ps"].at[0, k],
                r["s_ps"].at[1, k],
                (s, filt_peer(k)),
            )
        )
        pss[-1].start()

    pre = jnp.zeros((320, 256), F32)
    for ab in range(9):
        a, b = ab // 3, ab % 3
        patch = pz[a : a + 4, b : b + 10].reshape(320, 384).astype(BF)
        taps = jnp.concatenate([wg[3 * ab + c] for c in range(3)], axis=1)
        pre = pre + dot_t(patch, taps)
    sig = sigmoid(pre)
    g = (cot * (sig * (1.0 + pre * (1.0 - sig)))).astype(BF)
    gf = r["gf"]
    gf[...] = g.astype(F32).reshape(4, 10, 8, 256)
    r["act"][...] = (pre * sig).reshape(4, 10, 8, 256)[1:3, 1:9].reshape(128, 256)
    back = jnp.zeros((128, 384), F32)
    for ab in range(9):
        a, b = ab // 3, ab % 3
        patch = gf[2 - a : 4 - a, 2 - b : 10 - b].reshape(128, 256).astype(BF)
        taps = jnp.concatenate([wg[3 * ab + c] for c in range(3)], axis=1)
        back = back + dot(patch, taps)
    back = back.reshape(16, 8, 384)
    gpool = (
        shift_rows(back[:, :, 0:128], 1)
        + back[:, :, 128:256]
        + shift_rows(back[:, :, 256:384], -1)
    )
    gpool = gpool.astype(BF).astype(F32)
    tmp[:, pl.ds(0, 8, stride=2), :] = gpool
    tmp[:, pl.ds(1, 8, stride=2), :] = gpool
    for row in range(4):
        spread = tmp[8 * (row // 2) : 8 * (row // 2) + 8]
        spread = jnp.broadcast_to(spread[:, None], (8, 2, 16, 128)).reshape(16, 16, 128)
        grad = (spread * r["sg"][row]).astype(BF).astype(F32).reshape(256, 128)
        r["gt"][:, 256 * row : 256 * row + 256] = grad.T.astype(BF)

    gt = r["gt"][...]
    es, er, ea = r["es"], r["er"], r["ea"]
    pl.semaphore_wait(ready, 7)

    def group_of(k):
        return lax.rem(j + k, OWNERS)

    def x_copy(k):
        return rcopy(
            r["xs"].at[k], r["xr"].at[k], r["s_x"].at[0, k], r["s_x"].at[1, k], (sib, f)
        )

    gcs = []
    lanes_f = pl.ds(pl.multiple_of(128 * f, 128), 128)

    def send_gradients():
        for a in range(3):
            piece = gf[2 - a : 4 - a, 1:9].reshape(128, 256)
            r["gs"][:, a] = piece.T.astype(BF).reshape(2, 8, 16, 128)
        for k in range(1, FILT):
            gcs.append(
                rcopy(
                    r["gs"].at[:, :, filt_peer(k)],
                    r["gr"].at[:, :, :, lanes_f],
                    r["s_g"].at[0, k],
                    r["s_g"].at[1, k],
                    (s, filt_peer(k)),
                )
            )
            gcs[-1].start()
        r["gr"][:, :, :, lanes_f] = r["gs"][:, :, pl.ds(f, 1)].reshape(2, 3, 16, 128)

    for k in range(OWNERS + 1):
        if k < OWNERS:
            patches = []
            for n in range(GROUP):
                t = jnp.minimum(GROUP * group_of(k) + n, 26)
                a, b, c = lax.div(t, 9), lax.rem(lax.div(t, 3), 3), lax.rem(t, 3)
                lanes = pl.ds(pl.multiple_of(128 * c, 128), 128)
                patch = zc[pl.ds(a, 4), pl.ds(b, 16), :, lanes]
                patches.append(patch.reshape(1024, 128))
            term = dot(gt, jnp.concatenate(patches, axis=1))

            @pl.when(core == 0)
            def _():
                r["xo"][k] = term[0:64]
                r["xs"][k] = term[64:128].astype(BF)

            @pl.when(core == 1)
            def _():
                r["xo"][k] = term[64:128]
                r["xs"][k] = term[0:64].astype(BF)

            x_copy(k).start()
        if k == 1:
            send_gradients()
        if k >= 1:
            p = k - 1
            x_copy(p).wait_recv()
            total = r["xo"][p] + r["xr"][p].astype(F32)
            es[p] = total.reshape(8, 8, 512).astype(BF)
            to_j = group_of(p)
            dj = lax.rem(to_j - j + 8, 8)
            for df in range(8):
                copy = rcopy(
                    es.at[p, chips_f[df]],
                    er.at[8 * dj + df],
                    r["s_rs"].at[p],
                    r["r_rs"].at[0],
                    (2 * to_j + core, chips_f[df]),
                )
                if p == 0 and df == 0:
                    pl.when(j >= OWNERS)(copy.start)
                else:
                    copy.start()

    for c in pss:
        c.wait_recv()
    ps3 = r["ps3"]
    for row in range(2):
        x = r["ps"][row].astype(F32)
        ps3[row, :, :, 0:128] = shift_rows(x, -1)
        ps3[row, :, :, 128:256] = x
        ps3[row, :, :, 256:384] = shift_rows(x, 1)
    for q in range(8):
        for b in range(3):
            patch = ps3[:, 8 * q + b : 8 * q + b + 8].reshape(128, 384).astype(BF)
            r["pb"][128 * q : 128 * q + 128, 384 * b : 384 * b + 384] = patch
    for c in gcs:
        c.wait_recv()
    deep = dot(r["gr"][...].reshape(96, 1024), r["pb"][...])

    @pl.when(core == 0)
    def _():
        r["ho"][...] = deep[0:48]
        r["hs"][...] = deep[48:96].astype(BF)

    @pl.when(core == 1)
    def _():
        r["ho"][...] = deep[48:96]
        r["hs"][...] = deep[0:48].astype(BF)

    hcopy = rcopy(r["hs"], r["hr"], r["s_h"].at[0], r["s_h"].at[1], (sib, f))
    hcopy.start()


    act = swap_cells(r["cells"], r["act"][...])
    r["bs"][...] = act.T.astype(BF).reshape(2, 8, 16, 128)
    bos = []
    for k in range(1, FILT):
        bos.append(
            rcopy(
                r["bs"].at[:, filt_peer(k)],
                r["br"].at[f],
                r["s_bo"].at[0, k],
                r["s_bo"].at[1, k],
                (s, filt_peer(k)),
            )
        )
        bos[-1].start()
    r["br"][pl.ds(f, 1)] = r["bs"][:, pl.ds(f, 1)].reshape(1, 2, 16, 128)

    ag_sends = []
    for k in range(1, CHIPS):
        piece = ea.at[core, jnp.minimum(j, OWNERS - 1), f]
        device = (chips_s[k // 8], chips_f[k % 8])
        ag_sends.append(rcopy(piece, piece, r["s_ag"].at[0], r["r_ag"].at[k // 8], device))

    @pl.when(owner)
    def _():
        er[0] = es[0, pl.ds(f, 1)].reshape(8, 512)
        landed = er.at[1:CHIPS]
        rcopy(landed, landed, r["s_rs"].at[0], r["r_rs"].at[0], (s, f)).wait_recv()
        total = jnp.sum(er[0:8].astype(F32), axis=0)
        for n in range(1, 8):
            total = total + jnp.sum(er[8 * n : 8 * n + 8].astype(F32), axis=0)
        total = (total * early_scale).astype(BF).reshape(1, 1, 1, 8, 512)
        ea[pl.ds(core, 1), pl.ds(j, 1), pl.ds(f, 1)] = total
        for c in ag_sends:
            c.start()

    hcopy.wait_recv()
    dsd = r["dsd"]
    dsd[27:28] = jnp.zeros((1, 16, 128), BF)
    total = r["ho"][...] + r["hr"][...].astype(F32)
    for a in range(3):
        for bc in range(9):
            dsd[9 * a + bc] = total[16 * a : 16 * a + 16, 128 * bc : 128 * bc + 128].astype(BF)

    def first_of(jj):
        return jnp.minimum(GROUP * jj, GROUP * (OWNERS - 1))

    drs = []
    for k in range(1, 8):
        to_s = space_chip(k)
        to_j = lax.div(to_s, 2)
        copy = rcopy(
            dsd.at[pl.ds(first_of(to_j), GROUP)],
            r["dr"].at[k],
            r["s_drs"].at[0, k],
            r["s_drs"].at[1, k],
            (to_s, f),
        )
        pl.when(to_j < OWNERS)(copy.start)
        drs.append((copy, to_j < OWNERS))

    mine_t = pl.ds(first_of(j), GROUP)

    for c in bos:
        c.wait_recv()
    parts = [jnp.zeros((32, 128), F32)] * 16
    for q in range(FILT):
        x = r["br"][q].reshape(32, 128).astype(F32)
        for p in range(16):
            moved = pltpu.roll(x, (8 * q - 8 * p) % 128, 1)
            parts[p] = jnp.where(lane // 8 == q, moved, parts[p])
    for p in range(16):
        r["bo"][p] = parts[p][:, 0:64].astype(BF)
    bo_copy = pltpu.make_async_copy(r["bo"], bo_out, r["s_out"].at[0])
    bo_copy.start()

    da = r["da"]
    piece = da.at[core, mine_t]
    dag = []
    for k in range(1, 8):
        dag.append(
            rcopy(piece, piece, r["s_dag"].at[0, k], r["s_dag"].at[1, k], (space_chip(k), f))
        )

    @pl.when(owner)
    def _():
        total = dsd[mine_t].astype(F32)
        for k in range(1, 8):
            drs[k - 1][0].wait_recv()
            total = total + r["dr"][k].astype(F32)
        da[pl.ds(core, 1), mine_t] = (total * deep_scale).astype(BF).reshape(1, GROUP, 16, 128)
        for c in dag:
            c.start()

    def ear_copy(dj):
        piece = ea.at[core, lax.rem(j - dj + 8, 8)]
        return rcopy(piece, piece, r["s_ear"].at[0, dj], r["s_ear"].at[1, dj], (sib, f))

    def ea_copy(half, dj):
        g = lax.rem(j - dj + 8, 8)
        return pltpu.make_async_copy(ea.at[half, g], ea_out.at[half, g], r["s_ea"].at[half, dj])

    for dj in range(8):

        @pl.when(lax.rem(j - dj + 8, 8) < OWNERS)
        def _():
            landed = ea.at[core, lax.rem(j - dj + 8, 8), 0 : (8 if dj else 7)]
            rcopy(landed, landed, r["s_ag"].at[0], r["r_ag"].at[dj], (s, f)).wait_recv()
            ear_copy(dj).start()
            ea_copy(core, dj).start()

    for k in range(1, 8):
        from_j = lax.div(lax.rem(s + SPACE - 2 * k, SPACE), 2)
        pl.when(from_j < OWNERS)(dag[k - 1].wait_recv)
    dar = rcopy(da.at[core], da.at[core], r["s_dar"].at[0], r["s_dar"].at[1], (sib, f))
    dar.start()

    dar.wait_recv()
    for t in range(27):
        r["gd"][t] = da[:, t].reshape(32, 128).astype(F32)
    gd_copy = pltpu.make_async_copy(r["gd"], gd_out, r["s_out"].at[1])
    gd_copy.start()

    for dj in range(8):

        @pl.when(lax.rem(j - dj + 8, 8) < OWNERS)
        def _():
            ear_copy(dj).wait_recv()
            ea_copy(other, dj).start()

    for h in (halo_v, halo_p):
        h.wait_send()
    cot_all(0).wait_send()
    pl.when(s > 0)(cot_all(1).wait_send)
    pl.when(s < SPACE - 1)(cot_all(2).wait_send)
    for c in wa + wb + wy + relay + pss + bos + gcs + [hcopy, dar]:
        c.wait_send()
    for copy, active in drs:
        pl.when(active)(copy.wait_send)

    for k in range(OWNERS):
        x_copy(k).wait_send()

    def rs_sent(k, count):
        left = es.at[k, 0:count]
        rcopy(left, left, r["s_rs"].at[k], r["r_rs"].at[0], (s, f)).wait_send()

    for k in range(1, OWNERS):
        rs_sent(k, 8)

    @pl.when(owner)
    def _():
        rs_sent(0, 7)
        left = er.at[1:CHIPS]
        rcopy(left, left, r["s_ag"].at[0], r["r_rs"].at[0], (s, f)).wait_send()
        for c in dag:
            c.wait_send()

    pl.when(j >= OWNERS)(functools.partial(rs_sent, 0, 8))
    for dj in range(8):

        @pl.when(lax.rem(j - dj + 8, 8) < OWNERS)
        def _():
            ear_copy(dj).wait_send()
            ea_copy(core, dj).wait()
            ea_copy(other, dj).wait()

    bo_copy.wait()
    gd_copy.wait()


def results(bo_in, ea_in, gd_in, bo_out, ge_out, gd_out, bo, ea, gd, ge, sems):
    ins = [pltpu.make_async_copy(ea_in.at[:, g], ea.at[g], sems.at[0, g]) for g in range(OWNERS)]
    ins.append(pltpu.make_async_copy(bo_in, bo, sems.at[0, 7]))
    ins.append(pltpu.make_async_copy(gd_in, gd, sems.at[0, 8]))
    outs = []
    for g in range(OWNERS):
        taps = min(GROUP, 27 - GROUP * g)
        src, dst = ge.at[pl.ds(GROUP * g, taps)], ge_out.at[pl.ds(GROUP * g, taps)]
        outs.append(pltpu.make_async_copy(src, dst, sems.at[1, g]))
    outs.append(pltpu.make_async_copy(bo, bo_out, sems.at[1, 7]))
    outs.append(pltpu.make_async_copy(gd, gd_out, sems.at[1, 8]))
    for c in ins:
        c.start()
    for g in range(OWNERS):
        ins[g].wait()
        block = ea[g].reshape(128, 512).astype(F32)
        for t in range(GROUP * g, min(GROUP * g + GROUP, 27)):
            n = t - GROUP * g
            ge[t] = block[:, 128 * n : 128 * n + 128].T
        outs[g].start()
    for n in (7, 8):
        ins[n].wait()
        outs[n].start()
    for c in outs:
        c.wait()


def shards(volume, w_early, w_deep, cotangent):
    any_ = pl.BlockSpec(memory_space=pl.ANY)
    cells = volume.shape[0] * volume.shape[1] * volume.shape[2] * SPACE * FILT
    body = functools.partial(kernel, 1.0 / math.sqrt(cells), 1.0 / math.sqrt(cells // 8))
    block, early, deep = pl.pallas_call(
        body,
        out_shape=(
            jax.ShapeDtypeStruct((16, 32, 64), BF),
            jax.ShapeDtypeStruct((2, 7, 8, 8, 512), BF),
            jax.ShapeDtypeStruct((27, 32, 128), F32),
        ),
        in_specs=[any_] * 4,
        out_specs=(any_,) * 3,
        scratch_shapes=[pltpu.VMEM(*v) for v in SCRATCH.values()]
        + [pltpu.SemaphoreType.DMA(v) for v in SEMS.values()]
        + [pltpu.SemaphoreType.REGULAR],
        compiler_params=pltpu.CompilerParams(
            collective_id=0, has_side_effects=True, vmem_limit_bytes=56 << 20
        ),
        name="step",
    )(
        volume,
        w_early.reshape(9, 384, 128),
        w_deep.transpose(0, 2, 1),
        cotangent.transpose(0, 2, 3, 1).reshape(16, 32, 64),
    )
    block, early, deep = pl.pallas_call(
        results,
        out_shape=(
            jax.ShapeDtypeStruct((16, 32, 64), BF),
            jax.ShapeDtypeStruct((27, 128, 128), F32),
            jax.ShapeDtypeStruct((27, 32, 128), F32),
        ),
        in_specs=[any_] * 3,
        out_specs=(any_,) * 3,
        scratch_shapes=[
            pltpu.VMEM((16, 32, 64), BF),
            pltpu.VMEM((7, 2, 8, 8, 512), BF),
            pltpu.VMEM((27, 32, 128), F32),
            pltpu.VMEM((27, 128, 128), F32),
            pltpu.SemaphoreType.DMA((2, 9)),
        ],
        compiler_params=pltpu.CompilerParams(vmem_limit_bytes=60 << 20),
        name="results",
    )(block, early, deep)
    block = block.reshape(2, 8, 32, 64).transpose(0, 3, 1, 2)
    return block, early, deep.transpose(0, 2, 1)


def solution(mesh):
    return jax.shard_map(
        shards,
        mesh=mesh,
        in_specs=(
            P("space", "filt", None, None),
            P(),
            P(None, None, "filt"),
            P("space", None, None, "filt"),
        ),
        out_specs=(P("space", None, None, "filt"), P(), P(None, None, "filt")),
        check_vma=False,
    )
```

```python
import functools
import math

import jax
import jax.numpy as jnp
from jax import lax
from jax.experimental import pallas as pl
from jax.experimental.pallas import tpu as pltpu
from jax.sharding import PartitionSpec as P

MESH = pl.DeviceIdType.MESH
BF = jnp.bfloat16
F32 = jnp.float32
SPACE, FILT, CHIPS = 16, 8, 64
DIRS = [(ds, df) for ds in (-1, 0, 1) for df in (-1, 0, 1) if ds or df]
GROUP = 4
DIRECT = 15
SHARE = 3
OWNERS = 7


def rcopy(src, dst, send_sem, recv_sem, device):
    return pltpu.make_async_remote_copy(
        src_ref=src,
        dst_ref=dst,
        send_sem=send_sem,
        recv_sem=recv_sem,
        device_id=device,
        device_id_type=MESH,
    )


def sigmoid(v):
    return 1.0 / (1.0 + jnp.exp(-v))


def shift_rows(v, step):
    size = v.shape[1]
    row = lax.broadcasted_iota(jnp.int32, v.shape, 1)
    edge = size - 1 if step == 1 else 0
    rolled = pltpu.roll(v, (-step) % size, 1)
    return jnp.where(row == edge, 0.0, rolled)


def dot(a, b):
    return lax.dot_general(a, b, (((1,), (0,)), ((), ())), preferred_element_type=F32)


def dot_t(a, b):
    return lax.dot_general(a, b, (((1,), (1,)), ((), ())), preferred_element_type=F32)


def edges(step, size, width):
    if step == 1:
        return size - width, 0, width
    if step == -1:
        return 0, size + width, width
    return 0, width, size


def swap_cells(ref, v):
    halves = []
    for h in range(2):
        ref[h] = v[:, 128 * h : 128 * h + 128]
        rows = [ref[h, pl.ds(64 * x + n, 8, stride=8), :] for x in range(2) for n in range(8)]
        halves.append(jnp.concatenate(rows, axis=0))
    return jnp.concatenate(halves, axis=1)


class Halo:
    def __init__(self, source, base, padded, nx, ny, width, sems, s, f):
        self.items = []
        for k, (ds, df) in enumerate(DIRS):
            sx, dx, lx = edges(ds, nx, width)
            sy, dy, ly = edges(df, ny, width)
            src = source.at[base + sx : base + sx + lx, base + sy : base + sy + ly]
            dst = padded.at[dx : dx + lx, dy : dy + ly]
            to_s, to_f, from_s, from_f = s + ds, f + df, s - ds, f - df
            send = (to_s >= 0) & (to_s < SPACE) & (to_f >= 0) & (to_f < FILT)
            recv = (from_s >= 0) & (from_s < SPACE) & (from_f >= 0) & (from_f < FILT)
            copy = rcopy(src, dst, sems.at[0, k], sems.at[1, k], (to_s, to_f))
            self.items.append((copy, send, recv))

    def start(self):
        for copy, send, _ in self.items:
            pl.when(send)(copy.start)

    def wait_recv(self):
        for copy, _, recv in self.items:
            pl.when(recv)(copy.wait_recv)

    def wait_send(self):
        for copy, send, _ in self.items:
            pl.when(send)(copy.wait_send)


def zero_rim(padded, nx, ny, width, s, f):
    shape = padded.shape
    w = width

    @pl.when(s == 0)
    def _():
        padded[0:w] = jnp.zeros((w,) + shape[1:], padded.dtype)

    @pl.when(s == SPACE - 1)
    def _():
        padded[nx + w : nx + 2 * w] = jnp.zeros((w,) + shape[1:], padded.dtype)

    @pl.when(f == 0)
    def _():
        padded[:, 0:w] = jnp.zeros((shape[0], w) + shape[2:], padded.dtype)

    @pl.when(f == FILT - 1)
    def _():
        padded[:, ny + w : ny + 2 * w] = jnp.zeros((shape[0], w) + shape[2:], padded.dtype)


SCRATCH = dict(
    vp=((6, 18, 16, 128), BF),
    zc=((6, 18, 16, 384), BF),
    we=((9, 384, 128), BF),
    ct=((16, 32, 64), BF),
    wg=((27, 256, 128), BF),
    cs=((8, 2, 2, 16, 128), BF),
    cr=((4, 2, 8, 16, 128), BF),
    acc=((1024, 128), F32),
    sg=((4, 16, 16, 128), F32),
    tmp=((16, 16, 128), F32),
    cells=((2, 128, 128), F32),
    act=((128, 256), F32),
    pp=((6, 12, 8, 128), BF),
    pz=((6, 12, 8, 384), F32),
    ps=((2, 66, 8, 128), BF),
    ps3=((2, 66, 8, 384), F32),
    bs=((2, 8, 16, 128), BF),
    br=((8, 2, 16, 128), BF),
    gf=((4, 10, 8, 256), F32),
    gs=((2, 3, 8, 16, 128), BF),
    gr=((2, 3, 16, 1024), BF),
    gt=((128, 1024), BF),
    xs=((7, 64, 512), BF),
    xr=((7, 64, 512), BF),
    xo=((7, 64, 512), F32),
    es=((7, 8, 8, 512), BF),
    er=((64, 8, 512), BF),
    ea=((2, 7, 8, 8, 512), BF),
    bo=((16, 32, 64), BF),
    gd=((27, 32, 128), F32),
    pb=((1024, 1152), BF),
    hs=((48, 1152), BF),
    hr=((48, 1152), BF),
    ho=((48, 1152), F32),
    dsd=((28, 16, 128), BF),
    dr=((8, 4, 16, 128), BF),
    da=((2, 28, 16, 128), BF),
)
SEMS = dict(
    local=(4,),
    halo_v=(2, 8),
    halo_p=(2, 8),
    s_cot=(2, 3),
    s_wa=(2, 8),
    s_wb=(2, 8),
    s_wy=(2, 4),
    s_wrel=(2, 5),
    s_ps=(2, 8),
    s_bo=(2, 8),
    s_g=(2, 8),
    s_x=(2, 7),
    s_rs=(7,),
    r_rs=(1,),
    s_ag=(1,),
    r_ag=(8,),
    s_ear=(2, 8),
    s_out=(2,),
    s_ea=(2, 8),
    s_h=(2,),
    s_drs=(2, 8),
    s_dag=(2, 8),
    s_dar=(2,),
)


def kernel(early_scale, deep_scale, vol, we_in, wd_in, ct_in, bo_out, ea_out, gd_out, *scratch):
    r = dict(zip(list(SCRATCH) + list(SEMS), scratch))
    ready = scratch[-1]
    s = lax.axis_index("space")
    f = lax.axis_index("filt")
    core = lax.rem(s, 2)
    other = 1 - core
    sib = s + 1 - 2 * core
    j = lax.div(s, 2)

    def filt_peer(k):
        return lax.rem(f + k, FILT)

    def filt_from(k):
        return lax.rem(f + FILT - k, FILT)

    chips_s = [lax.rem(s + 2 * dj, SPACE) for dj in range(8)]
    chips_f = [lax.rem(f + df, FILT) for df in range(8)]
    owner = j < OWNERS

    barrier = pltpu.get_barrier_semaphore()

    def space_chip(k):
        return lax.rem(s + 2 * k, SPACE)

    x_hi, z = lax.div(f, 4), lax.rem(f, 4)
    near = s + 2 - 4 * lax.rem(j, 2)
    w_to = [(s, 4 * x_hi + lax.rem(z + k, 4)) for k in range(1, 4)]
    w_to += [(near, 4 * (1 - x_hi) + lax.rem(z + k, 4)) for k in range(4)]

    greeted = [(s, filt_peer(k)) for k in range(1, FILT)]
    greeted += [(space_chip(k), f) for k in range(1, 8)]
    greeted += [
        (lax.rem(s + d, SPACE), lax.rem(f + df, FILT))
        for d in (1, SPACE - 1)
        for df in range(FILT)
    ]
    greeted += w_to[3:]
    for device in greeted:
        pl.semaphore_signal(barrier, inc=1, device_id=device, device_id_type=MESH)

    own_vol = pltpu.make_async_copy(vol, r["vp"].at[1:5, 1:17], r["local"].at[0])
    own_vol.start()
    wg = r["wg"]
    w_rows = pl.ds(pl.multiple_of(128 * core + 16 * f, 16), 16)
    w_half = pl.ds(pl.multiple_of(16 * core, 16), 16)
    y = lax.div(s, 4)

    def share(yy):
        return pl.ds(DIRECT + SHARE * yy, SHARE)

    own_wd = [
        pltpu.make_async_copy(wd_in.at[taps, w_half], wg.at[taps, w_rows], r["local"].at[n])
        for n, taps in ((1, pl.ds(0, DIRECT)), (3, share(y)))
    ]
    for c in own_wd:
        c.start()
    own_ct = pltpu.make_async_copy(ct_in, r["ct"], r["local"].at[2])
    own_ct.start()
    own_ct.wait()
    lane = lax.broadcasted_iota(jnp.int32, (32, 128), 1)
    for x in range(2):
        parts = [jnp.zeros((32, 128), F32)] * FILT
        for z in range(8):
            v = r["ct"][8 * x + z].astype(F32)
            v = jnp.concatenate([v, jnp.zeros_like(v)], axis=1)
            here = (lane >= 16 * z) & (lane < 16 * z + 10)
            for q in range(FILT):
                moved = pltpu.roll(v, (16 * z - 8 * q + 1) % 128, 1)
                parts[q] = jnp.where(here, moved, parts[q])
        for q in range(FILT):
            r["cs"][q, x] = parts[q].astype(BF).reshape(2, 16, 128)

    @pl.when(s == 0)
    def _():
        r["cr"][0] = jnp.zeros((2, 8, 16, 128), BF)

    @pl.when(s == SPACE - 1)
    def _():
        r["cr"][3] = jnp.zeros((2, 8, 16, 128), BF)

    zero_rim(r["vp"], 4, 16, 1, s, f)
    zero_rim(r["pp"], 2, 8, 2, s, f)
    r["ps"][:, 0:1] = jnp.zeros((2, 1, 8, 128), BF)
    r["ps"][:, 65:66] = jnp.zeros((2, 1, 8, 128), BF)

    pl.semaphore_wait(barrier, len(greeted))
    halo_v = Halo(vol, 0, r["vp"], 4, 16, 1, r["halo_v"], s, f)
    halo_v.start()
    own_we = pltpu.make_async_copy(we_in, r["we"], r["local"].at[2])
    own_we.start()

    def w_send(taps, sems, k):
        return rcopy(
            wd_in.at[taps, w_half],
            wg.at[taps, w_rows],
            r[sems].at[0, k],
            r[sems].at[1, k],
            w_to[k - 1],
        )

    for k in range(1, 8):
        pl.semaphore_signal(ready, inc=1, device_id=(space_chip(k), f), device_id_type=MESH)

    wb = []
    for k in range(1, FILT):
        wb.append(w_send(share(y), "s_wb", k))
        wb[-1].start()

    wa = []
    for k in range(1, FILT):
        wa.append(w_send(pl.ds(0, DIRECT), "s_wa", k))
        wa[-1].start()

    def cot_copy(src, row, n, device):
        return rcopy(
            src, r["cr"].at[row, :, f], r["s_cot"].at[0, n], r["s_cot"].at[1, n], device
        )

    def cot_all(n):
        whole = r["cs"].at[0:7] if n == 0 else r["cr"].at[0]
        return rcopy(whole, whole, r["s_cot"].at[0, n], r["s_cot"].at[1, n], (s, f))

    for k in range(1, FILT):
        cot_copy(r["cs"].at[filt_peer(k)], slice(1, 3), 0, (s, filt_peer(k))).start()

    @pl.when(s > 0)
    def _():
        for q in range(FILT):
            cot_copy(r["cs"].at[q, 0], 3, 1, (s - 1, q)).start()

    @pl.when(s < SPACE - 1)
    def _():
        for q in range(FILT):
            cot_copy(r["cs"].at[q, 1], 0, 2, (s + 1, q)).start()

    r["cr"][1:3, :, pl.ds(f, 1)] = r["cs"][pl.ds(f, 1)].reshape(2, 2, 1, 16, 128)

    for c in own_wd:
        c.wait()
    for c in wb:
        c.wait_recv()
    w_core = pl.ds(pl.multiple_of(128 * core, 128), 128)

    def w_pass(taps, sems, k, device):
        piece = wg.at[taps, w_core]
        return rcopy(piece, piece, r[sems].at[0, k], r[sems].at[1, k], device)

    wy = []
    for k in range(1, 4):
        wy.append(w_pass(share(y), "s_wy", k, (lax.rem(s + 4 * k, SPACE), f)))
        wy[-1].start()
    relay = [w_pass(share(y), "s_wrel", 0, (sib, f))]
    relay[-1].start()
    own_vol.wait()
    halo_v.wait_recv()
    zc = r["zc"]
    for row in range(6):
        x = r["vp"][row].astype(F32)
        zc[row, :, :, 0:128] = shift_rows(x, -1).astype(BF)
        zc[row, :, :, 128:256] = r["vp"][row]
        zc[row, :, :, 256:384] = shift_rows(x, 1).astype(BF)
    own_we.wait()
    acc = r["acc"]
    for ab in range(9):
        a, b = ab // 3, ab % 3
        patch = zc[a : a + 4, b : b + 16].reshape(1024, 384)
        term = dot(patch, r["we"][ab])
        if ab == 0:
            acc[...] = term
        else:
            acc[...] += term
    for half in range(2):
        v = acc[512 * half : 512 * half + 512].reshape(2, 16, 16, 128)
        sig = sigmoid(v)
        r["sg"][2 * half : 2 * half + 2] = sig * (1.0 + v * (1.0 - sig)) * 0.125
        act = v * sig
        act = (act[0] + act[1]).reshape(8, 2, 16, 128)
        r["tmp"][8 * half : 8 * half + 8] = act[:, 0] + act[:, 1]
    tmp = r["tmp"]
    pooled = (tmp[:, pl.ds(0, 8, stride=2), :] + tmp[:, pl.ds(1, 8, stride=2), :]) * 0.125
    pooled = pooled.reshape(2, 8, 8, 128).astype(BF)
    r["pp"][2:4, 2:10] = pooled
    halo_p = Halo(r["pp"], 2, r["pp"], 2, 8, 2, r["halo_p"], s, f)
    halo_p.start()
    r["ps"][:, pl.ds(1 + 8 * f, 8)] = pooled

    for c in wa:
        c.wait_recv()
    relay.append(w_pass(pl.ds(0, DIRECT), "s_wrel", 4, (sib, f)))
    relay[-1].start()
    for k in range(1, 4):
        wy[k - 1].wait_recv()
        relay.append(w_pass(share(lax.rem(y + 4 - k, 4)), "s_wrel", k, (sib, f)))
        relay[-1].start()
    cot_all(0).wait_recv()
    pl.when(s > 0)(cot_all(2).wait_recv)
    pl.when(s < SPACE - 1)(cot_all(1).wait_recv)
    cells = r["cells"]
    cot = []
    for row in range(4):
        v = r["cr"][row].reshape(256, 128).astype(F32).T
        halves = []
        for h in range(2):
            cells[h] = v[:, 128 * h : 128 * h + 128]
            cols = [cells[h, pl.ds(col, 8, stride=16), :] for col in range(10)]
            halves.append(jnp.concatenate(cols, axis=0))
        cot.append(jnp.concatenate(halves, axis=1))
    cot = jnp.concatenate(cot, axis=0)
    halo_p.wait_recv()
    pz = r["pz"]
    for row in range(6):
        x = r["pp"][row].astype(F32)
        pz[row, :, :, 0:128] = shift_rows(x, -1)
        pz[row, :, :, 128:256] = x
        pz[row, :, :, 256:384] = shift_rows(x, 1)
    for c in relay:
        c.wait_recv()

    pss = []
    for k in range(1, FILT):
        pss.append(
            rcopy(
                r["pp"].at[2:4, 2:10],
                r["ps"].at[:, pl.ds(1 + 8 * f, 8)],
                r["s_ps"].at[0, k],
                r["s_ps"].at[1, k],
                (s, filt_peer(k)),
            )
        )
        pss[-1].start()

    pre = jnp.zeros((320, 256), F32)
    for ab in range(9):
        a, b = ab // 3, ab % 3
        patch = pz[a : a + 4, b : b + 10].reshape(320, 384).astype(BF)
        taps = jnp.concatenate([wg[3 * ab + c] for c in range(3)], axis=1)
        pre = pre + dot_t(patch, taps)
    sig = sigmoid(pre)
    g = (cot * (sig * (1.0 + pre * (1.0 - sig)))).astype(BF)
    gf = r["gf"]
    gf[...] = g.astype(F32).reshape(4, 10, 8, 256)
    r["act"][...] = (pre * sig).reshape(4, 10, 8, 256)[1:3, 1:9].reshape(128, 256)
    back = jnp.zeros((128, 384), F32)
    for ab in range(9):
        a, b = ab // 3, ab % 3
        patch = gf[2 - a : 4 - a, 2 - b : 10 - b].reshape(128, 256).astype(BF)
        taps = jnp.concatenate([wg[3 * ab + c] for c in range(3)], axis=1)
        back = back + dot(patch, taps)
    back = back.reshape(16, 8, 384)
    gpool = (
        shift_rows(back[:, :, 0:128], 1)
        + back[:, :, 128:256]
        + shift_rows(back[:, :, 256:384], -1)
    )
    gpool = gpool.astype(BF).astype(F32)
    tmp[:, pl.ds(0, 8, stride=2), :] = gpool
    tmp[:, pl.ds(1, 8, stride=2), :] = gpool
    for row in range(4):
        spread = tmp[8 * (row // 2) : 8 * (row // 2) + 8]
        spread = jnp.broadcast_to(spread[:, None], (8, 2, 16, 128)).reshape(16, 16, 128)
        grad = (spread * r["sg"][row]).astype(BF).astype(F32).reshape(256, 128)
        r["gt"][:, 256 * row : 256 * row + 256] = grad.T.astype(BF)

    gt = r["gt"][...]
    es, er, ea = r["es"], r["er"], r["ea"]
    pl.semaphore_wait(ready, 7)

    def group_of(k):
        return lax.rem(j + k, OWNERS)

    def x_copy(k):
        return rcopy(
            r["xs"].at[k], r["xr"].at[k], r["s_x"].at[0, k], r["s_x"].at[1, k], (sib, f)
        )

    gcs = []
    lanes_f = pl.ds(pl.multiple_of(128 * f, 128), 128)

    def send_gradients():
        for a in range(3):
            piece = gf[2 - a : 4 - a, 1:9].reshape(128, 256)
            r["gs"][:, a] = piece.T.astype(BF).reshape(2, 8, 16, 128)
        for k in range(1, FILT):
            gcs.append(
                rcopy(
                    r["gs"].at[:, :, filt_peer(k)],
                    r["gr"].at[:, :, :, lanes_f],
                    r["s_g"].at[0, k],
                    r["s_g"].at[1, k],
                    (s, filt_peer(k)),
                )
            )
            gcs[-1].start()
        r["gr"][:, :, :, lanes_f] = r["gs"][:, :, pl.ds(f, 1)].reshape(2, 3, 16, 128)

    for k in range(OWNERS + 1):
        if k < OWNERS:
            patches = []
            for n in range(GROUP):
                t = jnp.minimum(GROUP * group_of(k) + n, 26)
                a, b, c = lax.div(t, 9), lax.rem(lax.div(t, 3), 3), lax.rem(t, 3)
                lanes = pl.ds(pl.multiple_of(128 * c, 128), 128)
                patch = zc[pl.ds(a, 4), pl.ds(b, 16), :, lanes]
                patches.append(patch.reshape(1024, 128))
            term = dot(gt, jnp.concatenate(patches, axis=1))

            @pl.when(core == 0)
            def _():
                r["xo"][k] = term[0:64]
                r["xs"][k] = term[64:128].astype(BF)

            @pl.when(core == 1)
            def _():
                r["xo"][k] = term[64:128]
                r["xs"][k] = term[0:64].astype(BF)

            x_copy(k).start()
        if k == 1:
            send_gradients()
        if k >= 1:
            p = k - 1
            x_copy(p).wait_recv()
            total = r["xo"][p] + r["xr"][p].astype(F32)
            es[p] = total.reshape(8, 8, 512).astype(BF)
            to_j = group_of(p)
            dj = lax.rem(to_j - j + 8, 8)
            for df in range(8):
                copy = rcopy(
                    es.at[p, chips_f[df]],
                    er.at[8 * dj + df],
                    r["s_rs"].at[p],
                    r["r_rs"].at[0],
                    (2 * to_j + core, chips_f[df]),
                )
                if p == 0 and df == 0:
                    pl.when(j >= OWNERS)(copy.start)
                else:
                    copy.start()

    for c in pss:
        c.wait_recv()
    ps3 = r["ps3"]
    for row in range(2):
        x = r["ps"][row].astype(F32)
        ps3[row, :, :, 0:128] = shift_rows(x, -1)
        ps3[row, :, :, 128:256] = x
        ps3[row, :, :, 256:384] = shift_rows(x, 1)
    for q in range(8):
        for b in range(3):
            patch = ps3[:, 8 * q + b : 8 * q + b + 8].reshape(128, 384).astype(BF)
            r["pb"][128 * q : 128 * q + 128, 384 * b : 384 * b + 384] = patch
    for c in gcs:
        c.wait_recv()
    deep = dot(r["gr"][...].reshape(96, 1024), r["pb"][...])

    @pl.when(core == 0)
    def _():
        r["ho"][...] = deep[0:48]
        r["hs"][...] = deep[48:96].astype(BF)

    @pl.when(core == 1)
    def _():
        r["ho"][...] = deep[48:96]
        r["hs"][...] = deep[0:48].astype(BF)

    hcopy = rcopy(r["hs"], r["hr"], r["s_h"].at[0], r["s_h"].at[1], (sib, f))
    hcopy.start()


    act = swap_cells(r["cells"], r["act"][...])
    r["bs"][...] = act.T.astype(BF).reshape(2, 8, 16, 128)
    bos = []
    for k in range(1, FILT):
        bos.append(
            rcopy(
                r["bs"].at[:, filt_peer(k)],
                r["br"].at[f],
                r["s_bo"].at[0, k],
                r["s_bo"].at[1, k],
                (s, filt_peer(k)),
            )
        )
        bos[-1].start()
    r["br"][pl.ds(f, 1)] = r["bs"][:, pl.ds(f, 1)].reshape(1, 2, 16, 128)

    ag_sends = []
    for k in range(1, CHIPS):
        piece = ea.at[core, jnp.minimum(j, OWNERS - 1), f]
        device = (chips_s[k // 8], chips_f[k % 8])
        ag_sends.append(rcopy(piece, piece, r["s_ag"].at[0], r["r_ag"].at[k // 8], device))

    @pl.when(owner)
    def _():
        er[0] = es[0, pl.ds(f, 1)].reshape(8, 512)
        landed = er.at[1:CHIPS]
        rcopy(landed, landed, r["s_rs"].at[0], r["r_rs"].at[0], (s, f)).wait_recv()
        total = jnp.sum(er[0:8].astype(F32), axis=0)
        for n in range(1, 8):
            total = total + jnp.sum(er[8 * n : 8 * n + 8].astype(F32), axis=0)
        total = (total * early_scale).astype(BF).reshape(1, 1, 1, 8, 512)
        ea[pl.ds(core, 1), pl.ds(j, 1), pl.ds(f, 1)] = total
        for c in ag_sends:
            c.start()

    hcopy.wait_recv()
    dsd = r["dsd"]
    dsd[27:28] = jnp.zeros((1, 16, 128), BF)
    total = r["ho"][...] + r["hr"][...].astype(F32)
    for a in range(3):
        for bc in range(9):
            dsd[9 * a + bc] = total[16 * a : 16 * a + 16, 128 * bc : 128 * bc + 128].astype(BF)

    def first_of(jj):
        return jnp.minimum(GROUP * jj, GROUP * (OWNERS - 1))

    drs = []
    for k in range(1, 8):
        to_s = space_chip(k)
        to_j = lax.div(to_s, 2)
        copy = rcopy(
            dsd.at[pl.ds(first_of(to_j), GROUP)],
            r["dr"].at[k],
            r["s_drs"].at[0, k],
            r["s_drs"].at[1, k],
            (to_s, f),
        )
        pl.when(to_j < OWNERS)(copy.start)
        drs.append((copy, to_j < OWNERS))

    mine_t = pl.ds(first_of(j), GROUP)

    for c in bos:
        c.wait_recv()
    parts = [jnp.zeros((32, 128), F32)] * 16
    for q in range(FILT):
        x = r["br"][q].reshape(32, 128).astype(F32)
        for p in range(16):
            moved = pltpu.roll(x, (8 * q - 8 * p) % 128, 1)
            parts[p] = jnp.where(lane // 8 == q, moved, parts[p])
    for p in range(16):
        r["bo"][p] = parts[p][:, 0:64].astype(BF)
    bo_copy = pltpu.make_async_copy(r["bo"], bo_out, r["s_out"].at[0])
    bo_copy.start()

    da = r["da"]
    piece = da.at[core, mine_t]
    dag = []
    for k in range(1, 8):
        dag.append(
            rcopy(piece, piece, r["s_dag"].at[0, k], r["s_dag"].at[1, k], (space_chip(k), f))
        )

    @pl.when(owner)
    def _():
        total = dsd[mine_t].astype(F32)
        for k in range(1, 8):
            drs[k - 1][0].wait_recv()
            total = total + r["dr"][k].astype(F32)
        da[pl.ds(core, 1), mine_t] = (total * deep_scale).astype(BF).reshape(1, GROUP, 16, 128)
        for c in dag:
            c.start()

    def ear_copy(dj):
        piece = ea.at[core, lax.rem(j - dj + 8, 8)]
        return rcopy(piece, piece, r["s_ear"].at[0, dj], r["s_ear"].at[1, dj], (sib, f))

    def ea_copy(half, dj):
        g = lax.rem(j - dj + 8, 8)
        return pltpu.make_async_copy(ea.at[half, g], ea_out.at[half, g], r["s_ea"].at[half, dj])

    for dj in range(8):

        @pl.when(lax.rem(j - dj + 8, 8) < OWNERS)
        def _():
            landed = ea.at[core, lax.rem(j - dj + 8, 8), 0 : (8 if dj else 7)]
            rcopy(landed, landed, r["s_ag"].at[0], r["r_ag"].at[dj], (s, f)).wait_recv()
            ear_copy(dj).start()
            ea_copy(core, dj).start()

    for k in range(1, 8):
        from_j = lax.div(lax.rem(s + SPACE - 2 * k, SPACE), 2)
        pl.when(from_j < OWNERS)(dag[k - 1].wait_recv)
    dar = rcopy(da.at[core], da.at[core], r["s_dar"].at[0], r["s_dar"].at[1], (sib, f))
    dar.start()

    dar.wait_recv()
    for t in range(27):
        r["gd"][t] = da[:, t].reshape(32, 128).astype(F32)
    gd_copy = pltpu.make_async_copy(r["gd"], gd_out, r["s_out"].at[1])
    gd_copy.start()

    for dj in range(8):

        @pl.when(lax.rem(j - dj + 8, 8) < OWNERS)
        def _():
            ear_copy(dj).wait_recv()
            ea_copy(other, dj).start()

    for h in (halo_v, halo_p):
        h.wait_send()
    cot_all(0).wait_send()
    pl.when(s > 0)(cot_all(1).wait_send)
    pl.when(s < SPACE - 1)(cot_all(2).wait_send)
    for c in wa + wb + wy + relay + pss + bos + gcs + [hcopy, dar]:
        c.wait_send()
    for copy, active in drs:
        pl.when(active)(copy.wait_send)

    for k in range(OWNERS):
        x_copy(k).wait_send()

    def rs_sent(k, count):
        left = es.at[k, 0:count]
        rcopy(left, left, r["s_rs"].at[k], r["r_rs"].at[0], (s, f)).wait_send()

    for k in range(1, OWNERS):
        rs_sent(k, 8)

    @pl.when(owner)
    def _():
        rs_sent(0, 7)
        left = er.at[1:CHIPS]
        rcopy(left, left, r["s_ag"].at[0], r["r_rs"].at[0], (s, f)).wait_send()
        for c in dag:
            c.wait_send()

    pl.when(j >= OWNERS)(functools.partial(rs_sent, 0, 8))
    for dj in range(8):

        @pl.when(lax.rem(j - dj + 8, 8) < OWNERS)
        def _():
            ear_copy(dj).wait_send()
            ea_copy(core, dj).wait()
            ea_copy(other, dj).wait()

    bo_copy.wait()
    gd_copy.wait()


def results(bo_in, ea_in, gd_in, bo_out, ge_out, gd_out, bo, ea, gd, ge, sems):
    ins = [pltpu.make_async_copy(ea_in.at[:, g], ea.at[g], sems.at[0, g]) for g in range(OWNERS)]
    ins.append(pltpu.make_async_copy(bo_in, bo, sems.at[0, 7]))
    ins.append(pltpu.make_async_copy(gd_in, gd, sems.at[0, 8]))
    outs = []
    for g in range(OWNERS):
        taps = min(GROUP, 27 - GROUP * g)
        src, dst = ge.at[pl.ds(GROUP * g, taps)], ge_out.at[pl.ds(GROUP * g, taps)]
        outs.append(pltpu.make_async_copy(src, dst, sems.at[1, g]))
    outs.append(pltpu.make_async_copy(bo, bo_out, sems.at[1, 7]))
    outs.append(pltpu.make_async_copy(gd, gd_out, sems.at[1, 8]))
    for c in ins:
        c.start()
    for g in range(OWNERS):
        ins[g].wait()
        block = ea[g].reshape(128, 512).astype(F32)
        for t in range(GROUP * g, min(GROUP * g + GROUP, 27)):
            n = t - GROUP * g
            ge[t] = block[:, 128 * n : 128 * n + 128].T
        outs[g].start()
    for n in (7, 8):
        ins[n].wait()
        outs[n].start()
    for c in outs:
        c.wait()


def shards(volume, w_early, w_deep, cotangent):
    any_ = pl.BlockSpec(memory_space=pl.ANY)
    cells = volume.shape[0] * volume.shape[1] * volume.shape[2] * SPACE * FILT
    body = functools.partial(kernel, 1.0 / math.sqrt(cells), 1.0 / math.sqrt(cells // 8))
    block, early, deep = pl.pallas_call(
        body,
        out_shape=(
            jax.ShapeDtypeStruct((16, 32, 64), BF),
            jax.ShapeDtypeStruct((2, 7, 8, 8, 512), BF),
            jax.ShapeDtypeStruct((27, 32, 128), F32),
        ),
        in_specs=[any_] * 4,
        out_specs=(any_,) * 3,
        scratch_shapes=[pltpu.VMEM(*v) for v in SCRATCH.values()]
        + [pltpu.SemaphoreType.DMA(v) for v in SEMS.values()]
        + [pltpu.SemaphoreType.REGULAR],
        compiler_params=pltpu.CompilerParams(
            collective_id=0, has_side_effects=True, vmem_limit_bytes=56 << 20
        ),
        name="step",
    )(
        volume,
        w_early.reshape(9, 384, 128),
        w_deep.transpose(0, 2, 1),
        cotangent.transpose(0, 2, 3, 1).reshape(16, 32, 64),
    )
    block, early, deep = pl.pallas_call(
        results,
        out_shape=(
            jax.ShapeDtypeStruct((16, 32, 64), BF),
            jax.ShapeDtypeStruct((27, 128, 128), F32),
            jax.ShapeDtypeStruct((27, 32, 128), F32),
        ),
        in_specs=[any_] * 3,
        out_specs=(any_,) * 3,
        scratch_shapes=[
            pltpu.VMEM((16, 32, 64), BF),
            pltpu.VMEM((7, 2, 8, 8, 512), BF),
            pltpu.VMEM((27, 32, 128), F32),
            pltpu.VMEM((27, 128, 128), F32),
            pltpu.SemaphoreType.DMA((2, 9)),
        ],
        compiler_params=pltpu.CompilerParams(vmem_limit_bytes=60 << 20),
        name="results",
    )(block, early, deep)
    block = block.reshape(2, 8, 32, 64).transpose(0, 3, 1, 2)
    return block, early, deep.transpose(0, 2, 1)


def solution(mesh):
    return jax.shard_map(
        shards,
        mesh=mesh,
        in_specs=(
            P("space", "filt", None, None),
            P(),
            P(None, None, "filt"),
            P("space", None, None, "filt"),
        ),
        out_specs=(P("space", None, None, "filt"), P(), P(None, None, "filt")),
        check_vma=False,
    )
```

```python
import functools
import math

import jax
import jax.numpy as jnp
from jax import lax
from jax.experimental import pallas as pl
from jax.experimental.pallas import tpu as pltpu
from jax.sharding import PartitionSpec as P

MESH = pl.DeviceIdType.MESH
BF = jnp.bfloat16
F32 = jnp.float32
SPACE, FILT, CHIPS = 16, 8, 64
DIRS = [(ds, df) for ds in (-1, 0, 1) for df in (-1, 0, 1) if ds or df]
GROUP = 4
DIRECT = 15
SHARE = 3
OWNERS = 7


def rcopy(src, dst, send_sem, recv_sem, device):
    return pltpu.make_async_remote_copy(
        src_ref=src,
        dst_ref=dst,
        send_sem=send_sem,
        recv_sem=recv_sem,
        device_id=device,
        device_id_type=MESH,
    )


def sigmoid(v):
    return 1.0 / (1.0 + jnp.exp(-v))


def shift_rows(v, step):
    size = v.shape[1]
    row = lax.broadcasted_iota(jnp.int32, v.shape, 1)
    edge = size - 1 if step == 1 else 0
    rolled = pltpu.roll(v, (-step) % size, 1)
    return jnp.where(row == edge, 0.0, rolled)


def dot(a, b):
    return lax.dot_general(a, b, (((1,), (0,)), ((), ())), preferred_element_type=F32)


def dot_t(a, b):
    return lax.dot_general(a, b, (((1,), (1,)), ((), ())), preferred_element_type=F32)


def edges(step, size, width):
    if step == 1:
        return size - width, 0, width
    if step == -1:
        return 0, size + width, width
    return 0, width, size


def swap_cells(ref, v):
    halves = []
    for h in range(2):
        ref[h] = v[:, 128 * h : 128 * h + 128]
        rows = [ref[h, pl.ds(64 * x + n, 8, stride=8), :] for x in range(2) for n in range(8)]
        halves.append(jnp.concatenate(rows, axis=0))
    return jnp.concatenate(halves, axis=1)


class Halo:
    def __init__(self, source, base, padded, nx, ny, width, sems, s, f):
        self.items = []
        for k, (ds, df) in enumerate(DIRS):
            sx, dx, lx = edges(ds, nx, width)
            sy, dy, ly = edges(df, ny, width)
            src = source.at[base + sx : base + sx + lx, base + sy : base + sy + ly]
            dst = padded.at[dx : dx + lx, dy : dy + ly]
            to_s, to_f, from_s, from_f = s + ds, f + df, s - ds, f - df
            send = (to_s >= 0) & (to_s < SPACE) & (to_f >= 0) & (to_f < FILT)
            recv = (from_s >= 0) & (from_s < SPACE) & (from_f >= 0) & (from_f < FILT)
            copy = rcopy(src, dst, sems.at[0, k], sems.at[1, k], (to_s, to_f))
            self.items.append((copy, send, recv))

    def start(self):
        for copy, send, _ in self.items:
            pl.when(send)(copy.start)

    def wait_recv(self):
        for copy, _, recv in self.items:
            pl.when(recv)(copy.wait_recv)

    def wait_send(self):
        for copy, send, _ in self.items:
            pl.when(send)(copy.wait_send)


def zero_rim(padded, nx, ny, width, s, f):
    shape = padded.shape
    w = width

    @pl.when(s == 0)
    def _():
        padded[0:w] = jnp.zeros((w,) + shape[1:], padded.dtype)

    @pl.when(s == SPACE - 1)
    def _():
        padded[nx + w : nx + 2 * w] = jnp.zeros((w,) + shape[1:], padded.dtype)

    @pl.when(f == 0)
    def _():
        padded[:, 0:w] = jnp.zeros((shape[0], w) + shape[2:], padded.dtype)

    @pl.when(f == FILT - 1)
    def _():
        padded[:, ny + w : ny + 2 * w] = jnp.zeros((shape[0], w) + shape[2:], padded.dtype)


SCRATCH = dict(
    vp=((6, 18, 16, 128), BF),
    zc=((6, 18, 16, 384), BF),
    we=((9, 384, 128), BF),
    ct=((16, 32, 64), BF),
    wg=((27, 256, 128), BF),
    cs=((8, 2, 2, 16, 128), BF),
    cr=((4, 2, 8, 16, 128), BF),
    acc=((1024, 128), F32),
    sg=((4, 16, 16, 128), F32),
    tmp=((16, 16, 128), F32),
    cells=((2, 128, 128), F32),
    act=((128, 256), F32),
    pp=((6, 12, 8, 128), BF),
    pz=((6, 12, 8, 384), F32),
    ps=((2, 66, 8, 128), BF),
    ps3=((2, 66, 8, 384), F32),
    bs=((2, 8, 16, 128), BF),
    br=((8, 2, 16, 128), BF),
    gf=((4, 10, 8, 256), F32),
    gs=((2, 3, 8, 16, 128), BF),
    gr=((2, 3, 16, 1024), BF),
    gt=((128, 1024), BF),
    xs=((7, 64, 512), BF),
    xr=((7, 64, 512), BF),
    xo=((7, 64, 512), F32),
    es=((7, 8, 8, 512), BF),
    er=((64, 8, 512), BF),
    ea=((2, 7, 8, 8, 512), BF),
    bo=((16, 32, 64), BF),
    gd=((27, 32, 128), F32),
    pb=((1024, 1152), BF),
    hs=((48, 1152), BF),
    hr=((48, 1152), BF),
    ho=((48, 1152), F32),
    dsd=((28, 16, 128), BF),
    dr=((8, 4, 16, 128), BF),
    da=((2, 28, 16, 128), BF),
)
SEMS = dict(
    local=(4,),
    halo_v=(2, 8),
    halo_p=(2, 8),
    s_cot=(2, 3),
    s_wa=(2, 8),
    s_wb=(2, 8),
    s_wy=(2, 4),
    s_wrel=(2, 5),
    s_ps=(2, 8),
    s_bo=(2, 8),
    s_g=(2, 8),
    s_x=(2, 7),
    s_rs=(7,),
    r_rs=(1,),
    s_ag=(1,),
    r_ag=(8,),
    s_ear=(2, 8),
    s_out=(2,),
    s_ea=(2, 8),
    s_h=(2,),
    s_drs=(2, 8),
    s_dag=(2, 8),
    s_dar=(2,),
)


def kernel(early_scale, deep_scale, vol, we_in, wd_in, ct_in, bo_out, ea_out, gd_out, *scratch):
    r = dict(zip(list(SCRATCH) + list(SEMS), scratch))
    ready = scratch[-1]
    s = lax.axis_index("space")
    f = lax.axis_index("filt")
    core = lax.rem(s, 2)
    other = 1 - core
    sib = s + 1 - 2 * core
    j = lax.div(s, 2)

    def filt_peer(k):
        return lax.rem(f + k, FILT)

    def filt_from(k):
        return lax.rem(f + FILT - k, FILT)

    chips_s = [lax.rem(s + 2 * dj, SPACE) for dj in range(8)]
    chips_f = [lax.rem(f + df, FILT) for df in range(8)]
    owner = j < OWNERS

    barrier = pltpu.get_barrier_semaphore()

    def space_chip(k):
        return lax.rem(s + 2 * k, SPACE)

    x_hi, z = lax.div(f, 4), lax.rem(f, 4)
    near = s + 2 - 4 * lax.rem(j, 2)
    w_to = [(s, 4 * x_hi + lax.rem(z + k, 4)) for k in range(1, 4)]
    w_to += [(near, 4 * (1 - x_hi) + lax.rem(z + k, 4)) for k in range(4)]

    greeted = [(s, filt_peer(k)) for k in range(1, FILT)]
    greeted += [(space_chip(k), f) for k in range(1, 8)]
    greeted += [
        (lax.rem(s + d, SPACE), lax.rem(f + df, FILT))
        for d in (1, SPACE - 1)
        for df in range(FILT)
    ]
    greeted += w_to[3:]
    for device in greeted:
        pl.semaphore_signal(barrier, inc=1, device_id=device, device_id_type=MESH)

    own_vol = pltpu.make_async_copy(vol, r["vp"].at[1:5, 1:17], r["local"].at[0])
    own_vol.start()
    wg = r["wg"]
    w_rows = pl.ds(pl.multiple_of(128 * core + 16 * f, 16), 16)
    w_half = pl.ds(pl.multiple_of(16 * core, 16), 16)
    y = lax.div(s, 4)

    def share(yy):
        return pl.ds(DIRECT + SHARE * yy, SHARE)

    own_wd = [
        pltpu.make_async_copy(wd_in.at[taps, w_half], wg.at[taps, w_rows], r["local"].at[n])
        for n, taps in ((1, pl.ds(0, DIRECT)), (3, share(y)))
    ]
    for c in own_wd:
        c.start()
    own_ct = pltpu.make_async_copy(ct_in, r["ct"], r["local"].at[2])
    own_ct.start()
    own_ct.wait()
    lane = lax.broadcasted_iota(jnp.int32, (32, 128), 1)
    for x in range(2):
        parts = [jnp.zeros((32, 128), F32)] * FILT
        for z in range(8):
            v = r["ct"][8 * x + z].astype(F32)
            v = jnp.concatenate([v, jnp.zeros_like(v)], axis=1)
            here = (lane >= 16 * z) & (lane < 16 * z + 10)
            for q in range(FILT):
                moved = pltpu.roll(v, (16 * z - 8 * q + 1) % 128, 1)
                parts[q] = jnp.where(here, moved, parts[q])
        for q in range(FILT):
            r["cs"][q, x] = parts[q].astype(BF).reshape(2, 16, 128)

    @pl.when(s == 0)
    def _():
        r["cr"][0] = jnp.zeros((2, 8, 16, 128), BF)

    @pl.when(s == SPACE - 1)
    def _():
        r["cr"][3] = jnp.zeros((2, 8, 16, 128), BF)

    zero_rim(r["vp"], 4, 16, 1, s, f)
    zero_rim(r["pp"], 2, 8, 2, s, f)
    r["ps"][:, 0:1] = jnp.zeros((2, 1, 8, 128), BF)
    r["ps"][:, 65:66] = jnp.zeros((2, 1, 8, 128), BF)

    pl.semaphore_wait(barrier, len(greeted))
    halo_v = Halo(vol, 0, r["vp"], 4, 16, 1, r["halo_v"], s, f)
    halo_v.start()
    own_we = pltpu.make_async_copy(we_in, r["we"], r["local"].at[2])
    own_we.start()

    def w_send(taps, sems, k):
        return rcopy(
            wd_in.at[taps, w_half],
            wg.at[taps, w_rows],
            r[sems].at[0, k],
            r[sems].at[1, k],
            w_to[k - 1],
        )

    for k in range(1, 8):
        pl.semaphore_signal(ready, inc=1, device_id=(space_chip(k), f), device_id_type=MESH)

    wb = []
    for k in range(1, FILT):
        wb.append(w_send(share(y), "s_wb", k))
        wb[-1].start()

    wa = []
    for k in range(1, FILT):
        wa.append(w_send(pl.ds(0, DIRECT), "s_wa", k))
        wa[-1].start()

    def cot_copy(src, row, n, device):
        return rcopy(
            src, r["cr"].at[row, :, f], r["s_cot"].at[0, n], r["s_cot"].at[1, n], device
        )

    def cot_all(n):
        whole = r["cs"].at[0:7] if n == 0 else r["cr"].at[0]
        return rcopy(whole, whole, r["s_cot"].at[0, n], r["s_cot"].at[1, n], (s, f))

    for k in range(1, FILT):
        cot_copy(r["cs"].at[filt_peer(k)], slice(1, 3), 0, (s, filt_peer(k))).start()

    @pl.when(s > 0)
    def _():
        for q in range(FILT):
            cot_copy(r["cs"].at[q, 0], 3, 1, (s - 1, q)).start()

    @pl.when(s < SPACE - 1)
    def _():
        for q in range(FILT):
            cot_copy(r["cs"].at[q, 1], 0, 2, (s + 1, q)).start()

    r["cr"][1:3, :, pl.ds(f, 1)] = r["cs"][pl.ds(f, 1)].reshape(2, 2, 1, 16, 128)

    for c in own_wd:
        c.wait()
    for c in wb:
        c.wait_recv()
    w_core = pl.ds(pl.multiple_of(128 * core, 128), 128)

    def w_pass(taps, sems, k, device):
        piece = wg.at[taps, w_core]
        return rcopy(piece, piece, r[sems].at[0, k], r[sems].at[1, k], device)

    wy = []
    for k in range(1, 4):
        wy.append(w_pass(share(y), "s_wy", k, (lax.rem(s + 4 * k, SPACE), f)))
        wy[-1].start()
    relay = [w_pass(share(y), "s_wrel", 0, (sib, f))]
    relay[-1].start()
    own_vol.wait()
    halo_v.wait_recv()
    zc = r["zc"]
    for row in range(6):
        x = r["vp"][row].astype(F32)
        zc[row, :, :, 0:128] = shift_rows(x, -1).astype(BF)
        zc[row, :, :, 128:256] = r["vp"][row]
        zc[row, :, :, 256:384] = shift_rows(x, 1).astype(BF)
    own_we.wait()
    acc = r["acc"]
    for ab in range(9):
        a, b = ab // 3, ab % 3
        patch = zc[a : a + 4, b : b + 16].reshape(1024, 384)
        term = dot(patch, r["we"][ab])
        if ab == 0:
            acc[...] = term
        else:
            acc[...] += term
    for half in range(2):
        v = acc[512 * half : 512 * half + 512].reshape(2, 16, 16, 128)
        sig = sigmoid(v)
        r["sg"][2 * half : 2 * half + 2] = sig * (1.0 + v * (1.0 - sig)) * 0.125
        act = v * sig
        act = (act[0] + act[1]).reshape(8, 2, 16, 128)
        r["tmp"][8 * half : 8 * half + 8] = act[:, 0] + act[:, 1]
    tmp = r["tmp"]
    pooled = (tmp[:, pl.ds(0, 8, stride=2), :] + tmp[:, pl.ds(1, 8, stride=2), :]) * 0.125
    pooled = pooled.reshape(2, 8, 8, 128).astype(BF)
    r["pp"][2:4, 2:10] = pooled
    halo_p = Halo(r["pp"], 2, r["pp"], 2, 8, 2, r["halo_p"], s, f)
    halo_p.start()
    r["ps"][:, pl.ds(1 + 8 * f, 8)] = pooled

    for c in wa:
        c.wait_recv()
    relay.append(w_pass(pl.ds(0, DIRECT), "s_wrel", 4, (sib, f)))
    relay[-1].start()
    for k in range(1, 4):
        wy[k - 1].wait_recv()
        relay.append(w_pass(share(lax.rem(y + 4 - k, 4)), "s_wrel", k, (sib, f)))
        relay[-1].start()
    cot_all(0).wait_recv()
    pl.when(s > 0)(cot_all(2).wait_recv)
    pl.when(s < SPACE - 1)(cot_all(1).wait_recv)
    cells = r["cells"]
    cot = []
    for row in range(4):
        v = r["cr"][row].reshape(256, 128).astype(F32).T
        halves = []
        for h in range(2):
            cells[h] = v[:, 128 * h : 128 * h + 128]
            cols = [cells[h, pl.ds(col, 8, stride=16), :] for col in range(10)]
            halves.append(jnp.concatenate(cols, axis=0))
        cot.append(jnp.concatenate(halves, axis=1))
    cot = jnp.concatenate(cot, axis=0)
    halo_p.wait_recv()
    pz = r["pz"]
    for row in range(6):
        x = r["pp"][row].astype(F32)
        pz[row, :, :, 0:128] = shift_rows(x, -1)
        pz[row, :, :, 128:256] = x
        pz[row, :, :, 256:384] = shift_rows(x, 1)
    for c in relay:
        c.wait_recv()

    pss = []
    for k in range(1, FILT):
        pss.append(
            rcopy(
                r["pp"].at[2:4, 2:10],
                r["ps"].at[:, pl.ds(1 + 8 * f, 8)],
                r["s_ps"].at[0, k],
                r["s_ps"].at[1, k],
                (s, filt_peer(k)),
            )
        )
        pss[-1].start()

    pre = jnp.zeros((320, 256), F32)
    for ab in range(9):
        a, b = ab // 3, ab % 3
        patch = pz[a : a + 4, b : b + 10].reshape(320, 384).astype(BF)
        taps = jnp.concatenate([wg[3 * ab + c] for c in range(3)], axis=1)
        pre = pre + dot_t(patch, taps)
    sig = sigmoid(pre)
    g = (cot * (sig * (1.0 + pre * (1.0 - sig)))).astype(BF)
    gf = r["gf"]
    gf[...] = g.astype(F32).reshape(4, 10, 8, 256)
    r["act"][...] = (pre * sig).reshape(4, 10, 8, 256)[1:3, 1:9].reshape(128, 256)
    back = jnp.zeros((128, 384), F32)
    for ab in range(9):
        a, b = ab // 3, ab % 3
        patch = gf[2 - a : 4 - a, 2 - b : 10 - b].reshape(128, 256).astype(BF)
        taps = jnp.concatenate([wg[3 * ab + c] for c in range(3)], axis=1)
        back = back + dot(patch, taps)
    back = back.reshape(16, 8, 384)
    gpool = (
        shift_rows(back[:, :, 0:128], 1)
        + back[:, :, 128:256]
        + shift_rows(back[:, :, 256:384], -1)
    )
    gpool = gpool.astype(BF).astype(F32)
    tmp[:, pl.ds(0, 8, stride=2), :] = gpool
    tmp[:, pl.ds(1, 8, stride=2), :] = gpool
    for row in range(4):
        spread = tmp[8 * (row // 2) : 8 * (row // 2) + 8]
        spread = jnp.broadcast_to(spread[:, None], (8, 2, 16, 128)).reshape(16, 16, 128)
        grad = (spread * r["sg"][row]).astype(BF).astype(F32).reshape(256, 128)
        r["gt"][:, 256 * row : 256 * row + 256] = grad.T.astype(BF)

    gt = r["gt"][...]
    es, er, ea = r["es"], r["er"], r["ea"]
    pl.semaphore_wait(ready, 7)

    def group_of(k):
        return lax.rem(j + k, OWNERS)

    def x_copy(k):
        return rcopy(
            r["xs"].at[k], r["xr"].at[k], r["s_x"].at[0, k], r["s_x"].at[1, k], (sib, f)
        )

    gcs = []
    lanes_f = pl.ds(pl.multiple_of(128 * f, 128), 128)

    def send_gradients():
        for a in range(3):
            piece = gf[2 - a : 4 - a, 1:9].reshape(128, 256)
            r["gs"][:, a] = piece.T.astype(BF).reshape(2, 8, 16, 128)
        for k in range(1, FILT):
            gcs.append(
                rcopy(
                    r["gs"].at[:, :, filt_peer(k)],
                    r["gr"].at[:, :, :, lanes_f],
                    r["s_g"].at[0, k],
                    r["s_g"].at[1, k],
                    (s, filt_peer(k)),
                )
            )
            gcs[-1].start()
        r["gr"][:, :, :, lanes_f] = r["gs"][:, :, pl.ds(f, 1)].reshape(2, 3, 16, 128)

    for k in range(OWNERS + 1):
        if k < OWNERS:
            patches = []
            for n in range(GROUP):
                t = jnp.minimum(GROUP * group_of(k) + n, 26)
                a, b, c = lax.div(t, 9), lax.rem(lax.div(t, 3), 3), lax.rem(t, 3)
                lanes = pl.ds(pl.multiple_of(128 * c, 128), 128)
                patch = zc[pl.ds(a, 4), pl.ds(b, 16), :, lanes]
                patches.append(patch.reshape(1024, 128))
            term = dot(gt, jnp.concatenate(patches, axis=1))

            @pl.when(core == 0)
            def _():
                r["xo"][k] = term[0:64]
                r["xs"][k] = term[64:128].astype(BF)

            @pl.when(core == 1)
            def _():
                r["xo"][k] = term[64:128]
                r["xs"][k] = term[0:64].astype(BF)

            x_copy(k).start()
        if k == 1:
            send_gradients()
        if k >= 1:
            p = k - 1
            x_copy(p).wait_recv()
            total = r["xo"][p] + r["xr"][p].astype(F32)
            es[p] = total.reshape(8, 8, 512).astype(BF)
            to_j = group_of(p)
            dj = lax.rem(to_j - j + 8, 8)
            for df in range(8):
                copy = rcopy(
                    es.at[p, chips_f[df]],
                    er.at[8 * dj + df],
                    r["s_rs"].at[p],
                    r["r_rs"].at[0],
                    (2 * to_j + core, chips_f[df]),
                )
                if p == 0 and df == 0:
                    pl.when(j >= OWNERS)(copy.start)
                else:
                    copy.start()

    for c in pss:
        c.wait_recv()
    ps3 = r["ps3"]
    for row in range(2):
        x = r["ps"][row].astype(F32)
        ps3[row, :, :, 0:128] = shift_rows(x, -1)
        ps3[row, :, :, 128:256] = x
        ps3[row, :, :, 256:384] = shift_rows(x, 1)
    for q in range(8):
        for b in range(3):
            patch = ps3[:, 8 * q + b : 8 * q + b + 8].reshape(128, 384).astype(BF)
            r["pb"][128 * q : 128 * q + 128, 384 * b : 384 * b + 384] = patch
    for c in gcs:
        c.wait_recv()
    deep = dot(r["gr"][...].reshape(96, 1024), r["pb"][...])

    @pl.when(core == 0)
    def _():
        r["ho"][...] = deep[0:48]
        r["hs"][...] = deep[48:96].astype(BF)

    @pl.when(core == 1)
    def _():
        r["ho"][...] = deep[48:96]
        r["hs"][...] = deep[0:48].astype(BF)

    hcopy = rcopy(r["hs"], r["hr"], r["s_h"].at[0], r["s_h"].at[1], (sib, f))
    hcopy.start()


    act = swap_cells(r["cells"], r["act"][...])
    r["bs"][...] = act.T.astype(BF).reshape(2, 8, 16, 128)
    bos = []
    for k in range(1, FILT):
        bos.append(
            rcopy(
                r["bs"].at[:, filt_peer(k)],
                r["br"].at[f],
                r["s_bo"].at[0, k],
                r["s_bo"].at[1, k],
                (s, filt_peer(k)),
            )
        )
        bos[-1].start()
    r["br"][pl.ds(f, 1)] = r["bs"][:, pl.ds(f, 1)].reshape(1, 2, 16, 128)

    hcopy.wait_recv()
    dsd = r["dsd"]
    dsd[27:28] = jnp.zeros((1, 16, 128), BF)
    total = r["ho"][...] + r["hr"][...].astype(F32)
    for a in range(3):
        for bc in range(9):
            dsd[9 * a + bc] = total[16 * a : 16 * a + 16, 128 * bc : 128 * bc + 128].astype(BF)

    def first_of(jj):
        return jnp.minimum(GROUP * jj, GROUP * (OWNERS - 1))

    drs = []
    for k in range(1, 8):
        to_s = space_chip(k)
        to_j = lax.div(to_s, 2)
        copy = rcopy(
            dsd.at[pl.ds(first_of(to_j), GROUP)],
            r["dr"].at[k],
            r["s_drs"].at[0, k],
            r["s_drs"].at[1, k],
            (to_s, f),
        )
        pl.when(to_j < OWNERS)(copy.start)
        drs.append((copy, to_j < OWNERS))

    mine_t = pl.ds(first_of(j), GROUP)

    ag_sends = []
    for k in range(1, CHIPS):
        piece = ea.at[core, jnp.minimum(j, OWNERS - 1), f]
        device = (chips_s[k // 8], chips_f[k % 8])
        ag_sends.append(rcopy(piece, piece, r["s_ag"].at[0], r["r_ag"].at[k // 8], device))

    @pl.when(owner)
    def _():
        er[0] = es[0, pl.ds(f, 1)].reshape(8, 512)
        landed = er.at[1:CHIPS]
        rcopy(landed, landed, r["s_rs"].at[0], r["r_rs"].at[0], (s, f)).wait_recv()
        total = jnp.sum(er[0:8].astype(F32), axis=0)
        for n in range(1, 8):
            total = total + jnp.sum(er[8 * n : 8 * n + 8].astype(F32), axis=0)
        total = (total * early_scale).astype(BF).reshape(1, 1, 1, 8, 512)
        ea[pl.ds(core, 1), pl.ds(j, 1), pl.ds(f, 1)] = total
        for c in ag_sends:
            c.start()

    for c in bos:
        c.wait_recv()
    parts = [jnp.zeros((32, 128), F32)] * 16
    for q in range(FILT):
        x = r["br"][q].reshape(32, 128).astype(F32)
        for p in range(16):
            moved = pltpu.roll(x, (8 * q - 8 * p) % 128, 1)
            parts[p] = jnp.where(lane // 8 == q, moved, parts[p])
    for p in range(16):
        r["bo"][p] = parts[p][:, 0:64].astype(BF)
    bo_copy = pltpu.make_async_copy(r["bo"], bo_out, r["s_out"].at[0])
    bo_copy.start()

    da = r["da"]
    piece = da.at[core, mine_t]
    dag = []
    for k in range(1, 8):
        dag.append(
            rcopy(piece, piece, r["s_dag"].at[0, k], r["s_dag"].at[1, k], (space_chip(k), f))
        )

    @pl.when(owner)
    def _():
        total = dsd[mine_t].astype(F32)
        for k in range(1, 8):
            drs[k - 1][0].wait_recv()
            total = total + r["dr"][k].astype(F32)
        da[pl.ds(core, 1), mine_t] = (total * deep_scale).astype(BF).reshape(1, GROUP, 16, 128)
        for c in dag:
            c.start()

    def ear_copy(dj):
        piece = ea.at[core, lax.rem(j - dj + 8, 8)]
        return rcopy(piece, piece, r["s_ear"].at[0, dj], r["s_ear"].at[1, dj], (sib, f))

    def ea_copy(half, dj):
        g = lax.rem(j - dj + 8, 8)
        return pltpu.make_async_copy(ea.at[half, g], ea_out.at[half, g], r["s_ea"].at[half, dj])

    for dj in range(8):

        @pl.when(lax.rem(j - dj + 8, 8) < OWNERS)
        def _():
            landed = ea.at[core, lax.rem(j - dj + 8, 8), 0 : (8 if dj else 7)]
            rcopy(landed, landed, r["s_ag"].at[0], r["r_ag"].at[dj], (s, f)).wait_recv()
            ear_copy(dj).start()
            ea_copy(core, dj).start()

    for k in range(1, 8):
        from_j = lax.div(lax.rem(s + SPACE - 2 * k, SPACE), 2)
        pl.when(from_j < OWNERS)(dag[k - 1].wait_recv)
    dar = rcopy(da.at[core], da.at[core], r["s_dar"].at[0], r["s_dar"].at[1], (sib, f))
    dar.start()

    dar.wait_recv()
    for t in range(27):
        r["gd"][t] = da[:, t].reshape(32, 128).astype(F32)
    gd_copy = pltpu.make_async_copy(r["gd"], gd_out, r["s_out"].at[1])
    gd_copy.start()

    for dj in range(8):

        @pl.when(lax.rem(j - dj + 8, 8) < OWNERS)
        def _():
            ear_copy(dj).wait_recv()
            ea_copy(other, dj).start()

    for h in (halo_v, halo_p):
        h.wait_send()
    cot_all(0).wait_send()
    pl.when(s > 0)(cot_all(1).wait_send)
    pl.when(s < SPACE - 1)(cot_all(2).wait_send)
    for c in wa + wb + wy + relay + pss + bos + gcs + [hcopy, dar]:
        c.wait_send()
    for copy, active in drs:
        pl.when(active)(copy.wait_send)

    for k in range(OWNERS):
        x_copy(k).wait_send()

    def rs_sent(k, count):
        left = es.at[k, 0:count]
        rcopy(left, left, r["s_rs"].at[k], r["r_rs"].at[0], (s, f)).wait_send()

    for k in range(1, OWNERS):
        rs_sent(k, 8)

    @pl.when(owner)
    def _():
        rs_sent(0, 7)
        left = er.at[1:CHIPS]
        rcopy(left, left, r["s_ag"].at[0], r["r_rs"].at[0], (s, f)).wait_send()
        for c in dag:
            c.wait_send()

    pl.when(j >= OWNERS)(functools.partial(rs_sent, 0, 8))
    for dj in range(8):

        @pl.when(lax.rem(j - dj + 8, 8) < OWNERS)
        def _():
            ear_copy(dj).wait_send()
            ea_copy(core, dj).wait()
            ea_copy(other, dj).wait()

    bo_copy.wait()
    gd_copy.wait()


def results(bo_in, ea_in, gd_in, bo_out, ge_out, gd_out, bo, ea, gd, ge, sems):
    ins = [pltpu.make_async_copy(ea_in.at[:, g], ea.at[g], sems.at[0, g]) for g in range(OWNERS)]
    ins.append(pltpu.make_async_copy(bo_in, bo, sems.at[0, 7]))
    ins.append(pltpu.make_async_copy(gd_in, gd, sems.at[0, 8]))
    outs = []
    for g in range(OWNERS):
        taps = min(GROUP, 27 - GROUP * g)
        src, dst = ge.at[pl.ds(GROUP * g, taps)], ge_out.at[pl.ds(GROUP * g, taps)]
        outs.append(pltpu.make_async_copy(src, dst, sems.at[1, g]))
    outs.append(pltpu.make_async_copy(bo, bo_out, sems.at[1, 7]))
    outs.append(pltpu.make_async_copy(gd, gd_out, sems.at[1, 8]))
    for c in ins:
        c.start()
    for g in range(OWNERS):
        ins[g].wait()
        block = ea[g].reshape(128, 512).astype(F32)
        for t in range(GROUP * g, min(GROUP * g + GROUP, 27)):
            n = t - GROUP * g
            ge[t] = block[:, 128 * n : 128 * n + 128].T
        outs[g].start()
    for n in (7, 8):
        ins[n].wait()
        outs[n].start()
    for c in outs:
        c.wait()


def shards(volume, w_early, w_deep, cotangent):
    any_ = pl.BlockSpec(memory_space=pl.ANY)
    cells = volume.shape[0] * volume.shape[1] * volume.shape[2] * SPACE * FILT
    body = functools.partial(kernel, 1.0 / math.sqrt(cells), 1.0 / math.sqrt(cells // 8))
    block, early, deep = pl.pallas_call(
        body,
        out_shape=(
            jax.ShapeDtypeStruct((16, 32, 64), BF),
            jax.ShapeDtypeStruct((2, 7, 8, 8, 512), BF),
            jax.ShapeDtypeStruct((27, 32, 128), F32),
        ),
        in_specs=[any_] * 4,
        out_specs=(any_,) * 3,
        scratch_shapes=[pltpu.VMEM(*v) for v in SCRATCH.values()]
        + [pltpu.SemaphoreType.DMA(v) for v in SEMS.values()]
        + [pltpu.SemaphoreType.REGULAR],
        compiler_params=pltpu.CompilerParams(
            collective_id=0, has_side_effects=True, vmem_limit_bytes=56 << 20
        ),
        name="step",
    )(
        volume,
        w_early.reshape(9, 384, 128),
        w_deep.transpose(0, 2, 1),
        cotangent.transpose(0, 2, 3, 1).reshape(16, 32, 64),
    )
    block, early, deep = pl.pallas_call(
        results,
        out_shape=(
            jax.ShapeDtypeStruct((16, 32, 64), BF),
            jax.ShapeDtypeStruct((27, 128, 128), F32),
            jax.ShapeDtypeStruct((27, 32, 128), F32),
        ),
        in_specs=[any_] * 3,
        out_specs=(any_,) * 3,
        scratch_shapes=[
            pltpu.VMEM((16, 32, 64), BF),
            pltpu.VMEM((7, 2, 8, 8, 512), BF),
            pltpu.VMEM((27, 32, 128), F32),
            pltpu.VMEM((27, 128, 128), F32),
            pltpu.SemaphoreType.DMA((2, 9)),
        ],
        compiler_params=pltpu.CompilerParams(vmem_limit_bytes=60 << 20),
        name="results",
    )(block, early, deep)
    block = block.reshape(2, 8, 32, 64).transpose(0, 3, 1, 2)
    return block, early, deep.transpose(0, 2, 1)


def solution(mesh):
    return jax.shard_map(
        shards,
        mesh=mesh,
        in_specs=(
            P("space", "filt", None, None),
            P(),
            P(None, None, "filt"),
            P("space", None, None, "filt"),
        ),
        out_specs=(P("space", None, None, "filt"), P(), P(None, None, "filt")),
        check_vma=False,
    )
```

```python
import functools
import math

import jax
import jax.numpy as jnp
from jax import lax
from jax.experimental import pallas as pl
from jax.experimental.pallas import tpu as pltpu
from jax.sharding import PartitionSpec as P

MESH = pl.DeviceIdType.MESH
BF = jnp.bfloat16
F32 = jnp.float32
SPACE, FILT, CHIPS = 16, 8, 64
DIRS = [(ds, df) for ds in (-1, 0, 1) for df in (-1, 0, 1) if ds or df]
GROUP = 4
DIRECT = 15
SHARE = 3
OWNERS = 7


def rcopy(src, dst, send_sem, recv_sem, device):
    return pltpu.make_async_remote_copy(
        src_ref=src,
        dst_ref=dst,
        send_sem=send_sem,
        recv_sem=recv_sem,
        device_id=device,
        device_id_type=MESH,
    )


def sigmoid(v):
    return 1.0 / (1.0 + jnp.exp(-v))


def shift_rows(v, step):
    size = v.shape[1]
    row = lax.broadcasted_iota(jnp.int32, v.shape, 1)
    edge = size - 1 if step == 1 else 0
    rolled = pltpu.roll(v, (-step) % size, 1)
    return jnp.where(row == edge, 0.0, rolled)


def dot(a, b):
    return lax.dot_general(a, b, (((1,), (0,)), ((), ())), preferred_element_type=F32)


def dot_t(a, b):
    return lax.dot_general(a, b, (((1,), (1,)), ((), ())), preferred_element_type=F32)


def edges(step, size, width):
    if step == 1:
        return size - width, 0, width
    if step == -1:
        return 0, size + width, width
    return 0, width, size


def swap_cells(ref, v):
    halves = []
    for h in range(2):
        ref[h] = v[:, 128 * h : 128 * h + 128]
        rows = [ref[h, pl.ds(64 * x + n, 8, stride=8), :] for x in range(2) for n in range(8)]
        halves.append(jnp.concatenate(rows, axis=0))
    return jnp.concatenate(halves, axis=1)


class Halo:
    def __init__(self, source, base, padded, nx, ny, width, sems, s, f):
        self.items = []
        for k, (ds, df) in enumerate(DIRS):
            sx, dx, lx = edges(ds, nx, width)
            sy, dy, ly = edges(df, ny, width)
            src = source.at[base + sx : base + sx + lx, base + sy : base + sy + ly]
            dst = padded.at[dx : dx + lx, dy : dy + ly]
            to_s, to_f, from_s, from_f = s + ds, f + df, s - ds, f - df
            send = (to_s >= 0) & (to_s < SPACE) & (to_f >= 0) & (to_f < FILT)
            recv = (from_s >= 0) & (from_s < SPACE) & (from_f >= 0) & (from_f < FILT)
            copy = rcopy(src, dst, sems.at[0, k], sems.at[1, k], (to_s, to_f))
            self.items.append((copy, send, recv))

    def start(self):
        for copy, send, _ in self.items:
            pl.when(send)(copy.start)

    def wait_recv(self):
        for copy, _, recv in self.items:
            pl.when(recv)(copy.wait_recv)

    def wait_send(self):
        for copy, send, _ in self.items:
            pl.when(send)(copy.wait_send)


def zero_rim(padded, nx, ny, width, s, f):
    shape = padded.shape
    w = width

    @pl.when(s == 0)
    def _():
        padded[0:w] = jnp.zeros((w,) + shape[1:], padded.dtype)

    @pl.when(s == SPACE - 1)
    def _():
        padded[nx + w : nx + 2 * w] = jnp.zeros((w,) + shape[1:], padded.dtype)

    @pl.when(f == 0)
    def _():
        padded[:, 0:w] = jnp.zeros((shape[0], w) + shape[2:], padded.dtype)

    @pl.when(f == FILT - 1)
    def _():
        padded[:, ny + w : ny + 2 * w] = jnp.zeros((shape[0], w) + shape[2:], padded.dtype)


SCRATCH = dict(
    vp=((6, 18, 16, 128), BF),
    zc=((6, 18, 16, 384), BF),
    we=((9, 384, 128), BF),
    ct=((16, 32, 64), BF),
    wg=((27, 256, 128), BF),
    cs=((8, 2, 2, 16, 128), BF),
    cr=((4, 2, 8, 16, 128), BF),
    acc=((1024, 128), F32),
    sg=((4, 16, 16, 128), F32),
    tmp=((16, 16, 128), F32),
    cells=((2, 128, 128), F32),
    act=((128, 256), F32),
    pp=((6, 12, 8, 128), BF),
    pz=((6, 12, 8, 384), F32),
    ps=((2, 66, 8, 128), BF),
    ps3=((2, 66, 8, 384), F32),
    bs=((2, 8, 16, 128), BF),
    br=((8, 2, 16, 128), BF),
    gf=((4, 10, 8, 256), F32),
    gs=((2, 3, 8, 16, 128), BF),
    gr=((2, 3, 16, 1024), BF),
    gt=((128, 1024), BF),
    xs=((7, 64, 512), BF),
    xr=((7, 64, 512), BF),
    xo=((7, 64, 512), F32),
    es=((7, 8, 8, 512), BF),
    er=((64, 8, 512), BF),
    ea=((2, 7, 8, 8, 512), BF),
    bo=((16, 32, 64), BF),
    gd=((27, 32, 128), F32),
    pb=((1024, 1152), BF),
    hs=((48, 1152), BF),
    hr=((48, 1152), BF),
    ho=((48, 1152), F32),
    dsd=((28, 16, 128), BF),
    dr=((8, 4, 16, 128), BF),
    da=((2, 28, 16, 128), BF),
)
SEMS = dict(
    local=(4,),
    halo_v=(2, 8),
    halo_p=(2, 8),
    s_cot=(2, 3),
    s_wa=(2, 8),
    s_wb=(2, 8),
    s_wy=(2, 4),
    s_wrel=(2, 5),
    s_ps=(2, 8),
    s_bo=(2, 8),
    s_g=(2, 8),
    s_x=(2, 7),
    s_rs=(7,),
    r_rs=(1,),
    s_ag=(1,),
    r_ag=(8,),
    s_ear=(2, 8),
    s_out=(2,),
    s_ea=(2, 8),
    s_h=(2,),
    s_drs=(2, 8),
    s_dag=(2, 8),
    s_dar=(2,),
)


def kernel(early_scale, deep_scale, vol, we_in, wd_in, ct_in, bo_out, ea_out, gd_out, *scratch):
    r = dict(zip(list(SCRATCH) + list(SEMS), scratch))
    ready = scratch[-1]
    s = lax.axis_index("space")
    f = lax.axis_index("filt")
    core = lax.rem(s, 2)
    other = 1 - core
    sib = s + 1 - 2 * core
    j = lax.div(s, 2)

    def filt_peer(k):
        return lax.rem(f + k, FILT)

    def filt_from(k):
        return lax.rem(f + FILT - k, FILT)

    chips_s = [lax.rem(s + 2 * dj, SPACE) for dj in range(8)]
    chips_f = [lax.rem(f + df, FILT) for df in range(8)]
    owner = j < OWNERS

    barrier = pltpu.get_barrier_semaphore()

    def space_chip(k):
        return lax.rem(s + 2 * k, SPACE)

    x_hi, z = lax.div(f, 4), lax.rem(f, 4)
    near = s + 2 - 4 * lax.rem(j, 2)
    w_to = [(s, 4 * x_hi + lax.rem(z + k, 4)) for k in range(1, 4)]
    w_to += [(near, 4 * (1 - x_hi) + lax.rem(z + k, 4)) for k in range(4)]

    greeted = [(s, filt_peer(k)) for k in range(1, FILT)]
    greeted += [(space_chip(k), f) for k in range(1, 8)]
    greeted += [
        (lax.rem(s + d, SPACE), lax.rem(f + df, FILT))
        for d in (1, SPACE - 1)
        for df in range(FILT)
    ]
    greeted += w_to[3:]
    for device in greeted:
        pl.semaphore_signal(barrier, inc=1, device_id=device, device_id_type=MESH)

    own_vol = pltpu.make_async_copy(vol, r["vp"].at[1:5, 1:17], r["local"].at[0])
    own_vol.start()
    wg = r["wg"]
    w_rows = pl.ds(pl.multiple_of(128 * core + 16 * f, 16), 16)
    w_half = pl.ds(pl.multiple_of(16 * core, 16), 16)
    y = lax.div(s, 4)

    def share(yy):
        return pl.ds(DIRECT + SHARE * yy, SHARE)

    own_wd = [
        pltpu.make_async_copy(wd_in.at[taps, w_half], wg.at[taps, w_rows], r["local"].at[n])
        for n, taps in ((1, pl.ds(0, DIRECT)), (3, share(y)))
    ]
    for c in own_wd:
        c.start()
    own_ct = pltpu.make_async_copy(ct_in, r["ct"], r["local"].at[2])
    own_ct.start()
    own_ct.wait()
    lane = lax.broadcasted_iota(jnp.int32, (32, 128), 1)
    for x in range(2):
        parts = [jnp.zeros((32, 128), F32)] * FILT
        for z in range(8):
            v = r["ct"][8 * x + z].astype(F32)
            v = jnp.concatenate([v, jnp.zeros_like(v)], axis=1)
            here = (lane >= 16 * z) & (lane < 16 * z + 10)
            for q in range(FILT):
                moved = pltpu.roll(v, (16 * z - 8 * q + 1) % 128, 1)
                parts[q] = jnp.where(here, moved, parts[q])
        for q in range(FILT):
            r["cs"][q, x] = parts[q].astype(BF).reshape(2, 16, 128)

    @pl.when(s == 0)
    def _():
        r["cr"][0] = jnp.zeros((2, 8, 16, 128), BF)

    @pl.when(s == SPACE - 1)
    def _():
        r["cr"][3] = jnp.zeros((2, 8, 16, 128), BF)

    zero_rim(r["vp"], 4, 16, 1, s, f)
    zero_rim(r["pp"], 2, 8, 2, s, f)
    r["ps"][:, 0:1] = jnp.zeros((2, 1, 8, 128), BF)
    r["ps"][:, 65:66] = jnp.zeros((2, 1, 8, 128), BF)

    pl.semaphore_wait(barrier, len(greeted))
    halo_v = Halo(vol, 0, r["vp"], 4, 16, 1, r["halo_v"], s, f)
    halo_v.start()
    own_we = pltpu.make_async_copy(we_in, r["we"], r["local"].at[2])
    own_we.start()

    def w_send(taps, sems, k):
        return rcopy(
            wd_in.at[taps, w_half],
            wg.at[taps, w_rows],
            r[sems].at[0, k],
            r[sems].at[1, k],
            w_to[k - 1],
        )

    for k in range(1, 8):
        pl.semaphore_signal(ready, inc=1, device_id=(space_chip(k), f), device_id_type=MESH)

    wb = []
    for k in range(1, FILT):
        wb.append(w_send(share(y), "s_wb", k))
        wb[-1].start()

    wa = []
    for k in range(1, FILT):
        wa.append(w_send(pl.ds(0, DIRECT), "s_wa", k))
        wa[-1].start()

    def cot_copy(src, row, n, device):
        return rcopy(
            src, r["cr"].at[row, :, f], r["s_cot"].at[0, n], r["s_cot"].at[1, n], device
        )

    def cot_all(n):
        whole = r["cs"].at[0:7] if n == 0 else r["cr"].at[0]
        return rcopy(whole, whole, r["s_cot"].at[0, n], r["s_cot"].at[1, n], (s, f))

    for k in range(1, FILT):
        cot_copy(r["cs"].at[filt_peer(k)], slice(1, 3), 0, (s, filt_peer(k))).start()

    @pl.when(s > 0)
    def _():
        for q in range(FILT):
            cot_copy(r["cs"].at[q, 0], 3, 1, (s - 1, q)).start()

    @pl.when(s < SPACE - 1)
    def _():
        for q in range(FILT):
            cot_copy(r["cs"].at[q, 1], 0, 2, (s + 1, q)).start()

    r["cr"][1:3, :, pl.ds(f, 1)] = r["cs"][pl.ds(f, 1)].reshape(2, 2, 1, 16, 128)

    for c in own_wd:
        c.wait()
    for c in wb:
        c.wait_recv()
    w_core = pl.ds(pl.multiple_of(128 * core, 128), 128)

    def w_pass(taps, sems, k, device):
        piece = wg.at[taps, w_core]
        return rcopy(piece, piece, r[sems].at[0, k], r[sems].at[1, k], device)

    wy = []
    for k in range(1, 4):
        wy.append(w_pass(share(y), "s_wy", k, (lax.rem(s + 4 * k, SPACE), f)))
        wy[-1].start()
    relay = [w_pass(share(y), "s_wrel", 0, (sib, f))]
    relay[-1].start()
    own_vol.wait()
    halo_v.wait_recv()
    zc = r["zc"]
    for row in range(6):
        x = r["vp"][row].astype(F32)
        zc[row, :, :, 0:128] = shift_rows(x, -1).astype(BF)
        zc[row, :, :, 128:256] = r["vp"][row]
        zc[row, :, :, 256:384] = shift_rows(x, 1).astype(BF)
    own_we.wait()
    acc = r["acc"]
    for ab in range(9):
        a, b = ab // 3, ab % 3
        patch = zc[a : a + 4, b : b + 16].reshape(1024, 384)
        term = dot(patch, r["we"][ab])
        if ab == 0:
            acc[...] = term
        else:
            acc[...] += term
    for half in range(2):
        v = acc[512 * half : 512 * half + 512].reshape(2, 16, 16, 128)
        sig = sigmoid(v)
        r["sg"][2 * half : 2 * half + 2] = sig * (1.0 + v * (1.0 - sig)) * 0.125
        act = v * sig
        act = (act[0] + act[1]).reshape(8, 2, 16, 128)
        r["tmp"][8 * half : 8 * half + 8] = act[:, 0] + act[:, 1]
    tmp = r["tmp"]
    pooled = (tmp[:, pl.ds(0, 8, stride=2), :] + tmp[:, pl.ds(1, 8, stride=2), :]) * 0.125
    pooled = pooled.reshape(2, 8, 8, 128).astype(BF)
    r["pp"][2:4, 2:10] = pooled
    halo_p = Halo(r["pp"], 2, r["pp"], 2, 8, 2, r["halo_p"], s, f)
    halo_p.start()
    r["ps"][:, pl.ds(1 + 8 * f, 8)] = pooled

    for c in wa:
        c.wait_recv()
    relay.append(w_pass(pl.ds(0, DIRECT), "s_wrel", 4, (sib, f)))
    relay[-1].start()
    for k in range(1, 4):
        wy[k - 1].wait_recv()
        relay.append(w_pass(share(lax.rem(y + 4 - k, 4)), "s_wrel", k, (sib, f)))
        relay[-1].start()
    cot_all(0).wait_recv()
    pl.when(s > 0)(cot_all(2).wait_recv)
    pl.when(s < SPACE - 1)(cot_all(1).wait_recv)
    cells = r["cells"]
    cot = []
    for row in range(4):
        v = r["cr"][row].reshape(256, 128).astype(F32).T
        halves = []
        for h in range(2):
            cells[h] = v[:, 128 * h : 128 * h + 128]
            cols = [cells[h, pl.ds(col, 8, stride=16), :] for col in range(10)]
            halves.append(jnp.concatenate(cols, axis=0))
        cot.append(jnp.concatenate(halves, axis=1))
    cot = jnp.concatenate(cot, axis=0)
    halo_p.wait_recv()
    pz = r["pz"]
    for row in range(6):
        x = r["pp"][row].astype(F32)
        pz[row, :, :, 0:128] = shift_rows(x, -1)
        pz[row, :, :, 128:256] = x
        pz[row, :, :, 256:384] = shift_rows(x, 1)
    for c in relay:
        c.wait_recv()

    pss = []
    for k in range(1, FILT):
        pss.append(
            rcopy(
                r["pp"].at[2:4, 2:10],
                r["ps"].at[:, pl.ds(1 + 8 * f, 8)],
                r["s_ps"].at[0, k],
                r["s_ps"].at[1, k],
                (s, filt_peer(k)),
            )
        )
        pss[-1].start()

    pre = jnp.zeros((320, 256), F32)
    for ab in range(9):
        a, b = ab // 3, ab % 3
        patch = pz[a : a + 4, b : b + 10].reshape(320, 384).astype(BF)
        taps = jnp.concatenate([wg[3 * ab + c] for c in range(3)], axis=1)
        pre = pre + dot_t(patch, taps)
    sig = sigmoid(pre)
    g = (cot * (sig * (1.0 + pre * (1.0 - sig)))).astype(BF)
    gf = r["gf"]
    gf[...] = g.astype(F32).reshape(4, 10, 8, 256)
    r["act"][...] = (pre * sig).reshape(4, 10, 8, 256)[1:3, 1:9].reshape(128, 256)
    back = jnp.zeros((128, 384), F32)
    for ab in range(9):
        a, b = ab // 3, ab % 3
        patch = gf[2 - a : 4 - a, 2 - b : 10 - b].reshape(128, 256).astype(BF)
        taps = jnp.concatenate([wg[3 * ab + c] for c in range(3)], axis=1)
        back = back + dot(patch, taps)
    back = back.reshape(16, 8, 384)
    gpool = (
        shift_rows(back[:, :, 0:128], 1)
        + back[:, :, 128:256]
        + shift_rows(back[:, :, 256:384], -1)
    )
    gpool = gpool.astype(BF).astype(F32)
    tmp[:, pl.ds(0, 8, stride=2), :] = gpool
    tmp[:, pl.ds(1, 8, stride=2), :] = gpool
    for row in range(4):
        spread = tmp[8 * (row // 2) : 8 * (row // 2) + 8]
        spread = jnp.broadcast_to(spread[:, None], (8, 2, 16, 128)).reshape(16, 16, 128)
        grad = (spread * r["sg"][row]).astype(BF).astype(F32).reshape(256, 128)
        r["gt"][:, 256 * row : 256 * row + 256] = grad.T.astype(BF)

    gt = r["gt"][...]
    es, er, ea = r["es"], r["er"], r["ea"]
    pl.semaphore_wait(ready, 7)

    def group_of(k):
        return lax.rem(j + k, OWNERS)

    def x_copy(k):
        return rcopy(
            r["xs"].at[k], r["xr"].at[k], r["s_x"].at[0, k], r["s_x"].at[1, k], (sib, f)
        )

    gcs = []
    lanes_f = pl.ds(pl.multiple_of(128 * f, 128), 128)

    def send_gradients():
        for a in range(3):
            piece = gf[2 - a : 4 - a, 1:9].reshape(128, 256)
            r["gs"][:, a] = piece.T.astype(BF).reshape(2, 8, 16, 128)
        for k in range(1, FILT):
            gcs.append(
                rcopy(
                    r["gs"].at[:, :, filt_peer(k)],
                    r["gr"].at[:, :, :, lanes_f],
                    r["s_g"].at[0, k],
                    r["s_g"].at[1, k],
                    (s, filt_peer(k)),
                )
            )
            gcs[-1].start()
        r["gr"][:, :, :, lanes_f] = r["gs"][:, :, pl.ds(f, 1)].reshape(2, 3, 16, 128)

    for k in range(OWNERS + 1):
        if k < OWNERS:
            patches = []
            for n in range(GROUP):
                t = jnp.minimum(GROUP * group_of(k) + n, 26)
                a, b, c = lax.div(t, 9), lax.rem(lax.div(t, 3), 3), lax.rem(t, 3)
                lanes = pl.ds(pl.multiple_of(128 * c, 128), 128)
                patch = zc[pl.ds(a, 4), pl.ds(b, 16), :, lanes]
                patches.append(patch.reshape(1024, 128))
            term = dot(gt, jnp.concatenate(patches, axis=1))

            @pl.when(core == 0)
            def _():
                r["xo"][k] = term[0:64]
                r["xs"][k] = term[64:128].astype(BF)

            @pl.when(core == 1)
            def _():
                r["xo"][k] = term[64:128]
                r["xs"][k] = term[0:64].astype(BF)

            x_copy(k).start()
        if k == 1:
            send_gradients()
        if k >= 1:
            p = k - 1
            x_copy(p).wait_recv()
            total = r["xo"][p] + r["xr"][p].astype(F32)
            es[p] = total.reshape(8, 8, 512).astype(BF)
            to_j = group_of(p)
            dj = lax.rem(to_j - j + 8, 8)
            for df in range(8):
                copy = rcopy(
                    es.at[p, chips_f[df]],
                    er.at[8 * dj + df],
                    r["s_rs"].at[p],
                    r["r_rs"].at[0],
                    (2 * to_j + core, chips_f[df]),
                )
                if p == 0 and df == 0:
                    pl.when(j >= OWNERS)(copy.start)
                else:
                    copy.start()

    for c in pss:
        c.wait_recv()
    ps3 = r["ps3"]
    for row in range(2):
        x = r["ps"][row].astype(F32)
        ps3[row, :, :, 0:128] = shift_rows(x, -1)
        ps3[row, :, :, 128:256] = x
        ps3[row, :, :, 256:384] = shift_rows(x, 1)
    for q in range(8):
        for b in range(3):
            patch = ps3[:, 8 * q + b : 8 * q + b + 8].reshape(128, 384).astype(BF)
            r["pb"][128 * q : 128 * q + 128, 384 * b : 384 * b + 384] = patch
    for c in gcs:
        c.wait_recv()
    deep = dot(r["gr"][...].reshape(96, 1024), r["pb"][...])

    @pl.when(core == 0)
    def _():
        r["ho"][...] = deep[0:48]
        r["hs"][...] = deep[48:96].astype(BF)

    @pl.when(core == 1)
    def _():
        r["ho"][...] = deep[48:96]
        r["hs"][...] = deep[0:48].astype(BF)

    hcopy = rcopy(r["hs"], r["hr"], r["s_h"].at[0], r["s_h"].at[1], (sib, f))
    hcopy.start()


    act = swap_cells(r["cells"], r["act"][...])
    r["bs"][...] = act.T.astype(BF).reshape(2, 8, 16, 128)
    bos = []
    for k in range(1, FILT):
        bos.append(
            rcopy(
                r["bs"].at[:, filt_peer(k)],
                r["br"].at[f],
                r["s_bo"].at[0, k],
                r["s_bo"].at[1, k],
                (s, filt_peer(k)),
            )
        )
        bos[-1].start()
    r["br"][pl.ds(f, 1)] = r["bs"][:, pl.ds(f, 1)].reshape(1, 2, 16, 128)

    hcopy.wait_recv()
    dsd = r["dsd"]
    dsd[27:28] = jnp.zeros((1, 16, 128), BF)
    total = r["ho"][...] + r["hr"][...].astype(F32)
    for a in range(3):
        for bc in range(9):
            dsd[9 * a + bc] = total[16 * a : 16 * a + 16, 128 * bc : 128 * bc + 128].astype(BF)

    def first_of(jj):
        return jnp.minimum(GROUP * jj, GROUP * (OWNERS - 1))

    drs = []
    for k in range(1, 8):
        to_s = space_chip(k)
        to_j = lax.div(to_s, 2)
        copy = rcopy(
            dsd.at[pl.ds(first_of(to_j), GROUP)],
            r["dr"].at[k],
            r["s_drs"].at[0, k],
            r["s_drs"].at[1, k],
            (to_s, f),
        )
        pl.when(to_j < OWNERS)(copy.start)
        drs.append((copy, to_j < OWNERS))

    mine_t = pl.ds(first_of(j), GROUP)

    ag_sends = []
    for k in range(1, CHIPS):
        piece = ea.at[core, jnp.minimum(j, OWNERS - 1), f]
        device = (chips_s[k // 8], chips_f[k % 8])
        ag_sends.append(rcopy(piece, piece, r["s_ag"].at[0], r["r_ag"].at[k // 8], device))

    @pl.when(owner)
    def _():
        er[0] = es[0, pl.ds(f, 1)].reshape(8, 512)
        landed = er.at[1:CHIPS]
        rcopy(landed, landed, r["s_rs"].at[0], r["r_rs"].at[0], (s, f)).wait_recv()
        total = jnp.sum(er[0:8].astype(F32), axis=0)
        for n in range(1, 8):
            total = total + jnp.sum(er[8 * n : 8 * n + 8].astype(F32), axis=0)
        total = (total * early_scale).astype(BF).reshape(1, 1, 1, 8, 512)
        ea[pl.ds(core, 1), pl.ds(j, 1), pl.ds(f, 1)] = total
        for c in ag_sends:
            c.start()

    for c in bos:
        c.wait_recv()
    parts = [jnp.zeros((32, 128), F32)] * 16
    for q in range(FILT):
        x = r["br"][q].reshape(32, 128).astype(F32)
        for p in range(16):
            moved = pltpu.roll(x, (8 * q - 8 * p) % 128, 1)
            parts[p] = jnp.where(lane // 8 == q, moved, parts[p])
    for p in range(16):
        r["bo"][p] = parts[p][:, 0:64].astype(BF)
    bo_copy = pltpu.make_async_copy(r["bo"], bo_out, r["s_out"].at[0])
    bo_copy.start()

    da = r["da"]
    piece = da.at[core, mine_t]
    dag = []
    for k in range(1, 8):
        dag.append(
            rcopy(piece, piece, r["s_dag"].at[0, k], r["s_dag"].at[1, k], (space_chip(k), f))
        )

    @pl.when(owner)
    def _():
        total = dsd[mine_t].astype(F32)
        for k in range(1, 8):
            drs[k - 1][0].wait_recv()
            total = total + r["dr"][k].astype(F32)
        da[pl.ds(core, 1), mine_t] = (total * deep_scale).astype(BF).reshape(1, GROUP, 16, 128)
        for c in dag:
            c.start()

    for k in range(1, 8):
        from_j = lax.div(lax.rem(s + SPACE - 2 * k, SPACE), 2)
        pl.when(from_j < OWNERS)(dag[k - 1].wait_recv)
    dar = rcopy(da.at[core], da.at[core], r["s_dar"].at[0], r["s_dar"].at[1], (sib, f))
    dar.start()

    def ear_copy(dj):
        piece = ea.at[core, lax.rem(j - dj + 8, 8)]
        return rcopy(piece, piece, r["s_ear"].at[0, dj], r["s_ear"].at[1, dj], (sib, f))

    def ea_copy(half, dj):
        g = lax.rem(j - dj + 8, 8)
        return pltpu.make_async_copy(ea.at[half, g], ea_out.at[half, g], r["s_ea"].at[half, dj])

    for dj in range(8):

        @pl.when(lax.rem(j - dj + 8, 8) < OWNERS)
        def _():
            landed = ea.at[core, lax.rem(j - dj + 8, 8), 0 : (8 if dj else 7)]
            rcopy(landed, landed, r["s_ag"].at[0], r["r_ag"].at[dj], (s, f)).wait_recv()
            ear_copy(dj).start()
            ea_copy(core, dj).start()

    dar.wait_recv()
    for t in range(27):
        r["gd"][t] = da[:, t].reshape(32, 128).astype(F32)
    gd_copy = pltpu.make_async_copy(r["gd"], gd_out, r["s_out"].at[1])
    gd_copy.start()

    for dj in range(8):

        @pl.when(lax.rem(j - dj + 8, 8) < OWNERS)
        def _():
            ear_copy(dj).wait_recv()
            ea_copy(other, dj).start()

    for h in (halo_v, halo_p):
        h.wait_send()
    cot_all(0).wait_send()
    pl.when(s > 0)(cot_all(1).wait_send)
    pl.when(s < SPACE - 1)(cot_all(2).wait_send)
    for c in wa + wb + wy + relay + pss + bos + gcs + [hcopy, dar]:
        c.wait_send()
    for copy, active in drs:
        pl.when(active)(copy.wait_send)

    for k in range(OWNERS):
        x_copy(k).wait_send()

    def rs_sent(k, count):
        left = es.at[k, 0:count]
        rcopy(left, left, r["s_rs"].at[k], r["r_rs"].at[0], (s, f)).wait_send()

    for k in range(1, OWNERS):
        rs_sent(k, 8)

    @pl.when(owner)
    def _():
        rs_sent(0, 7)
        left = er.at[1:CHIPS]
        rcopy(left, left, r["s_ag"].at[0], r["r_rs"].at[0], (s, f)).wait_send()
        for c in dag:
            c.wait_send()

    pl.when(j >= OWNERS)(functools.partial(rs_sent, 0, 8))
    for dj in range(8):

        @pl.when(lax.rem(j - dj + 8, 8) < OWNERS)
        def _():
            ear_copy(dj).wait_send()
            ea_copy(core, dj).wait()
            ea_copy(other, dj).wait()

    bo_copy.wait()
    gd_copy.wait()


def results(bo_in, ea_in, gd_in, bo_out, ge_out, gd_out, bo, ea, gd, ge, sems):
    ins = [pltpu.make_async_copy(ea_in.at[:, g], ea.at[g], sems.at[0, g]) for g in range(OWNERS)]
    ins.append(pltpu.make_async_copy(bo_in, bo, sems.at[0, 7]))
    ins.append(pltpu.make_async_copy(gd_in, gd, sems.at[0, 8]))
    outs = []
    for g in range(OWNERS):
        taps = min(GROUP, 27 - GROUP * g)
        src, dst = ge.at[pl.ds(GROUP * g, taps)], ge_out.at[pl.ds(GROUP * g, taps)]
        outs.append(pltpu.make_async_copy(src, dst, sems.at[1, g]))
    outs.append(pltpu.make_async_copy(bo, bo_out, sems.at[1, 7]))
    outs.append(pltpu.make_async_copy(gd, gd_out, sems.at[1, 8]))
    for c in ins:
        c.start()
    for g in range(OWNERS):
        ins[g].wait()
        block = ea[g].reshape(128, 512).astype(F32)
        for t in range(GROUP * g, min(GROUP * g + GROUP, 27)):
            n = t - GROUP * g
            ge[t] = block[:, 128 * n : 128 * n + 128].T
        outs[g].start()
    for n in (7, 8):
        ins[n].wait()
        outs[n].start()
    for c in outs:
        c.wait()


def shards(volume, w_early, w_deep, cotangent):
    any_ = pl.BlockSpec(memory_space=pl.ANY)
    cells = volume.shape[0] * volume.shape[1] * volume.shape[2] * SPACE * FILT
    body = functools.partial(kernel, 1.0 / math.sqrt(cells), 1.0 / math.sqrt(cells // 8))
    block, early, deep = pl.pallas_call(
        body,
        out_shape=(
            jax.ShapeDtypeStruct((16, 32, 64), BF),
            jax.ShapeDtypeStruct((2, 7, 8, 8, 512), BF),
            jax.ShapeDtypeStruct((27, 32, 128), F32),
        ),
        in_specs=[any_] * 4,
        out_specs=(any_,) * 3,
        scratch_shapes=[pltpu.VMEM(*v) for v in SCRATCH.values()]
        + [pltpu.SemaphoreType.DMA(v) for v in SEMS.values()]
        + [pltpu.SemaphoreType.REGULAR],
        compiler_params=pltpu.CompilerParams(
            collective_id=0, has_side_effects=True, vmem_limit_bytes=56 << 20
        ),
        name="step",
    )(
        volume,
        w_early.reshape(9, 384, 128),
        w_deep.transpose(0, 2, 1),
        cotangent.transpose(0, 2, 3, 1).reshape(16, 32, 64),
    )
    block, early, deep = pl.pallas_call(
        results,
        out_shape=(
            jax.ShapeDtypeStruct((16, 32, 64), BF),
            jax.ShapeDtypeStruct((27, 128, 128), F32),
            jax.ShapeDtypeStruct((27, 32, 128), F32),
        ),
        in_specs=[any_] * 3,
        out_specs=(any_,) * 3,
        scratch_shapes=[
            pltpu.VMEM((16, 32, 64), BF),
            pltpu.VMEM((7, 2, 8, 8, 512), BF),
            pltpu.VMEM((27, 32, 128), F32),
            pltpu.VMEM((27, 128, 128), F32),
            pltpu.SemaphoreType.DMA((2, 9)),
        ],
        compiler_params=pltpu.CompilerParams(vmem_limit_bytes=60 << 20),
        name="results",
    )(block, early, deep)
    block = block.reshape(2, 8, 32, 64).transpose(0, 3, 1, 2)
    return block, early, deep.transpose(0, 2, 1)


def solution(mesh):
    return jax.shard_map(
        shards,
        mesh=mesh,
        in_specs=(
            P("space", "filt", None, None),
            P(),
            P(None, None, "filt"),
            P("space", None, None, "filt"),
        ),
        out_specs=(P("space", None, None, "filt"), P(), P(None, None, "filt")),
        check_vma=False,
    )
```

```python
import functools
import math

import jax
import jax.numpy as jnp
from jax import lax
from jax.experimental import pallas as pl
from jax.experimental.pallas import tpu as pltpu
from jax.sharding import PartitionSpec as P

MESH = pl.DeviceIdType.MESH
BF = jnp.bfloat16
F32 = jnp.float32
SPACE, FILT, CHIPS = 16, 8, 64
DIRS = [(ds, df) for ds in (-1, 0, 1) for df in (-1, 0, 1) if ds or df]
GROUP = 4
DIRECT = 15
SHARE = 3
OWNERS = 7


def rcopy(src, dst, send_sem, recv_sem, device):
    return pltpu.make_async_remote_copy(
        src_ref=src,
        dst_ref=dst,
        send_sem=send_sem,
        recv_sem=recv_sem,
        device_id=device,
        device_id_type=MESH,
    )


def sigmoid(v):
    return 1.0 / (1.0 + jnp.exp(-v))


def shift_rows(v, step):
    size = v.shape[1]
    row = lax.broadcasted_iota(jnp.int32, v.shape, 1)
    edge = size - 1 if step == 1 else 0
    rolled = pltpu.roll(v, (-step) % size, 1)
    return jnp.where(row == edge, 0.0, rolled)


def dot(a, b):
    return lax.dot_general(a, b, (((1,), (0,)), ((), ())), preferred_element_type=F32)


def dot_t(a, b):
    return lax.dot_general(a, b, (((1,), (1,)), ((), ())), preferred_element_type=F32)


def edges(step, size, width):
    if step == 1:
        return size - width, 0, width
    if step == -1:
        return 0, size + width, width
    return 0, width, size


def swap_cells(ref, v):
    halves = []
    for h in range(2):
        ref[h] = v[:, 128 * h : 128 * h + 128]
        rows = [ref[h, pl.ds(64 * x + n, 8, stride=8), :] for x in range(2) for n in range(8)]
        halves.append(jnp.concatenate(rows, axis=0))
    return jnp.concatenate(halves, axis=1)


class Halo:
    def __init__(self, source, base, padded, nx, ny, width, sems, s, f):
        self.items = []
        for k, (ds, df) in enumerate(DIRS):
            sx, dx, lx = edges(ds, nx, width)
            sy, dy, ly = edges(df, ny, width)
            src = source.at[base + sx : base + sx + lx, base + sy : base + sy + ly]
            dst = padded.at[dx : dx + lx, dy : dy + ly]
            to_s, to_f, from_s, from_f = s + ds, f + df, s - ds, f - df
            send = (to_s >= 0) & (to_s < SPACE) & (to_f >= 0) & (to_f < FILT)
            recv = (from_s >= 0) & (from_s < SPACE) & (from_f >= 0) & (from_f < FILT)
            copy = rcopy(src, dst, sems.at[0, k], sems.at[1, k], (to_s, to_f))
            self.items.append((copy, send, recv))

    def start(self):
        for copy, send, _ in self.items:
            pl.when(send)(copy.start)

    def wait_recv(self):
        for copy, _, recv in self.items:
            pl.when(recv)(copy.wait_recv)

    def wait_send(self):
        for copy, send, _ in self.items:
            pl.when(send)(copy.wait_send)


def zero_rim(padded, nx, ny, width, s, f):
    shape = padded.shape
    w = width

    @pl.when(s == 0)
    def _():
        padded[0:w] = jnp.zeros((w,) + shape[1:], padded.dtype)

    @pl.when(s == SPACE - 1)
    def _():
        padded[nx + w : nx + 2 * w] = jnp.zeros((w,) + shape[1:], padded.dtype)

    @pl.when(f == 0)
    def _():
        padded[:, 0:w] = jnp.zeros((shape[0], w) + shape[2:], padded.dtype)

    @pl.when(f == FILT - 1)
    def _():
        padded[:, ny + w : ny + 2 * w] = jnp.zeros((shape[0], w) + shape[2:], padded.dtype)


SCRATCH = dict(
    vp=((6, 18, 16, 128), BF),
    zc=((6, 18, 16, 384), BF),
    we=((9, 384, 128), BF),
    ct=((16, 32, 64), BF),
    wg=((27, 256, 128), BF),
    cs=((8, 2, 2, 16, 128), BF),
    cr=((4, 2, 8, 16, 128), BF),
    acc=((1024, 128), F32),
    sg=((4, 16, 16, 128), F32),
    tmp=((16, 16, 128), F32),
    cells=((2, 128, 128), F32),
    act=((128, 256), F32),
    pp=((6, 12, 8, 128), BF),
    pz=((6, 12, 8, 384), F32),
    ps=((2, 66, 8, 128), BF),
    ps3=((2, 66, 8, 384), F32),
    bs=((2, 8, 16, 128), BF),
    br=((8, 2, 16, 128), BF),
    gf=((4, 10, 8, 256), F32),
    gs=((2, 3, 8, 16, 128), BF),
    gr=((2, 3, 16, 1024), BF),
    gt=((128, 1024), BF),
    xs=((7, 64, 512), BF),
    xr=((7, 64, 512), BF),
    xo=((7, 64, 512), F32),
    es=((7, 8, 8, 512), BF),
    er=((64, 8, 512), BF),
    ea=((2, 7, 8, 8, 512), BF),
    bo=((16, 32, 64), BF),
    gd=((27, 32, 128), F32),
    pb=((1024, 1152), BF),
    hs=((48, 1152), BF),
    hr=((48, 1152), BF),
    ho=((48, 1152), F32),
    dsd=((28, 16, 128), BF),
    dr=((8, 4, 16, 128), BF),
    da=((2, 28, 16, 128), BF),
)
SEMS = dict(
    local=(4,),
    halo_v=(2, 8),
    halo_p=(2, 8),
    s_cot=(2, 3),
    s_wa=(2, 8),
    s_wb=(2, 8),
    s_wy=(2, 4),
    s_wrel=(2, 5),
    s_ps=(2, 8),
    s_bo=(2, 8),
    s_g=(2, 8),
    s_x=(2, 7),
    s_rs=(7,),
    r_rs=(1,),
    s_ag=(1,),
    r_ag=(8,),
    s_ear=(2, 8),
    s_out=(2,),
    s_ea=(2, 8),
    s_h=(2,),
    s_drs=(2, 8),
    s_dag=(2, 8),
    s_dar=(2,),
)


def kernel(early_scale, deep_scale, vol, we_in, wd_in, ct_in, bo_out, ea_out, gd_out, *scratch):
    r = dict(zip(list(SCRATCH) + list(SEMS), scratch))
    ready = scratch[-1]
    s = lax.axis_index("space")
    f = lax.axis_index("filt")
    core = lax.rem(s, 2)
    other = 1 - core
    sib = s + 1 - 2 * core
    j = lax.div(s, 2)

    def filt_peer(k):
        return lax.rem(f + k, FILT)

    def filt_from(k):
        return lax.rem(f + FILT - k, FILT)

    chips_s = [lax.rem(s + 2 * dj, SPACE) for dj in range(8)]
    chips_f = [lax.rem(f + df, FILT) for df in range(8)]
    owner = j < OWNERS

    barrier = pltpu.get_barrier_semaphore()

    def space_chip(k):
        return lax.rem(s + 2 * k, SPACE)

    x_hi, z = lax.div(f, 4), lax.rem(f, 4)
    near = s + 2 - 4 * lax.rem(j, 2)
    w_to = [(s, 4 * x_hi + lax.rem(z + k, 4)) for k in range(1, 4)]
    w_to += [(near, 4 * (1 - x_hi) + lax.rem(z + k, 4)) for k in range(4)]

    greeted = [(s, filt_peer(k)) for k in range(1, FILT)]
    greeted += [(space_chip(k), f) for k in range(1, 8)]
    greeted += [
        (lax.rem(s + d, SPACE), lax.rem(f + df, FILT))
        for d in (1, SPACE - 1)
        for df in range(FILT)
    ]
    greeted += w_to[3:]
    for device in greeted:
        pl.semaphore_signal(barrier, inc=1, device_id=device, device_id_type=MESH)

    own_vol = pltpu.make_async_copy(vol, r["vp"].at[1:5, 1:17], r["local"].at[0])
    own_vol.start()
    wg = r["wg"]
    w_rows = pl.ds(pl.multiple_of(128 * core + 16 * f, 16), 16)
    w_half = pl.ds(pl.multiple_of(16 * core, 16), 16)
    y = lax.div(s, 4)

    def share(yy):
        return pl.ds(DIRECT + SHARE * yy, SHARE)

    own_wd = [
        pltpu.make_async_copy(wd_in.at[taps, w_half], wg.at[taps, w_rows], r["local"].at[n])
        for n, taps in ((1, pl.ds(0, DIRECT)), (3, share(y)))
    ]
    for c in own_wd:
        c.start()
    own_ct = pltpu.make_async_copy(ct_in, r["ct"], r["local"].at[2])
    own_ct.start()
    own_ct.wait()
    lane = lax.broadcasted_iota(jnp.int32, (32, 128), 1)
    for x in range(2):
        parts = [jnp.zeros((32, 128), F32)] * FILT
        for z in range(8):
            v = r["ct"][8 * x + z].astype(F32)
            v = jnp.concatenate([v, jnp.zeros_like(v)], axis=1)
            here = (lane >= 16 * z) & (lane < 16 * z + 10)
            for q in range(FILT):
                moved = pltpu.roll(v, (16 * z - 8 * q + 1) % 128, 1)
                parts[q] = jnp.where(here, moved, parts[q])
        for q in range(FILT):
            r["cs"][q, x] = parts[q].astype(BF).reshape(2, 16, 128)

    @pl.when(s == 0)
    def _():
        r["cr"][0] = jnp.zeros((2, 8, 16, 128), BF)

    @pl.when(s == SPACE - 1)
    def _():
        r["cr"][3] = jnp.zeros((2, 8, 16, 128), BF)

    zero_rim(r["vp"], 4, 16, 1, s, f)
    zero_rim(r["pp"], 2, 8, 2, s, f)
    r["ps"][:, 0:1] = jnp.zeros((2, 1, 8, 128), BF)
    r["ps"][:, 65:66] = jnp.zeros((2, 1, 8, 128), BF)

    pl.semaphore_wait(barrier, len(greeted))
    halo_v = Halo(vol, 0, r["vp"], 4, 16, 1, r["halo_v"], s, f)
    halo_v.start()
    own_we = pltpu.make_async_copy(we_in, r["we"], r["local"].at[2])
    own_we.start()

    def w_send(taps, sems, k):
        return rcopy(
            wd_in.at[taps, w_half],
            wg.at[taps, w_rows],
            r[sems].at[0, k],
            r[sems].at[1, k],
            w_to[k - 1],
        )

    for k in range(1, 8):
        pl.semaphore_signal(ready, inc=1, device_id=(space_chip(k), f), device_id_type=MESH)

    wb = []
    for k in range(1, FILT):
        wb.append(w_send(share(y), "s_wb", k))
        wb[-1].start()

    wa = []
    for k in range(1, FILT):
        wa.append(w_send(pl.ds(0, DIRECT), "s_wa", k))
        wa[-1].start()

    def cot_copy(src, row, n, device):
        return rcopy(
            src, r["cr"].at[row, :, f], r["s_cot"].at[0, n], r["s_cot"].at[1, n], device
        )

    def cot_all(n):
        whole = r["cs"].at[0:7] if n == 0 else r["cr"].at[0]
        return rcopy(whole, whole, r["s_cot"].at[0, n], r["s_cot"].at[1, n], (s, f))

    for k in range(1, FILT):
        cot_copy(r["cs"].at[filt_peer(k)], slice(1, 3), 0, (s, filt_peer(k))).start()

    @pl.when(s > 0)
    def _():
        for q in range(FILT):
            cot_copy(r["cs"].at[q, 0], 3, 1, (s - 1, q)).start()

    @pl.when(s < SPACE - 1)
    def _():
        for q in range(FILT):
            cot_copy(r["cs"].at[q, 1], 0, 2, (s + 1, q)).start()

    r["cr"][1:3, :, pl.ds(f, 1)] = r["cs"][pl.ds(f, 1)].reshape(2, 2, 1, 16, 128)

    for c in own_wd:
        c.wait()
    for c in wb:
        c.wait_recv()
    w_core = pl.ds(pl.multiple_of(128 * core, 128), 128)

    def w_pass(taps, sems, k, device):
        piece = wg.at[taps, w_core]
        return rcopy(piece, piece, r[sems].at[0, k], r[sems].at[1, k], device)

    wy = []
    for k in range(1, 4):
        wy.append(w_pass(share(y), "s_wy", k, (lax.rem(s + 4 * k, SPACE), f)))
        wy[-1].start()
    relay = [w_pass(share(y), "s_wrel", 0, (sib, f))]
    relay[-1].start()
    own_vol.wait()
    halo_v.wait_recv()
    zc = r["zc"]
    for row in range(6):
        x = r["vp"][row].astype(F32)
        zc[row, :, :, 0:128] = shift_rows(x, -1).astype(BF)
        zc[row, :, :, 128:256] = r["vp"][row]
        zc[row, :, :, 256:384] = shift_rows(x, 1).astype(BF)
    own_we.wait()
    acc = r["acc"]
    for ab in range(9):
        a, b = ab // 3, ab % 3
        patch = zc[a : a + 4, b : b + 16].reshape(1024, 384)
        term = dot(patch, r["we"][ab])
        if ab == 0:
            acc[...] = term
        else:
            acc[...] += term
    for half in range(2):
        v = acc[512 * half : 512 * half + 512].reshape(2, 16, 16, 128)
        sig = sigmoid(v)
        r["sg"][2 * half : 2 * half + 2] = sig * (1.0 + v * (1.0 - sig)) * 0.125
        act = v * sig
        act = (act[0] + act[1]).reshape(8, 2, 16, 128)
        r["tmp"][8 * half : 8 * half + 8] = act[:, 0] + act[:, 1]
    tmp = r["tmp"]
    pooled = (tmp[:, pl.ds(0, 8, stride=2), :] + tmp[:, pl.ds(1, 8, stride=2), :]) * 0.125
    pooled = pooled.reshape(2, 8, 8, 128).astype(BF)
    r["pp"][2:4, 2:10] = pooled
    halo_p = Halo(r["pp"], 2, r["pp"], 2, 8, 2, r["halo_p"], s, f)
    halo_p.start()
    r["ps"][:, pl.ds(1 + 8 * f, 8)] = pooled

    for c in wa:
        c.wait_recv()
    relay.append(w_pass(pl.ds(0, DIRECT), "s_wrel", 4, (sib, f)))
    relay[-1].start()
    for k in range(1, 4):
        wy[k - 1].wait_recv()
        relay.append(w_pass(share(lax.rem(y + 4 - k, 4)), "s_wrel", k, (sib, f)))
        relay[-1].start()
    cot_all(0).wait_recv()
    pl.when(s > 0)(cot_all(2).wait_recv)
    pl.when(s < SPACE - 1)(cot_all(1).wait_recv)
    cells = r["cells"]
    cot = []
    for row in range(4):
        v = r["cr"][row].reshape(256, 128).astype(F32).T
        halves = []
        for h in range(2):
            cells[h] = v[:, 128 * h : 128 * h + 128]
            cols = [cells[h, pl.ds(col, 8, stride=16), :] for col in range(10)]
            halves.append(jnp.concatenate(cols, axis=0))
        cot.append(jnp.concatenate(halves, axis=1))
    cot = jnp.concatenate(cot, axis=0)
    halo_p.wait_recv()
    pz = r["pz"]
    for row in range(6):
        x = r["pp"][row].astype(F32)
        pz[row, :, :, 0:128] = shift_rows(x, -1)
        pz[row, :, :, 128:256] = x
        pz[row, :, :, 256:384] = shift_rows(x, 1)
    for c in relay:
        c.wait_recv()

    pss = []
    for k in range(1, FILT):
        pss.append(
            rcopy(
                r["pp"].at[2:4, 2:10],
                r["ps"].at[:, pl.ds(1 + 8 * f, 8)],
                r["s_ps"].at[0, k],
                r["s_ps"].at[1, k],
                (s, filt_peer(k)),
            )
        )
        pss[-1].start()

    pre = jnp.zeros((320, 256), F32)
    for ab in range(9):
        a, b = ab // 3, ab % 3
        patch = pz[a : a + 4, b : b + 10].reshape(320, 384).astype(BF)
        taps = jnp.concatenate([wg[3 * ab + c] for c in range(3)], axis=1)
        pre = pre + dot_t(patch, taps)
    sig = sigmoid(pre)
    g = (cot * (sig * (1.0 + pre * (1.0 - sig)))).astype(BF)
    gf = r["gf"]
    gf[...] = g.astype(F32).reshape(4, 10, 8, 256)
    r["act"][...] = (pre * sig).reshape(4, 10, 8, 256)[1:3, 1:9].reshape(128, 256)
    back = jnp.zeros((128, 384), F32)
    for ab in range(9):
        a, b = ab // 3, ab % 3
        patch = gf[2 - a : 4 - a, 2 - b : 10 - b].reshape(128, 256).astype(BF)
        taps = jnp.concatenate([wg[3 * ab + c] for c in range(3)], axis=1)
        back = back + dot(patch, taps)
    back = back.reshape(16, 8, 384)
    gpool = (
        shift_rows(back[:, :, 0:128], 1)
        + back[:, :, 128:256]
        + shift_rows(back[:, :, 256:384], -1)
    )
    gpool = gpool.astype(BF).astype(F32)
    tmp[:, pl.ds(0, 8, stride=2), :] = gpool
    tmp[:, pl.ds(1, 8, stride=2), :] = gpool
    for row in range(4):
        spread = tmp[8 * (row // 2) : 8 * (row // 2) + 8]
        spread = jnp.broadcast_to(spread[:, None], (8, 2, 16, 128)).reshape(16, 16, 128)
        grad = (spread * r["sg"][row]).astype(BF).astype(F32).reshape(256, 128)
        r["gt"][:, 256 * row : 256 * row + 256] = grad.T.astype(BF)

    gt = r["gt"][...]
    es, er, ea = r["es"], r["er"], r["ea"]
    pl.semaphore_wait(ready, 7)

    def group_of(k):
        return lax.rem(j + k, OWNERS)

    def x_copy(k):
        return rcopy(
            r["xs"].at[k], r["xr"].at[k], r["s_x"].at[0, k], r["s_x"].at[1, k], (sib, f)
        )

    gcs = []
    lanes_f = pl.ds(pl.multiple_of(128 * f, 128), 128)

    def send_gradients():
        for a in range(3):
            piece = gf[2 - a : 4 - a, 1:9].reshape(128, 256)
            r["gs"][:, a] = piece.T.astype(BF).reshape(2, 8, 16, 128)
        for k in range(1, FILT):
            gcs.append(
                rcopy(
                    r["gs"].at[:, :, filt_peer(k)],
                    r["gr"].at[:, :, :, lanes_f],
                    r["s_g"].at[0, k],
                    r["s_g"].at[1, k],
                    (s, filt_peer(k)),
                )
            )
            gcs[-1].start()
        r["gr"][:, :, :, lanes_f] = r["gs"][:, :, pl.ds(f, 1)].reshape(2, 3, 16, 128)

    for k in range(OWNERS + 1):
        if k < OWNERS:
            patches = []
            for n in range(GROUP):
                t = jnp.minimum(GROUP * group_of(k) + n, 26)
                a, b, c = lax.div(t, 9), lax.rem(lax.div(t, 3), 3), lax.rem(t, 3)
                lanes = pl.ds(pl.multiple_of(128 * c, 128), 128)
                patch = zc[pl.ds(a, 4), pl.ds(b, 16), :, lanes]
                patches.append(patch.reshape(1024, 128))
            term = dot(gt, jnp.concatenate(patches, axis=1))

            @pl.when(core == 0)
            def _():
                r["xo"][k] = term[0:64]
                r["xs"][k] = term[64:128].astype(BF)

            @pl.when(core == 1)
            def _():
                r["xo"][k] = term[64:128]
                r["xs"][k] = term[0:64].astype(BF)

            x_copy(k).start()
        if k == 1:
            send_gradients()
        if k >= 1:
            p = k - 1
            x_copy(p).wait_recv()
            total = r["xo"][p] + r["xr"][p].astype(F32)
            es[p] = total.reshape(8, 8, 512).astype(BF)
            to_j = group_of(p)
            dj = lax.rem(to_j - j + 8, 8)
            for df in range(8):
                copy = rcopy(
                    es.at[p, chips_f[df]],
                    er.at[8 * dj + df],
                    r["s_rs"].at[p],
                    r["r_rs"].at[0],
                    (2 * to_j + core, chips_f[df]),
                )
                if p == 0 and df == 0:
                    pl.when(j >= OWNERS)(copy.start)
                else:
                    copy.start()

    for c in pss:
        c.wait_recv()
    ps3 = r["ps3"]
    for row in range(2):
        x = r["ps"][row].astype(F32)
        ps3[row, :, :, 0:128] = shift_rows(x, -1)
        ps3[row, :, :, 128:256] = x
        ps3[row, :, :, 256:384] = shift_rows(x, 1)
    for q in range(8):
        for b in range(3):
            patch = ps3[:, 8 * q + b : 8 * q + b + 8].reshape(128, 384).astype(BF)
            r["pb"][128 * q : 128 * q + 128, 384 * b : 384 * b + 384] = patch
    for c in gcs:
        c.wait_recv()
    deep = dot(r["gr"][...].reshape(96, 1024), r["pb"][...])

    @pl.when(core == 0)
    def _():
        r["ho"][...] = deep[0:48]
        r["hs"][...] = deep[48:96].astype(BF)

    @pl.when(core == 1)
    def _():
        r["ho"][...] = deep[48:96]
        r["hs"][...] = deep[0:48].astype(BF)

    hcopy = rcopy(r["hs"], r["hr"], r["s_h"].at[0], r["s_h"].at[1], (sib, f))
    hcopy.start()


    act = swap_cells(r["cells"], r["act"][...])
    r["bs"][...] = act.T.astype(BF).reshape(2, 8, 16, 128)
    bos = []
    for k in range(1, FILT):
        bos.append(
            rcopy(
                r["bs"].at[:, filt_peer(k)],
                r["br"].at[f],
                r["s_bo"].at[0, k],
                r["s_bo"].at[1, k],
                (s, filt_peer(k)),
            )
        )
        bos[-1].start()
    r["br"][pl.ds(f, 1)] = r["bs"][:, pl.ds(f, 1)].reshape(1, 2, 16, 128)

    hcopy.wait_recv()
    dsd = r["dsd"]
    dsd[27:28] = jnp.zeros((1, 16, 128), BF)
    total = r["ho"][...] + r["hr"][...].astype(F32)
    for a in range(3):
        for bc in range(9):
            dsd[9 * a + bc] = total[16 * a : 16 * a + 16, 128 * bc : 128 * bc + 128].astype(BF)

    def first_of(jj):
        return jnp.minimum(GROUP * jj, GROUP * (OWNERS - 1))

    drs = []
    for k in range(1, 8):
        to_s = space_chip(k)
        to_j = lax.div(to_s, 2)
        copy = rcopy(
            dsd.at[pl.ds(first_of(to_j), GROUP)],
            r["dr"].at[k],
            r["s_drs"].at[0, k],
            r["s_drs"].at[1, k],
            (to_s, f),
        )
        pl.when(to_j < OWNERS)(copy.start)
        drs.append((copy, to_j < OWNERS))

    mine_t = pl.ds(first_of(j), GROUP)

    ag_sends = []
    for k in range(1, CHIPS):
        piece = ea.at[core, jnp.minimum(j, OWNERS - 1), f]
        device = (chips_s[k // 8], chips_f[k % 8])
        ag_sends.append(rcopy(piece, piece, r["s_ag"].at[0], r["r_ag"].at[k // 8], device))

    @pl.when(owner)
    def _():
        er[0] = es[0, pl.ds(f, 1)].reshape(8, 512)
        landed = er.at[1:CHIPS]
        rcopy(landed, landed, r["s_rs"].at[0], r["r_rs"].at[0], (s, f)).wait_recv()
        total = jnp.sum(er[0:8].astype(F32), axis=0)
        for n in range(1, 8):
            total = total + jnp.sum(er[8 * n : 8 * n + 8].astype(F32), axis=0)
        total = (total * early_scale).astype(BF).reshape(1, 1, 1, 8, 512)
        ea[pl.ds(core, 1), pl.ds(j, 1), pl.ds(f, 1)] = total
        for c in ag_sends:
            c.start()

    da = r["da"]
    piece = da.at[core, mine_t]
    dag = []
    for k in range(1, 8):
        dag.append(
            rcopy(piece, piece, r["s_dag"].at[0, k], r["s_dag"].at[1, k], (space_chip(k), f))
        )

    @pl.when(owner)
    def _():
        total = dsd[mine_t].astype(F32)
        for k in range(1, 8):
            drs[k - 1][0].wait_recv()
            total = total + r["dr"][k].astype(F32)
        da[pl.ds(core, 1), mine_t] = (total * deep_scale).astype(BF).reshape(1, GROUP, 16, 128)
        for c in dag:
            c.start()

    for c in bos:
        c.wait_recv()
    parts = [jnp.zeros((32, 128), F32)] * 16
    for q in range(FILT):
        x = r["br"][q].reshape(32, 128).astype(F32)
        for p in range(16):
            moved = pltpu.roll(x, (8 * q - 8 * p) % 128, 1)
            parts[p] = jnp.where(lane // 8 == q, moved, parts[p])
    for p in range(16):
        r["bo"][p] = parts[p][:, 0:64].astype(BF)
    bo_copy = pltpu.make_async_copy(r["bo"], bo_out, r["s_out"].at[0])
    bo_copy.start()

    for k in range(1, 8):
        from_j = lax.div(lax.rem(s + SPACE - 2 * k, SPACE), 2)
        pl.when(from_j < OWNERS)(dag[k - 1].wait_recv)
    dar = rcopy(da.at[core], da.at[core], r["s_dar"].at[0], r["s_dar"].at[1], (sib, f))
    dar.start()

    def ear_copy(dj):
        piece = ea.at[core, lax.rem(j - dj + 8, 8)]
        return rcopy(piece, piece, r["s_ear"].at[0, dj], r["s_ear"].at[1, dj], (sib, f))

    def ea_copy(half, dj):
        g = lax.rem(j - dj + 8, 8)
        return pltpu.make_async_copy(ea.at[half, g], ea_out.at[half, g], r["s_ea"].at[half, dj])

    for dj in range(8):

        @pl.when(lax.rem(j - dj + 8, 8) < OWNERS)
        def _():
            landed = ea.at[core, lax.rem(j - dj + 8, 8), 0 : (8 if dj else 7)]
            rcopy(landed, landed, r["s_ag"].at[0], r["r_ag"].at[dj], (s, f)).wait_recv()
            ear_copy(dj).start()
            ea_copy(core, dj).start()

    dar.wait_recv()
    for t in range(27):
        r["gd"][t] = da[:, t].reshape(32, 128).astype(F32)
    gd_copy = pltpu.make_async_copy(r["gd"], gd_out, r["s_out"].at[1])
    gd_copy.start()

    for dj in range(8):

        @pl.when(lax.rem(j - dj + 8, 8) < OWNERS)
        def _():
            ear_copy(dj).wait_recv()
            ea_copy(other, dj).start()

    for h in (halo_v, halo_p):
        h.wait_send()
    cot_all(0).wait_send()
    pl.when(s > 0)(cot_all(1).wait_send)
    pl.when(s < SPACE - 1)(cot_all(2).wait_send)
    for c in wa + wb + wy + relay + pss + bos + gcs + [hcopy, dar]:
        c.wait_send()
    for copy, active in drs:
        pl.when(active)(copy.wait_send)

    for k in range(OWNERS):
        x_copy(k).wait_send()

    def rs_sent(k, count):
        left = es.at[k, 0:count]
        rcopy(left, left, r["s_rs"].at[k], r["r_rs"].at[0], (s, f)).wait_send()

    for k in range(1, OWNERS):
        rs_sent(k, 8)

    @pl.when(owner)
    def _():
        rs_sent(0, 7)
        left = er.at[1:CHIPS]
        rcopy(left, left, r["s_ag"].at[0], r["r_rs"].at[0], (s, f)).wait_send()
        for c in dag:
            c.wait_send()

    pl.when(j >= OWNERS)(functools.partial(rs_sent, 0, 8))
    for dj in range(8):

        @pl.when(lax.rem(j - dj + 8, 8) < OWNERS)
        def _():
            ear_copy(dj).wait_send()
            ea_copy(core, dj).wait()
            ea_copy(other, dj).wait()

    bo_copy.wait()
    gd_copy.wait()


def results(bo_in, ea_in, gd_in, bo_out, ge_out, gd_out, bo, ea, gd, ge, sems):
    ins = [pltpu.make_async_copy(ea_in.at[:, g], ea.at[g], sems.at[0, g]) for g in range(OWNERS)]
    ins.append(pltpu.make_async_copy(bo_in, bo, sems.at[0, 7]))
    ins.append(pltpu.make_async_copy(gd_in, gd, sems.at[0, 8]))
    outs = []
    for g in range(OWNERS):
        taps = min(GROUP, 27 - GROUP * g)
        src, dst = ge.at[pl.ds(GROUP * g, taps)], ge_out.at[pl.ds(GROUP * g, taps)]
        outs.append(pltpu.make_async_copy(src, dst, sems.at[1, g]))
    outs.append(pltpu.make_async_copy(bo, bo_out, sems.at[1, 7]))
    outs.append(pltpu.make_async_copy(gd, gd_out, sems.at[1, 8]))
    for c in ins:
        c.start()
    for g in range(OWNERS):
        ins[g].wait()
        block = ea[g].reshape(128, 512).astype(F32)
        for t in range(GROUP * g, min(GROUP * g + GROUP, 27)):
            n = t - GROUP * g
            ge[t] = block[:, 128 * n : 128 * n + 128].T
        outs[g].start()
    for n in (7, 8):
        ins[n].wait()
        outs[n].start()
    for c in outs:
        c.wait()


def shards(volume, w_early, w_deep, cotangent):
    any_ = pl.BlockSpec(memory_space=pl.ANY)
    cells = volume.shape[0] * volume.shape[1] * volume.shape[2] * SPACE * FILT
    body = functools.partial(kernel, 1.0 / math.sqrt(cells), 1.0 / math.sqrt(cells // 8))
    block, early, deep = pl.pallas_call(
        body,
        out_shape=(
            jax.ShapeDtypeStruct((16, 32, 64), BF),
            jax.ShapeDtypeStruct((2, 7, 8, 8, 512), BF),
            jax.ShapeDtypeStruct((27, 32, 128), F32),
        ),
        in_specs=[any_] * 4,
        out_specs=(any_,) * 3,
        scratch_shapes=[pltpu.VMEM(*v) for v in SCRATCH.values()]
        + [pltpu.SemaphoreType.DMA(v) for v in SEMS.values()]
        + [pltpu.SemaphoreType.REGULAR],
        compiler_params=pltpu.CompilerParams(
            collective_id=0, has_side_effects=True, vmem_limit_bytes=56 << 20
        ),
        name="step",
    )(
        volume,
        w_early.reshape(9, 384, 128),
        w_deep.transpose(0, 2, 1),
        cotangent.transpose(0, 2, 3, 1).reshape(16, 32, 64),
    )
    block, early, deep = pl.pallas_call(
        results,
        out_shape=(
            jax.ShapeDtypeStruct((16, 32, 64), BF),
            jax.ShapeDtypeStruct((27, 128, 128), F32),
            jax.ShapeDtypeStruct((27, 32, 128), F32),
        ),
        in_specs=[any_] * 3,
        out_specs=(any_,) * 3,
        scratch_shapes=[
            pltpu.VMEM((16, 32, 64), BF),
            pltpu.VMEM((7, 2, 8, 8, 512), BF),
            pltpu.VMEM((27, 32, 128), F32),
            pltpu.VMEM((27, 128, 128), F32),
            pltpu.SemaphoreType.DMA((2, 9)),
        ],
        compiler_params=pltpu.CompilerParams(vmem_limit_bytes=60 << 20),
        name="results",
    )(block, early, deep)
    block = block.reshape(2, 8, 32, 64).transpose(0, 3, 1, 2)
    return block, early, deep.transpose(0, 2, 1)


def solution(mesh):
    return jax.shard_map(
        shards,
        mesh=mesh,
        in_specs=(
            P("space", "filt", None, None),
            P(),
            P(None, None, "filt"),
            P("space", None, None, "filt"),
        ),
        out_specs=(P("space", None, None, "filt"), P(), P(None, None, "filt")),
        check_vma=False,
    )
```
